32 devices in a mesh: groups: 2 (over x), ctx: 8 (over z, y), exp: 2 (over core).
Axes of the slice: x: 2, y: 2, z: 4, core: 2. Of those that a mesh axis runs over, the one named last changes fastest.
Arguments:
- queries_in: bfloat16 [4096, 24, 128], P(('groups', 'ctx'), 'exp'), parts along dimension 0, may hold values from -42 to 42
- rotated_keys: bfloat16 [4096, 4, 128], P(('groups', 'ctx'), 'exp'), parts along dimension 0, may hold values from -6 to 6
- value_inputs: bfloat16 [4096, 4, 128], P(('groups', 'ctx'), 'exp'), parts along dimension 0, may hold values from -6 to 6
- stream_in: bfloat16 [4096, 3072], P(('groups', 'ctx', 'exp')), parts along dimension 0, may hold values from -6 to 6
- w_out: bfloat16 [24, 128, 3072], P('exp', 'ctx'), may hold values from -0.4375 to 0.4375
- w_router: bfloat16 [3072, 8], replicated, may hold values from -0.109375 to 0.109375
- routes: int32 [4096, 2], P(('groups', 'ctx', 'exp')), parts along dimension 0, may hold values from 0 to 7, all different within a row; in each aligned block of 128 rows (0 to 127, 128 to 255, ...) at most 64 rows name the same one
- expert_out: bfloat16 [16, 8, 2, 64, 3072], P(('groups', 'ctx'), 'exp'), parts along dimension 0, may hold values from -6 to 6
- grad_out: bfloat16 [4096, 3072], P(('groups', 'ctx', 'exp')), parts along dimension 0, may hold values from -6 to 6
Outputs:
- mixed: bfloat16 [4096, 3072], P(('groups', 'ctx', 'exp')), parts along dimension 0
- grad_input: bfloat16 [4096, 3072], P(('groups', 'ctx', 'exp')), parts along dimension 0
- grad_expert: bfloat16 [16, 8, 2, 64, 3072], P(('groups', 'ctx'), 'exp'), parts along dimension 0
- grad_q: bfloat16 [4096, 24, 128], P(('groups', 'ctx'), 'exp'), parts along dimension 0
- grad_k: bfloat16 [4096, 4, 128], P(('groups', 'ctx'), 'exp'), parts along dimension 0
- grad_v: bfloat16 [4096, 4, 128], P(('groups', 'ctx'), 'exp'), parts along dimension 0
The draws below stay inside these ranges and needn't reach their ends.
There are 2 independent parts, one for each index of `groups`. The reference program is written for one: setup_inputs(seed, part) draws one part's arguments, and reference() takes and returns one part's arrays. A program takes and returns all parts, laid end to end along the dimension named above; an argument that names none is the same for every part. Nothing has to cross between parts.
Inputs may be any that keep to these rules, and one draw needn't show every extreme that they name: `routes`: each row names 2 different experts; among the rows of one device no expert is named by more than 64 rows, and in every draw some device's rows name some expert exactly 64 times.
All inputs are finite; a program needn't handle non-finite values.
Results may differ from the reference program's by a relative error of at most 0.012.
The reference program's roundings to bfloat16 on the way count: a program that leaves them out, or rounds other values in their place, can miss the bound.
Values may be sent and summed in bfloat16 or wider, within the bound.
No kernel may reach another device: no remote copies, remote signals or barrier semaphores. Data moves between devices by JAX's collectives and lax.ppermute only.
A program may use at most 128 MiB of HBM per device.

```python
import math
import jax
import jax.numpy as jnp
import numpy as np
from jax import lax

D = 3072
QUERY_HEADS = 24
KEY_VALUE_HEADS = 4
HEAD_SIZE = 128
EXPERTS = 8
TOPK = 2
BAND_BLOCKS = 4
TOKENS_PER_SHARD = 256
SEQUENCE_TOKENS = 2048
ROWS = 128
CAP = 64
N_CTX = 8
N_EXP = 2


def attention_pair(key):
    base = jax.random.fold_in(key, 11)
    key_q, random_key_keys = jax.random.split(base, 2)
    query_rows = jnp.clip(jax.random.normal(key_q, (SEQUENCE_TOKENS, QUERY_HEADS, HEAD_SIZE), jnp.float32), -6.0, 6.0)
    key_rows = jnp.clip(jax.random.normal(random_key_keys, (SEQUENCE_TOKENS, KEY_VALUE_HEADS, HEAD_SIZE), jnp.float32), -6.0, 6.0)
    return (query_rows, key_rows)


def draw_queries_in(key, part):
    query_rows, key_rows = attention_pair(key)
    return query_rows.astype(jnp.bfloat16)


def draw_rotated_keys(key, part):
    query_rows, key_rows = attention_pair(key)
    return key_rows.astype(jnp.bfloat16)


def block_levels(rng, dims, pieces, smallest, largest):
    loudness = 1.0
    for position, shards_of in pieces:
        steps = jax.random.uniform(jax.random.fold_in(jax.random.fold_in(rng, 6), position), (shards_of,), jnp.float32, smallest / len(pieces), largest / len(pieces))
        loudness = loudness * jnp.repeat(jnp.exp(steps), dims[position] // shards_of).reshape((-1,) + (1,) * (len(dims) - 1 - position))
    return loudness


def assign_block(stream_key, own, number, rows, count, top, bound, skew):
    ranking = jax.random.permutation(stream_key, count)
    crowded, ordinary = shares(count, rows * top, bound, skew, True), shares(count, rows * top, bound, skew, False)
    places = jnp.arange(count)

    def named(sizes, rotation):
        used = int((sizes > 0).sum())
        fixed = max(1, used // 4)
        moved = fixed + (places - fixed + rotation * (used - fixed)) % max(1, count - fixed)
        return jnp.zeros((count,), jnp.int32).at[ranking[jnp.where(places < fixed, places, moved)]].set(jnp.asarray(sizes, jnp.int32))

    sizes = jnp.where(number % 4 == 0, named(crowded, number // 4), named(ordinary, number - number // 4 - 1))
    mixed = jax.random.permutation(jax.random.fold_in(own, 3), count)
    giver, receiver = mixed[0:count // 2 * 2:2], mixed[1:count // 2 * 2:2]
    room = jnp.minimum(sizes[giver] - 1, bound - sizes[receiver]) // 2
    room = jnp.where((giver == ranking[0]) | (receiver == ranking[0]) | (sizes[receiver] == 0), 0, jnp.maximum(room, 0))
    moved = jax.random.randint(jax.random.fold_in(own, 4), (count // 2,), 0, 1 << 20) % (room + 1)
    sizes = sizes.at[giver].add(-moved).at[receiver].add(moved)
    members = jnp.searchsorted(jnp.cumsum(sizes), jnp.arange(rows * top), side="right").astype(jnp.int32)
    table = members.reshape(top, rows).T
    table = table[jax.random.permutation(jax.random.fold_in(own, 1), rows)]
    rotation = jax.random.randint(jax.random.fold_in(own, 2), (rows, 1), 0, top)
    return jnp.take_along_axis(table, (jnp.arange(top)[None, :] + rotation) % top, axis=1)


def shares(amount, total, most, skew, full):
    portions = [(1 << 20) // math.isqrt(grade ** skew) + 1 for grade in range(1, amount + 1)]
    largest = most if full else min(most, max(-(-total // amount), total * portions[0] // sum(portions)))
    least = 1 if total - largest >= amount - 1 else 0
    counts, surplus = [largest] + [least] * (amount - 1), total - largest - least * (amount - 1)
    while surplus > 0:
        movable = [i for i in range(1, amount) if counts[i] < largest] or [i for i in range(1, amount) if counts[i] < most]
        whole, left = sum([portions[i] for i in movable]), surplus
        for i in movable:
            extra = min(most - counts[i], max(1, left * portions[i] // whole), surplus)
            counts[i] = counts[i] + extra
            surplus = surplus - extra
    return np.array(counts)


def normal_values(own_key, extent, deviation, most, pieces=(), kind=jnp.bfloat16):
    gain = block_levels(own_key, extent, pieces, -0.22, 0.18) if pieces else 1.0
    entries = jax.random.normal(own_key, extent, jnp.float32) * deviation * gain
    return jnp.minimum(jnp.maximum(entries, -most), most).astype(kind)


def setup_inputs(seed: int = 0, part: int = 0) -> dict:
    key_of = jax.random.split(jax.random.key(seed), 10)
    part_keys = jax.random.split(jax.random.fold_in(key_of[9], part), 10)
    queries_in = draw_queries_in(jax.random.fold_in(jax.random.fold_in(key_of[9], part), 71), part)
    rotated_keys = draw_rotated_keys(jax.random.fold_in(jax.random.fold_in(key_of[9], part), 71), part)
    value_inputs = normal_values(part_keys[2], (SEQUENCE_TOKENS, KEY_VALUE_HEADS, HEAD_SIZE), 1.0, 6.0, ((0, 8), (1, 2)))
    stream_in = normal_values(part_keys[3], (SEQUENCE_TOKENS, D), 1.0, 6.0, ((0, 16),))
    w_out = normal_values(key_of[4], (QUERY_HEADS, HEAD_SIZE, D), (QUERY_HEADS * HEAD_SIZE // 16) ** -0.5, 0.4375, ((0, 2), (1, 8)))
    w_router = normal_values(key_of[5], (D, EXPERTS), D ** -0.5, 0.109375)
    routes_keys = jax.random.split(jax.random.fold_in(part_keys[6], 1), SEQUENCE_TOKENS // ROWS)
    routes_turns = jax.random.permutation(jax.random.fold_in(part_keys[6], 3), SEQUENCE_TOKENS // ROWS)
    routes = jax.vmap(lambda own, number: assign_block(jax.random.fold_in(part_keys[6], 2), own, number, ROWS, EXPERTS, TOPK, CAP, 1))(routes_keys, routes_turns).reshape((SEQUENCE_TOKENS, TOPK))
    expert_out = normal_values(part_keys[7], (N_CTX, EXPERTS, N_EXP, CAP, D), 1.0, 6.0, ((0, 8), (1, 2)))
    grad_out = normal_values(part_keys[8], (SEQUENCE_TOKENS, D), 1.0, 6.0, ((0, 16),))
    return dict(queries_in=queries_in, rotated_keys=rotated_keys, value_inputs=value_inputs, stream_in=stream_in, w_out=w_out, w_router=w_router, routes=routes, expert_out=expert_out, grad_out=grad_out)


def band_scores(query_tile, k_band, place):
    query_group = QUERY_HEADS // KEY_VALUE_HEADS
    query_rows = query_tile.reshape(TOKENS_PER_SHARD, KEY_VALUE_HEADS, query_group, HEAD_SIZE).astype(jnp.float32)
    scores = jnp.einsum('tgad,sgd->gats', query_rows, k_band.astype(jnp.float32)) * HEAD_SIZE ** (-0.5)
    qpos = place * TOKENS_PER_SHARD + jnp.arange(TOKENS_PER_SHARD, dtype=jnp.int32)
    kpos = (place - BAND_BLOCKS + 1) * TOKENS_PER_SHARD + jnp.arange(BAND_BLOCKS * TOKENS_PER_SHARD, dtype=jnp.int32)
    admitted = (kpos[None, :] <= qpos[:, None]) & (kpos[None, :] >= 0)
    admitted = admitted & (kpos[None, :] // TOKENS_PER_SHARD >= qpos[:, None] // TOKENS_PER_SHARD - BAND_BLOCKS + 1)
    scores = jnp.where(admitted, scores, -1e+30)
    top = lax.optimization_barrier(jnp.max(scores, axis=-1, keepdims=True))
    lse = top + jnp.log(lax.optimization_barrier(jnp.sum(jnp.exp(scores - top), axis=-1, keepdims=True)))
    probs = lax.optimization_barrier(jnp.exp(scores - lse).astype(jnp.bfloat16))
    return (query_rows, probs)

def reference(queries_in, rotated_keys, value_inputs, stream_in, w_out, w_router, routes, expert_out, grad_out):
    query_group = QUERY_HEADS // KEY_VALUE_HEADS
    scale = HEAD_SIZE ** (-0.5)
    nblk = N_CTX * N_EXP
    padding_rows = jnp.zeros(((BAND_BLOCKS - 1) * TOKENS_PER_SHARD, KEY_VALUE_HEADS, HEAD_SIZE), rotated_keys.dtype)
    kpad = jnp.concatenate([padding_rows, rotated_keys], axis=0)
    padded_values = jnp.concatenate([padding_rows, value_inputs], axis=0)
    places = jnp.arange(N_CTX, dtype=jnp.int32)

    def slices(place):
        start_index = (place * TOKENS_PER_SHARD).astype(jnp.int32)
        query_tile = lax.dynamic_slice_in_dim(queries_in, start_index, TOKENS_PER_SHARD, 0)
        k_band = lax.dynamic_slice_in_dim(kpad, start_index, BAND_BLOCKS * TOKENS_PER_SHARD, 0)
        value_window = lax.dynamic_slice_in_dim(padded_values, start_index, BAND_BLOCKS * TOKENS_PER_SHARD, 0)
        return (start_index, query_tile, k_band, value_window)

    def forward_block(place):
        start_index, query_tile, k_band, value_window = slices(place)
        query_rows, probs = band_scores(query_tile, k_band, place)
        attention_tile = jnp.einsum('gats,sgd->tgad', probs.astype(jnp.float32), value_window.astype(jnp.float32))
        return attention_tile.astype(jnp.bfloat16).reshape(TOKENS_PER_SHARD, QUERY_HEADS, HEAD_SIZE)
    attention_out = lax.map(forward_block, places).reshape(SEQUENCE_TOKENS, QUERY_HEADS, HEAD_SIZE)
    proj = jnp.dot(attention_out.reshape(SEQUENCE_TOKENS, QUERY_HEADS * HEAD_SIZE), w_out.reshape(QUERY_HEADS * HEAD_SIZE, D), preferred_element_type=jnp.float32)
    resid = stream_in.astype(jnp.float32) + proj
    inv_rms = lax.rsqrt(lax.optimization_barrier(jnp.mean(resid * resid, axis=-1, keepdims=True)) + 1e-05)
    normed = (resid * inv_rms).astype(jnp.bfloat16)
    logits = jnp.dot(normed, w_router, preferred_element_type=jnp.float32)
    choose = (routes[:, :, None] == jnp.arange(EXPERTS, dtype=jnp.int32)[None, None, :]).astype(jnp.int32)
    flat_choose = choose.reshape(nblk, ROWS * TOPK, EXPERTS)
    before = jnp.cumsum(flat_choose, axis=1) - flat_choose
    rank = lax.optimization_barrier(jnp.sum(before * flat_choose, axis=-1))
    slots = routes.reshape(nblk, ROWS * TOPK) * CAP + rank
    table = jnp.transpose(expert_out, (0, 2, 1, 3, 4)).reshape(nblk, EXPERTS * CAP, D)
    picked = jnp.take_along_axis(table, slots[:, :, None], axis=1).reshape(SEQUENCE_TOKENS, TOPK, D)
    chosen = jnp.take_along_axis(logits, routes, axis=1)
    gate_first = 1.0 / (1.0 + jnp.exp(chosen[:, 1] - chosen[:, 0]))
    gates = jnp.stack([gate_first, 1.0 - gate_first], axis=1)
    picked_f = picked.astype(jnp.float32)
    mixed = (resid + jnp.einsum('tk,tkd->td', gates, picked_f)).astype(jnp.bfloat16)
    dyf = grad_out.astype(jnp.float32)
    dgate = jnp.einsum('td,tkd->tk', dyf, picked_f)
    spread = gates * (dgate - lax.optimization_barrier(jnp.sum(gates * dgate, axis=1, keepdims=True)))
    dlogit = jnp.einsum('tk,tke->te', spread, choose.astype(jnp.float32))
    dnormed = jnp.dot(dlogit, w_router.astype(jnp.float32).T, precision=lax.Precision.HIGHEST)
    grad_input = dyf + inv_rms * dnormed - resid * inv_rms ** 3 * lax.optimization_barrier(jnp.mean(dnormed * resid, axis=-1, keepdims=True))
    grad_input = grad_input.astype(jnp.bfloat16)
    contrib = (gates[:, :, None] * dyf[:, None, :]).astype(jnp.bfloat16).reshape(nblk, ROWS * TOPK, D)
    buffer = jnp.zeros((nblk, EXPERTS * CAP, D), jnp.bfloat16)
    buffer = buffer.at[jnp.arange(nblk, dtype=jnp.int32)[:, None], slots].set(contrib)
    grad_expert = jnp.transpose(buffer.reshape(N_CTX, N_EXP, EXPERTS, CAP, D), (0, 2, 1, 3, 4))
    attention_gradient = jnp.dot(grad_input, w_out.reshape(QUERY_HEADS * HEAD_SIZE, D).T, preferred_element_type=jnp.float32)
    attention_gradient = attention_gradient.astype(jnp.bfloat16).reshape(SEQUENCE_TOKENS, QUERY_HEADS, HEAD_SIZE)

    def backward_block(carry, place):
        dk_acc, dv_acc = carry
        start_index, query_tile, k_band, value_window = slices(place)
        query_rows, probs = band_scores(query_tile, k_band, place)
        probs_f = probs.astype(jnp.float32)
        attention_tile = lax.dynamic_slice_in_dim(attention_out, start_index, TOKENS_PER_SHARD, 0).reshape(TOKENS_PER_SHARD, KEY_VALUE_HEADS, query_group, HEAD_SIZE).astype(jnp.float32)
        input_gradient = lax.dynamic_slice_in_dim(attention_gradient, start_index, TOKENS_PER_SHARD, 0).reshape(TOKENS_PER_SHARD, KEY_VALUE_HEADS, query_group, HEAD_SIZE).astype(jnp.float32)
        delta = jnp.einsum('tgad,tgad->gat', input_gradient, attention_tile)
        dprob = jnp.einsum('tgad,sgd->gats', input_gradient, value_window.astype(jnp.float32))
        dscore = (probs_f * (dprob - delta[..., None])).astype(jnp.bfloat16).astype(jnp.float32)
        dq = (jnp.einsum('gats,sgd->tgad', dscore, k_band.astype(jnp.float32)) * scale).astype(jnp.bfloat16)
        dkey = jnp.einsum('gats,tgad->sgd', dscore, query_rows) * scale
        dval = jnp.einsum('gats,tgad->sgd', probs_f, input_gradient)
        dk_acc = lax.dynamic_update_slice_in_dim(dk_acc, lax.dynamic_slice_in_dim(dk_acc, start_index, BAND_BLOCKS * TOKENS_PER_SHARD, 0) + dkey, start_index, 0)
        dv_acc = lax.dynamic_update_slice_in_dim(dv_acc, lax.dynamic_slice_in_dim(dv_acc, start_index, BAND_BLOCKS * TOKENS_PER_SHARD, 0) + dval, start_index, 0)
        return ((dk_acc, dv_acc), dq.reshape(TOKENS_PER_SHARD, QUERY_HEADS, HEAD_SIZE))
    empty_block = jnp.zeros(((BAND_BLOCKS - 1) * TOKENS_PER_SHARD + SEQUENCE_TOKENS, KEY_VALUE_HEADS, HEAD_SIZE), jnp.float32)
    (dk_acc, dv_acc), grad_q = lax.scan(backward_block, (empty_block, empty_block), places)
    grad_q = grad_q.reshape(SEQUENCE_TOKENS, QUERY_HEADS, HEAD_SIZE)
    grad_k = dk_acc[(BAND_BLOCKS - 1) * TOKENS_PER_SHARD:].astype(jnp.bfloat16)
    grad_v = dv_acc[(BAND_BLOCKS - 1) * TOKENS_PER_SHARD:].astype(jnp.bfloat16)
    return (mixed, grad_input, grad_expert, grad_q, grad_k, grad_v)
```

```python
import functools

import jax
import jax.numpy as jnp
from jax import lax
from jax.experimental import pallas as pl
from jax.experimental.pallas import tpu as pltpu
from jax.sharding import PartitionSpec as P

BAND_BLOCKS = 4
F32 = jnp.float32
BF16 = jnp.bfloat16
VMEM_LIMIT = 48 * 1024 * 1024


def params(limit=VMEM_LIMIT):
    return pltpu.CompilerParams(vmem_limit_bytes=limit)


def cost(flops, nbytes, exps=0):
    return pl.CostEstimate(flops=flops, bytes_accessed=nbytes, transcendentals=exps)


def dot_nn(a, b):
    return lax.dot_general(a, b, (((1,), (0,)), ((), ())), preferred_element_type=F32)


def dot_nt(a, b):
    return lax.dot_general(a, b, (((1,), (1,)), ((), ())), preferred_element_type=F32)


def dot_tn(a, b):
    return lax.dot_general(a, b, (((0,), (0,)), ((), ())), preferred_element_type=F32)


def passed_along(value, axis, steps):
    count = lax.axis_size(axis)
    initial, last = (max(0, -steps), min(count, count - steps))
    return lax.ppermute(value, axis, [(source, source + steps) for source in range(initial, last)])


def swapped(value, axis):
    return lax.ppermute(value, axis, [(0, 1), (1, 0)])


def gathered(w_out):
    heads, depth, _ = w_out.shape
    count = lax.axis_size("ctx")
    place = lax.axis_index("ctx")
    if count != 8 or lax.axis_size("groups") != 2 or heads % 3:
        full = lax.all_gather(w_out, "ctx", axis=1, tiled=True)
        return [full], jnp.zeros((1,), jnp.int32), [(0, 0, heads, 0, 0)]
    side = lax.axis_index("groups")
    third = heads // 3
    mine = lax.dynamic_slice_in_dim(w_out, side * third, third, 0)
    ring = [(c, (c + 2) % count) for c in range(count)]
    pairs = [(c, c ^ 1) for c in range(count)]
    held = [jnp.concatenate([mine, w_out[2 * third :]], axis=0)]
    arrays, plan = [w_out], [(0, 0, heads, 0, 4)]
    table = [0, side * third, (1 - side) * third, 2 * third]
    table += [depth * ((place - 2 * k) % count) for k in range(4)]
    table += [depth * (((place - 2 * k) % count) ^ 1) for k in range(4)]

    def add(array, parts, row):
        arrays.append(array)
        for start, size, head in parts:
            plan.append((len(arrays) - 1, start, size, head, row))

    both = [(0, third, 1), (third, third, 3)]
    for k in range(1, 4):
        held.append(lax.ppermute(held[-1], "ctx", ring))
        add(held[k], both, 4 + k)
        add(swapped(held[k][:third], "groups"), [(0, third, 2)], 4 + k)
    for k in range(3):
        across = lax.ppermute(held[k], "ctx", pairs)
        add(across, both, 8 + k)
        add(swapped(across[:third], "groups"), [(0, third, 2)], 8 + k)
    across = lax.ppermute(held[3][:third], "ctx", pairs)
    add(across, [(0, third, 1)], 11)
    add(swapped(across, "groups"), [(0, third, 2)], 11)
    add(lax.ppermute(held[3][third:], "ctx", pairs), [(0, third, 3)], 11)
    return arrays, jnp.stack([jnp.asarray(t, jnp.int32) for t in table]), plan


def piece_copies(plan, table, pieces, buf, sem, chunk, chunk_size):
    copies = []
    columns = pl.ds(pl.multiple_of(chunk * chunk_size, chunk_size), chunk_size)
    depth_of = [p.shape[1] for p in pieces]
    for number, (array, start, size, head, row) in enumerate(plan):
        rows = pl.ds(pl.multiple_of(table[row], depth_of[array]), depth_of[array])
        copies.append(
            pltpu.make_async_copy(
                pieces[array].at[pl.ds(start, size), :, columns],
                buf.at[pl.ds(table[head], size), rows, columns],
                sem.at[number, chunk],
            )
        )
    return copies


CHUNKS = 3


def wait_chunk(plan, table, pieces, buf, sem, width):
    step = pl.program_id(0)
    size = width // CHUNKS

    @pl.when(step == 0)
    def _():
        for chunk in range(CHUNKS):
            for copy in piece_copies(plan, table, pieces, buf, sem, chunk, size):
                copy.start()

    for copy in piece_copies(plan, table, pieces, buf, sem, step, size):
        copy.wait()
    return pl.ds(pl.multiple_of(step * size, size), size)


def project_kernel(plan, count, table, core, attn, *refs):
    pieces, (own, other, buf, sem) = refs[:count], refs[count:]
    heads, head_dim, width = buf.shape
    columns = wait_chunk(plan, table, pieces, buf, sem, width)
    weights = buf[:, :, columns].reshape(heads * head_dim, width // CHUNKS)
    result = dot_nn(attn[...], weights)
    rows = own.shape[0]

    @pl.when(core[0] == 0)
    def _():
        own[...] = result[:rows]
        other[...] = result[rows:]

    @pl.when(core[0] != 0)
    def _():
        own[...] = result[rows:]
        other[...] = result[:rows]


def project(attn, arrays, table, plan, core, heads, head_dim, width, rows):
    tok = attn.shape[0]
    size = width // CHUNKS
    return pl.pallas_call(
        functools.partial(project_kernel, plan, len(arrays)),
        grid_spec=pltpu.PrefetchScalarGridSpec(
            num_scalar_prefetch=2,
            grid=(CHUNKS,),
            in_specs=[pl.BlockSpec((tok, heads * head_dim), lambda i, *_: (0, 0))]
            + [pl.BlockSpec(memory_space=pltpu.HBM)] * len(arrays),
            out_specs=[pl.BlockSpec((rows, size), lambda i, *_: (0, i))] * 2,
            scratch_shapes=[
                pltpu.VMEM((heads, head_dim, width), BF16),
                pltpu.SemaphoreType.DMA((len(plan), CHUNKS)),
            ],
        ),
        out_shape=[jax.ShapeDtypeStruct((rows, width), F32)] * 2,
        compiler_params=params(),
        cost_estimate=cost(2 * tok * heads * head_dim * width, 2 * heads * head_dim * width),
        name="project",
    )(table, core, attn, *arrays)


def dattn_kernel(plan, count, table, core, own, recv, *refs):
    pieces, (out, grad, acc, buf, sem) = refs[:count], refs[count:]
    heads, head_dim, width = buf.shape
    rows = own.shape[0]
    step = pl.program_id(0)

    @pl.when(core[0] == 0)
    def _():
        grad[:rows] = own[...]
        grad[rows:] = recv[...]

    @pl.when(core[0] != 0)
    def _():
        grad[rows:] = own[...]
        grad[:rows] = recv[...]

    columns = wait_chunk(plan, table, pieces, buf, sem, width)
    weights = buf[:, :, columns].reshape(heads * head_dim, width // CHUNKS)
    part = dot_nt(grad[...], weights)

    @pl.when(step == 0)
    def _():
        acc[...] = part

    @pl.when(step > 0)
    def _():
        acc[...] += part

    @pl.when(step == CHUNKS - 1)
    def _():
        out[...] = acc[...].astype(BF16)


def dattention(own, recv, arrays, table, plan, core, heads, head_dim, width):
    rows = own.shape[0]
    size = width // CHUNKS
    return pl.pallas_call(
        functools.partial(dattn_kernel, plan, len(arrays)),
        grid_spec=pltpu.PrefetchScalarGridSpec(
            num_scalar_prefetch=2,
            grid=(CHUNKS,),
            in_specs=[pl.BlockSpec((rows, size), lambda i, *_: (0, i))] * 2
            + [pl.BlockSpec(memory_space=pltpu.HBM)] * len(arrays),
            out_specs=pl.BlockSpec((2 * rows, heads * head_dim), lambda i, *_: (0, 0)),
            scratch_shapes=[
                pltpu.VMEM((2 * rows, size), BF16),
                pltpu.VMEM((2 * rows, heads * head_dim), F32),
                pltpu.VMEM((heads, head_dim, width), BF16),
                pltpu.SemaphoreType.DMA((len(plan), CHUNKS)),
            ],
        ),
        out_shape=jax.ShapeDtypeStruct((2 * rows, heads * head_dim), BF16),
        compiler_params=params(),
        cost_estimate=cost(4 * rows * heads * head_dim * width, 2 * heads * head_dim * width),
        name="dattention",
    )(table, core, own, recv, *arrays)


def band_of(refs):
    return jnp.concatenate([r[...] for r in refs], axis=0)


def attention_kernel(scale, place, q, *refs):
    keys, values, (attn, probs) = refs[:BAND_BLOCKS], refs[BAND_BLOCKS : 2 * BAND_BLOCKS], refs[-2:]
    tok = q.shape[0]
    scores = dot_nt(q[...], band_of(keys)) * scale
    shape = scores.shape
    row = lax.broadcasted_iota(jnp.int32, shape, 0)
    column = lax.broadcasted_iota(jnp.int32, shape, 1)
    offset = column - (BAND_BLOCKS - 1) * tok
    admitted = (offset <= row) & (offset + place[0] * tok >= 0)
    scores = jnp.where(admitted, scores, -1e30)
    top = jnp.max(scores, axis=-1, keepdims=True)
    grown = jnp.exp(scores - top)
    weight = (grown * (1.0 / jnp.sum(grown, axis=-1, keepdims=True))).astype(BF16)
    probs[0] = weight
    attn[...] = dot_nn(weight, band_of(values)).astype(BF16)


def attention(queries, bands, place, heads, heads_kv, head_dim, scale):
    tok = queries.shape[0]
    group = heads // heads_kv
    keys = pl.BlockSpec((tok, head_dim), lambda h, *_: (0, h // group))
    values = pl.BlockSpec((tok, head_dim), lambda h, *_: (0, heads_kv + h // group))
    per_head = pl.BlockSpec((tok, head_dim), lambda h, *_: (0, h))
    span = BAND_BLOCKS * tok
    return pl.pallas_call(
        functools.partial(attention_kernel, scale),
        grid_spec=pltpu.PrefetchScalarGridSpec(
            num_scalar_prefetch=1,
            grid=(heads,),
            in_specs=[per_head] + [keys] * BAND_BLOCKS + [values] * BAND_BLOCKS,
            out_specs=[per_head, pl.BlockSpec((1, tok, span), lambda h, *_: (h, 0, 0))],
        ),
        out_shape=[
            jax.ShapeDtypeStruct((tok, heads * head_dim), BF16),
            jax.ShapeDtypeStruct((heads, tok, span), BF16),
        ],
        compiler_params=params(),
        cost_estimate=cost(4 * tok * span * heads * head_dim, 2 * heads * tok * span, heads * tok * span),
        name="attention",
    )(place, queries, *bands, *bands)


def attention_grad_kernel(scale, group, heads_kv, q, dout, attn, probs, *refs):
    keys, values = refs[:BAND_BLOCKS], refs[BAND_BLOCKS : 2 * BAND_BLOCKS]
    dq, outs, (dk, dv) = refs[2 * BAND_BLOCKS], refs[2 * BAND_BLOCKS + 1 : -2], refs[-2:]
    tok, head_dim = q.shape
    head = pl.program_id(0)
    grad = dout[...]
    weight = probs[0]
    delta = jnp.sum(grad.astype(F32) * attn[...].astype(F32), axis=-1, keepdims=True)
    dprob = dot_nt(grad, band_of(values))
    dscore = (weight.astype(F32) * (dprob - delta)).astype(BF16)
    dq[...] = (dot_nn(dscore, band_of(keys)) * scale).astype(BF16)
    dkey = dot_tn(dscore, q[...])
    dvalue = dot_tn(weight, grad)

    @pl.when(head % group == 0)
    def _():
        dk[...] = dkey
        dv[...] = dvalue

    @pl.when(head % group > 0)
    def _():
        dk[...] += dkey
        dv[...] += dvalue

    @pl.when(head % group == group - 1)
    def _():
        lanes_k = pl.ds(pl.multiple_of(head // group * head_dim, head_dim), head_dim)
        lanes_v = pl.ds(pl.multiple_of((heads_kv + head // group) * head_dim, head_dim), head_dim)
        for block, out in enumerate(outs):
            rows = pl.ds(block * tok, tok)
            out[:, lanes_k] = (dk[rows, :] * scale).astype(out.dtype)
            out[:, lanes_v] = dv[rows, :].astype(out.dtype)


def attention_grad(queries, dout, attn, probs, bands, heads, heads_kv, head_dim, scale):
    tok = queries.shape[0]
    group = heads // heads_kv
    keys = pl.BlockSpec((tok, head_dim), lambda h: (0, h // group))
    values = pl.BlockSpec((tok, head_dim), lambda h: (0, heads_kv + h // group))
    per_head = pl.BlockSpec((tok, head_dim), lambda h: (0, h))
    span = BAND_BLOCKS * tok
    lanes = 2 * heads_kv * head_dim
    whole = pl.BlockSpec((tok, lanes), lambda h: (0, 0))
    return pl.pallas_call(
        functools.partial(attention_grad_kernel, scale, group, heads_kv),
        grid=(heads,),
        in_specs=[per_head] * 3
        + [pl.BlockSpec((1, tok, span), lambda h: (h, 0, 0))]
        + [keys] * BAND_BLOCKS
        + [values] * BAND_BLOCKS,
        out_specs=[per_head] + [whole] * BAND_BLOCKS,
        out_shape=[jax.ShapeDtypeStruct((tok, heads * head_dim), BF16)]
        + [jax.ShapeDtypeStruct((tok, lanes), BF16)] * (BAND_BLOCKS - 1)
        + [jax.ShapeDtypeStruct((tok, lanes), F32)],
        scratch_shapes=[pltpu.VMEM((span, head_dim), F32)] * 2,
        compiler_params=params(),
        cost_estimate=cost(8 * tok * span * heads * head_dim, 2 * heads * tok * span),
        name="attention_grad",
    )(queries, dout, attn, probs, *bands, *bands)


def pick_kernel(slots, here, there, gout, first, second, dgate):
    step = pl.program_id(0)
    rows, width = gout.shape
    room = here.shape[0]
    column = lax.broadcasted_iota(jnp.int32, (rows, room), 1)
    grad = gout[...].astype(F32)
    sums = []
    for i, out in enumerate((first, second)):
        near = (slots[:, i : i + 1] == column).astype(BF16)
        far = (slots[:, i : i + 1] == column + room).astype(BF16)
        row = dot_nn(near, here[...]) + dot_nn(far, there[...])
        out[...] = row.astype(BF16)
        sums.append(jnp.sum(grad * row, axis=-1, keepdims=True))
    lane = lax.broadcasted_iota(jnp.int32, dgate.shape, 1)
    total = jnp.where(lane == 0, sums[0], jnp.where(lane == 1, sums[1], 0.0))

    @pl.when(step == 0)
    def _():
        dgate[...] = total

    @pl.when(step > 0)
    def _():
        dgate[...] += total


def pick(slots, here, there, grad_out):
    rows, width = grad_out.shape
    room = here.shape[0]
    size = width // CHUNKS
    by_column = lambda n: pl.BlockSpec((n, size), lambda i: (0, i))
    return pl.pallas_call(
        pick_kernel,
        grid=(CHUNKS,),
        in_specs=[pl.BlockSpec((rows, 2), lambda i: (0, 0)), by_column(room), by_column(room), by_column(rows)],
        out_specs=[by_column(rows), by_column(rows), pl.BlockSpec((rows, 128), lambda i: (0, 0))],
        out_shape=[jax.ShapeDtypeStruct((rows, width), BF16)] * 2 + [jax.ShapeDtypeStruct((rows, 128), F32)],
        compiler_params=params(),
        cost_estimate=cost(8 * rows * room * width, 8 * rows * width + 4 * room * width),
        name="pick",
    )(slots, here, there, grad_out)


def middle_kernel(routes, own, recv, stream, first, second, gout, dgate, router, router_t, mixed, grad, gates):
    resid = stream[...].astype(F32) + (own[...] + recv[...])
    inverse = lax.rsqrt(jnp.mean(resid * resid, axis=-1, keepdims=True) + 1e-05)
    normed = (resid * inverse).astype(BF16)
    logits = dot_nn(normed, router[...])
    lane = lax.broadcasted_iota(jnp.int32, logits.shape, 1)
    is_first, is_second = lane == routes[:, 0:1], lane == routes[:, 1:2]
    chosen_first = jnp.sum(jnp.where(is_first, logits, 0.0), axis=-1, keepdims=True)
    chosen_second = jnp.sum(jnp.where(is_second, logits, 0.0), axis=-1, keepdims=True)
    gate_first = 1.0 / (1.0 + jnp.exp(chosen_second - chosen_first))
    gate_second = 1.0 - gate_first
    mixed[...] = (
        resid + gate_first * first[...].astype(F32) + gate_second * second[...].astype(F32)
    ).astype(BF16)
    d_first, d_second = dgate[:, 0:1], dgate[:, 1:2]
    common = gate_first * d_first + gate_second * d_second
    dlogit = jnp.where(is_first, gate_first * (d_first - common), 0.0)
    dlogit = dlogit + jnp.where(is_second, gate_second * (d_second - common), 0.0)
    high = dlogit.astype(BF16)
    rest = dlogit - high.astype(F32)
    middle = rest.astype(BF16)
    low = (rest - middle.astype(F32)).astype(BF16)
    weights = router_t[...]
    dnormed = dot_nn(high, weights) + (dot_nn(middle, weights) + dot_nn(low, weights))
    mean = jnp.mean(dnormed * resid, axis=-1, keepdims=True)
    grad[...] = (
        gout[...].astype(F32) + inverse * dnormed - resid * (inverse * inverse * inverse * mean)
    ).astype(BF16)
    gates[...] = jnp.where(lane == 0, gate_first, jnp.where(lane == 1, gate_second, 0.0))


def middle(routes, own, recv, stream, first, second, grad_out, dgate, router, router_t):
    rows, width = stream.shape
    size = 32 if rows % 32 == 0 else rows
    by_row = lambda n: pl.BlockSpec((size, n), lambda i: (i, 0))
    whole = lambda a: pl.BlockSpec(a.shape, lambda i: (0, 0))
    return pl.pallas_call(
        middle_kernel,
        grid=(rows // size,),
        in_specs=[by_row(2)] + [by_row(width)] * 6 + [by_row(128), whole(router), whole(router_t)],
        out_specs=[by_row(width), by_row(width), by_row(128)],
        out_shape=[jax.ShapeDtypeStruct((rows, width), BF16)] * 2 + [jax.ShapeDtypeStruct((rows, 128), F32)],
        compiler_params=params(),
        cost_estimate=cost(2 * rows * 128 * width * 4, 20 * rows * width),
        name="middle",
    )(routes, own, recv, stream, first, second, grad_out, dgate, router, router_t)


def spread_kernel(slots, gates, gout, here, there):
    room = here.shape[0]
    rows = gout.shape[0]
    place = lax.broadcasted_iota(jnp.int32, (room, rows), 0)
    grad = gout[...].astype(F32)
    near, far = 0.0, 0.0
    for i in range(2):
        part = (gates[:, i : i + 1] * grad).astype(BF16)
        near = near + dot_nn((slots[i : i + 1, :] == place).astype(BF16), part)
        far = far + dot_nn((slots[i : i + 1, :] == place + room).astype(BF16), part)
    here[...] = near.astype(BF16)
    there[...] = far.astype(BF16)


def spread(slots_t, gates, grad_out, room):
    rows, width = grad_out.shape
    size = width // CHUNKS
    by_column = lambda n: pl.BlockSpec((n, size), lambda i: (0, i))
    return pl.pallas_call(
        spread_kernel,
        grid=(CHUNKS,),
        in_specs=[
            pl.BlockSpec((2, rows), lambda i: (0, 0)),
            pl.BlockSpec((rows, 128), lambda i: (0, 0)),
            by_column(rows),
        ],
        out_specs=[by_column(room)] * 2,
        out_shape=[jax.ShapeDtypeStruct((room, width), BF16)] * 2,
        compiler_params=params(),
        cost_estimate=cost(8 * rows * room * width, 2 * rows * width + 4 * room * width),
        name="spread",
    )(slots_t, gates, grad_out)


def local(
    queries_in, rotated_keys, value_inputs, stream_in, w_out, w_router, routes, expert_out, grad_out
):
    place = lax.axis_index("ctx")
    core = lax.axis_index("exp")
    tok, heads_q, head_dim = queries_in.shape
    heads_kv = rotated_keys.shape[1]
    rows, width = stream_in.shape
    experts = w_router.shape[1]
    held, capacity = expert_out.shape[1], expert_out.shape[3]
    room = held * capacity
    scale = head_dim ** (-0.5)
    core_arg = core.astype(jnp.int32).reshape(1)
    place_arg = place.astype(jnp.int32).reshape(1)

    arrays, table, plan = gathered(w_out)

    own_band = jnp.concatenate(
        [rotated_keys.reshape(tok, heads_kv * head_dim), value_inputs.reshape(tok, heads_kv * head_dim)], axis=1
    )
    bands = [own_band] + [passed_along(own_band, "ctx", step) for step in range(1, BAND_BLOCKS)]
    bands = bands[::-1]

    sent = lax.dynamic_index_in_dim(expert_out[0], 1 - core, 1, keepdims=False).reshape(room, width)
    kept = lax.dynamic_index_in_dim(expert_out[0], core, 1, keepdims=False).reshape(room, width)
    arrived = swapped(sent, "exp")
    flat = routes.reshape(-1)
    number = jnp.arange(2 * rows, dtype=jnp.int32)
    earlier = (flat[None, :] == flat[:, None]) & (number[None, :] < number[:, None])
    rank = jnp.sum(earlier.astype(jnp.int32), axis=1)
    slots = (flat * capacity + rank - core * room) % (experts * capacity)
    slots = slots.reshape(rows, 2)
    first, second, dgate = pick(slots, kept, arrived, grad_out)

    queries = queries_in.reshape(tok, heads_q * head_dim)
    attn, probs = attention(queries, bands, place_arg, heads_q, heads_kv, head_dim, scale)

    own, other = project(attn, arrays, table, plan, core_arg, heads_q, head_dim, width, rows)
    router = jnp.pad(w_router, ((0, 0), (0, 128 - experts)))
    mixed, grad_input, gates = middle(
        routes, own, swapped(other, "exp"), stream_in, first, second, grad_out, dgate, router, router.T
    )
    grad_other = swapped(grad_input, "exp")
    here, there = spread(slots.T, gates, grad_out, room)
    back = swapped(there, "exp").reshape(held, 1, capacity, width)
    here = here.reshape(held, 1, capacity, width)
    grad_expert = jnp.where(
        core == 0, jnp.concatenate([here, back], axis=1), jnp.concatenate([back, here], axis=1)
    )[None]

    dattn = dattention(grad_input, grad_other, arrays, table, plan, core_arg, heads_q, head_dim, width)
    grads = attention_grad(queries, dattn, attn, probs, bands, heads_q, heads_kv, head_dim, scale)
    grad_q = grads[0].reshape(tok, heads_q, head_dim)
    total = grads[BAND_BLOCKS]
    for step in range(1, BAND_BLOCKS):
        total = total + passed_along(grads[BAND_BLOCKS - step], "ctx", -step).astype(F32)
    total = total.astype(BF16).reshape(tok, 2, heads_kv, head_dim)
    return (mixed, grad_input, grad_expert, grad_q, total[:, 0], total[:, 1])


def solution(mesh):
    in_specs = (
        P(("groups", "ctx"), "exp", None),
        P(("groups", "ctx"), "exp", None),
        P(("groups", "ctx"), "exp", None),
        P(("groups", "ctx", "exp"), None),
        P("exp", "ctx", None),
        P(),
        P(("groups", "ctx", "exp"), None),
        P(("groups", "ctx"), "exp", None, None, None),
        P(("groups", "ctx", "exp"), None),
    )
    out_specs = (
        P(("groups", "ctx", "exp"), None),
        P(("groups", "ctx", "exp"), None),
        P(("groups", "ctx"), "exp", None, None, None),
        P(("groups", "ctx"), "exp", None),
        P(("groups", "ctx"), "exp", None),
        P(("groups", "ctx"), "exp", None),
    )
    return jax.shard_map(local, mesh=mesh, in_specs=in_specs, out_specs=out_specs, check_vma=False)
```

```python
import functools

import jax
import jax.numpy as jnp
from jax import lax
from jax.experimental import pallas as pl
from jax.experimental.pallas import tpu as pltpu
from jax.sharding import PartitionSpec as P

BAND_BLOCKS = 4
F32 = jnp.float32
BF16 = jnp.bfloat16
VMEM_LIMIT = 24 * 1024 * 1024


def params(limit=VMEM_LIMIT):
    return pltpu.CompilerParams(vmem_limit_bytes=limit)


def cost(flops, nbytes, exps=0):
    return pl.CostEstimate(flops=flops, bytes_accessed=nbytes, transcendentals=exps)


def dot_nn(a, b):
    return lax.dot_general(a, b, (((1,), (0,)), ((), ())), preferred_element_type=F32)


def dot_nt(a, b):
    return lax.dot_general(a, b, (((1,), (1,)), ((), ())), preferred_element_type=F32)


def dot_tn(a, b):
    return lax.dot_general(a, b, (((0,), (0,)), ((), ())), preferred_element_type=F32)


def passed_along(value, axis, steps):
    count = lax.axis_size(axis)
    initial, last = (max(0, -steps), min(count, count - steps))
    return lax.ppermute(value, axis, [(source, source + steps) for source in range(initial, last)])


def swapped(value, axis):
    return lax.ppermute(value, axis, [(0, 1), (1, 0)])


def after(values, *others):
    return lax.optimization_barrier((tuple(values), others))[0]


def gathered(w_out, work):
    heads, depth, _ = w_out.shape
    count = lax.axis_size("ctx")
    place = lax.axis_index("ctx")
    if count != 8 or lax.axis_size("groups") != 2 or heads % 3:
        full = lax.all_gather(w_out, "ctx", axis=1, tiled=True)
        for task in work:
            task(())
        return [full], jnp.zeros((1,), jnp.int32), [(0, 0, heads, 0, 0)]
    side = lax.axis_index("groups")
    third = heads // 3
    mine = lax.dynamic_slice_in_dim(w_out, side * third, third, 0)
    ring = [(c, (c + 2) % count) for c in range(count)]
    pairs = [(c, c ^ 1) for c in range(count)]
    arrays, plan = [w_out], [(0, 0, heads, 0, 4)]
    table = [0, side * third, (1 - side) * third, 2 * third]
    table += [depth * ((place - 2 * k) % count) for k in range(4)]
    table += [depth * (((place - 2 * k) % count) ^ 1) for k in range(4)]

    def add(array, parts, row):
        arrays.append(array)
        for start, size, head in parts:
            plan.append((len(arrays) - 1, start, size, head, row))

    both = [(0, third, 1), (third, third, 3)]
    held, across = jnp.concatenate([mine, w_out[2 * third :]], axis=0), None
    for k in range(3):
        moved = lax.ppermute(held, "ctx", ring)
        paired = lax.ppermute(held, "ctx", pairs)
        sent = [moved, paired]
        if k > 0:
            sent.append(swapped(held[:third], "groups"))
            sent.append(swapped(across[:third], "groups"))
        done = work[k]([held])
        sent = after(sent, *done)
        add(sent[0], both, 5 + k)
        add(sent[1], both, 8 + k)
        if k > 0:
            add(sent[2], [(0, third, 2)], 4 + k)
            add(sent[3], [(0, third, 2)], 7 + k)
        held, across = sent[0], sent[1]
    first = lax.ppermute(held[:third], "ctx", pairs)
    last = lax.ppermute(held[third:], "ctx", pairs)
    beside = swapped(held[:third], "groups")
    beyond = swapped(across[:third], "groups")
    done = work[3]([held])
    first = after([first], *done)[0]
    final = swapped(first, "groups")
    work[4]([first])
    add(first, [(0, third, 1)], 11)
    add(last, [(0, third, 3)], 11)
    add(beside, [(0, third, 2)], 7)
    add(beyond, [(0, third, 2)], 10)
    add(final, [(0, third, 2)], 11)
    return arrays, jnp.stack([jnp.asarray(t, jnp.int32) for t in table]), plan


def piece_copies(plan, table, pieces, buf, sem, chunk, chunk_size):
    copies = []
    columns = pl.ds(pl.multiple_of(chunk * chunk_size, chunk_size), chunk_size)
    depth_of = [p.shape[1] for p in pieces]
    for number, (array, start, size, head, row) in enumerate(plan):
        rows = pl.ds(pl.multiple_of(table[row], depth_of[array]), depth_of[array])
        copies.append(
            pltpu.make_async_copy(
                pieces[array].at[pl.ds(start, size), :, columns],
                buf.at[pl.ds(table[head], size), rows, columns],
                sem.at[number, chunk],
            )
        )
    return copies


CHUNKS = 3


def wait_chunk(plan, table, pieces, buf, sem, width):
    step = pl.program_id(0)
    size = width // CHUNKS

    @pl.when(step == 0)
    def _():
        for chunk in range(CHUNKS):
            for copy in piece_copies(plan, table, pieces, buf, sem, chunk, size):
                copy.start()

    for copy in piece_copies(plan, table, pieces, buf, sem, step, size):
        copy.wait()
    return pl.ds(pl.multiple_of(step * size, size), size)


def project_kernel(plan, count, parts, table, core, *refs):
    attn = jnp.concatenate([r[...] for r in refs[:parts]], axis=1)
    refs = refs[parts:]
    pieces, (own, other, buf, sem) = refs[:count], refs[count:]
    heads, head_dim, width = buf.shape
    columns = wait_chunk(plan, table, pieces, buf, sem, width)
    weights = buf[:, :, columns].reshape(heads * head_dim, width // CHUNKS)
    result = dot_nn(attn, weights)
    rows = own.shape[0]

    @pl.when(core[0] == 0)
    def _():
        own[...] = result[:rows]
        other[...] = result[rows:]

    @pl.when(core[0] != 0)
    def _():
        own[...] = result[rows:]
        other[...] = result[:rows]


def project(attn, arrays, table, plan, core, heads, head_dim, width, rows):
    tok = attn[0].shape[0]
    size = width // CHUNKS
    return pl.pallas_call(
        functools.partial(project_kernel, plan, len(arrays), len(attn)),
        grid_spec=pltpu.PrefetchScalarGridSpec(
            num_scalar_prefetch=2,
            grid=(CHUNKS,),
            in_specs=[pl.BlockSpec(a.shape, lambda i, *_: (0, 0)) for a in attn]
            + [pl.BlockSpec(memory_space=pl.ANY)] * len(arrays),
            out_specs=[pl.BlockSpec((rows, size), lambda i, *_: (0, i))] * 2,
            scratch_shapes=[
                pltpu.VMEM((heads, head_dim, width), BF16),
                pltpu.SemaphoreType.DMA((len(plan), CHUNKS)),
            ],
        ),
        out_shape=[jax.ShapeDtypeStruct((rows, width), F32)] * 2,
        compiler_params=params(),
        cost_estimate=cost(2 * tok * heads * head_dim * width, 2 * heads * head_dim * width),
        name="project",
    )(table, core, *attn, *arrays)


def dattn_kernel(plan, count, table, core, own, recv, *refs):
    pieces, (out, grad, acc, buf, sem) = refs[:count], refs[count:]
    heads, head_dim, width = buf.shape
    rows = own.shape[0]
    step = pl.program_id(0)

    @pl.when(core[0] == 0)
    def _():
        grad[:rows] = own[...]
        grad[rows:] = recv[...]

    @pl.when(core[0] != 0)
    def _():
        grad[rows:] = own[...]
        grad[:rows] = recv[...]

    columns = wait_chunk(plan, table, pieces, buf, sem, width)
    weights = buf[:, :, columns].reshape(heads * head_dim, width // CHUNKS)
    part = dot_nt(grad[...], weights)

    @pl.when(step == 0)
    def _():
        acc[...] = part

    @pl.when(step > 0)
    def _():
        acc[...] += part

    @pl.when(step == CHUNKS - 1)
    def _():
        out[...] = acc[...].astype(BF16)


def dattention(own, recv, arrays, table, plan, core, heads, head_dim, width):
    rows = own.shape[0]
    size = width // CHUNKS
    return pl.pallas_call(
        functools.partial(dattn_kernel, plan, len(arrays)),
        grid_spec=pltpu.PrefetchScalarGridSpec(
            num_scalar_prefetch=2,
            grid=(CHUNKS,),
            in_specs=[pl.BlockSpec((rows, size), lambda i, *_: (0, i))] * 2
            + [pl.BlockSpec(memory_space=pl.ANY)] * len(arrays),
            out_specs=pl.BlockSpec((2 * rows, heads * head_dim), lambda i, *_: (0, 0)),
            scratch_shapes=[
                pltpu.VMEM((2 * rows, size), BF16),
                pltpu.VMEM((2 * rows, heads * head_dim), F32),
                pltpu.VMEM((heads, head_dim, width), BF16),
                pltpu.SemaphoreType.DMA((len(plan), CHUNKS)),
            ],
        ),
        out_shape=jax.ShapeDtypeStruct((2 * rows, heads * head_dim), BF16),
        compiler_params=params(),
        cost_estimate=cost(4 * rows * heads * head_dim * width, 2 * heads * head_dim * width),
        name="dattention",
    )(table, core, own, recv, *arrays)


def band_of(refs):
    return jnp.concatenate([r[...] for r in refs], axis=0)


def attention_kernel(scale, place, q, *refs):
    keys, values, (attn, probs) = refs[:BAND_BLOCKS], refs[BAND_BLOCKS : 2 * BAND_BLOCKS], refs[-2:]
    tok = q.shape[0]
    scores = dot_nt(q[...], band_of(keys)) * scale
    shape = scores.shape
    row = lax.broadcasted_iota(jnp.int32, shape, 0)
    column = lax.broadcasted_iota(jnp.int32, shape, 1)
    offset = column - (BAND_BLOCKS - 1) * tok
    admitted = (offset <= row) & (offset + place[0] * tok >= 0)
    scores = jnp.where(admitted, scores, -1e30)
    top = jnp.max(scores, axis=-1, keepdims=True)
    grown = jnp.exp(scores - top)
    weight = (grown * (1.0 / jnp.sum(grown, axis=-1, keepdims=True))).astype(BF16)
    probs[0] = weight
    attn[...] = dot_nn(weight, band_of(values)).astype(BF16)


def attention(queries, bands, place, which, heads, heads_kv, head_dim, scale):
    tok = queries.shape[0]
    group = heads // heads_kv
    keys = pl.BlockSpec((tok, head_dim), lambda h, *_: (0, which))
    values = pl.BlockSpec((tok, head_dim), lambda h, *_: (0, heads_kv + which))
    span = BAND_BLOCKS * tok
    return pl.pallas_call(
        functools.partial(attention_kernel, scale),
        grid_spec=pltpu.PrefetchScalarGridSpec(
            num_scalar_prefetch=1,
            grid=(group,),
            in_specs=[pl.BlockSpec((tok, head_dim), lambda h, *_: (0, which * group + h))]
            + [keys] * BAND_BLOCKS
            + [values] * BAND_BLOCKS,
            out_specs=[
                pl.BlockSpec((tok, head_dim), lambda h, *_: (0, h)),
                pl.BlockSpec((1, tok, span), lambda h, *_: (h, 0, 0)),
            ],
        ),
        out_shape=[
            jax.ShapeDtypeStruct((tok, group * head_dim), BF16),
            jax.ShapeDtypeStruct((group, tok, span), BF16),
        ],
        compiler_params=params(),
        cost_estimate=cost(4 * tok * span * group * head_dim, 2 * group * tok * span, group * tok * span),
        name="attention",
    )(place, queries, *bands, *bands)


def attention_grad_kernel(scale, group, q, dout, attn, probs, *refs):
    keys, values = refs[:BAND_BLOCKS], refs[BAND_BLOCKS : 2 * BAND_BLOCKS]
    dq, outs, (dk, dv) = refs[2 * BAND_BLOCKS], refs[2 * BAND_BLOCKS + 1 : -2], refs[-2:]
    tok, head_dim = q.shape
    head = pl.program_id(0)
    grad = dout[...]
    weight = probs[0]
    delta = jnp.sum(grad.astype(F32) * attn[...].astype(F32), axis=-1, keepdims=True)
    dprob = dot_nt(grad, band_of(values))
    dscore = (weight.astype(F32) * (dprob - delta)).astype(BF16)
    dq[...] = (dot_nn(dscore, band_of(keys)) * scale).astype(BF16)
    dkey = dot_tn(dscore, q[...])
    dvalue = dot_tn(weight, grad)

    @pl.when(head == 0)
    def _():
        dk[...] = dkey
        dv[...] = dvalue

    @pl.when(head > 0)
    def _():
        dk[...] += dkey
        dv[...] += dvalue

    @pl.when(head == group - 1)
    def _():
        for block, out in enumerate(outs):
            rows = pl.ds(block * tok, tok)
            out[:, :head_dim] = (dk[rows, :] * scale).astype(out.dtype)
            out[:, head_dim:] = dv[rows, :].astype(out.dtype)


def attention_grad(queries, dout, attn, probs, bands, which, heads, heads_kv, head_dim, scale):
    tok = queries.shape[0]
    group = heads // heads_kv
    keys = pl.BlockSpec((tok, head_dim), lambda h: (0, which))
    values = pl.BlockSpec((tok, head_dim), lambda h: (0, heads_kv + which))
    per_head = pl.BlockSpec((tok, head_dim), lambda h: (0, h))
    of_all = pl.BlockSpec((tok, head_dim), lambda h: (0, which * group + h))
    span = BAND_BLOCKS * tok
    whole = pl.BlockSpec((tok, 2 * head_dim), lambda h: (0, 0))
    return pl.pallas_call(
        functools.partial(attention_grad_kernel, scale, group),
        grid=(group,),
        in_specs=[of_all, of_all, per_head]
        + [pl.BlockSpec((1, tok, span), lambda h: (h, 0, 0))]
        + [keys] * BAND_BLOCKS
        + [values] * BAND_BLOCKS,
        out_specs=[per_head] + [whole] * BAND_BLOCKS,
        out_shape=[jax.ShapeDtypeStruct((tok, group * head_dim), BF16)]
        + [jax.ShapeDtypeStruct((tok, 2 * head_dim), BF16)] * (BAND_BLOCKS - 1)
        + [jax.ShapeDtypeStruct((tok, 2 * head_dim), F32)],
        scratch_shapes=[pltpu.VMEM((span, head_dim), F32)] * 2,
        compiler_params=params(),
        cost_estimate=cost(8 * tok * span * group * head_dim, 2 * group * tok * span),
        name="attention_grad",
    )(queries, dout, attn, probs, *bands, *bands)


def pick_kernel(slots, here, there, gout, first, second, dgate):
    step = pl.program_id(0)
    rows, width = gout.shape
    room = here.shape[0]
    column = lax.broadcasted_iota(jnp.int32, (rows, room), 1)
    grad = gout[...].astype(F32)
    sums = []
    for i, out in enumerate((first, second)):
        near = (slots[:, i : i + 1] == column).astype(BF16)
        far = (slots[:, i : i + 1] == column + room).astype(BF16)
        row = dot_nn(near, here[...]) + dot_nn(far, there[...])
        out[...] = row.astype(BF16)
        sums.append(jnp.sum(grad * row, axis=-1, keepdims=True))
    lane = lax.broadcasted_iota(jnp.int32, dgate.shape, 1)
    total = jnp.where(lane == 0, sums[0], jnp.where(lane == 1, sums[1], 0.0))

    @pl.when(step == 0)
    def _():
        dgate[...] = total

    @pl.when(step > 0)
    def _():
        dgate[...] += total


def pick(slots, here, there, grad_out):
    rows, width = grad_out.shape
    room = here.shape[0]
    size = width // CHUNKS
    by_column = lambda n: pl.BlockSpec((n, size), lambda i: (0, i))
    return pl.pallas_call(
        pick_kernel,
        grid=(CHUNKS,),
        in_specs=[pl.BlockSpec((rows, 2), lambda i: (0, 0)), by_column(room), by_column(room), by_column(rows)],
        out_specs=[by_column(rows), by_column(rows), pl.BlockSpec((rows, 128), lambda i: (0, 0))],
        out_shape=[jax.ShapeDtypeStruct((rows, width), BF16)] * 2 + [jax.ShapeDtypeStruct((rows, 128), F32)],
        compiler_params=params(),
        cost_estimate=cost(8 * rows * room * width, 8 * rows * width + 4 * room * width),
        name="pick",
    )(slots, here, there, grad_out)


def middle_kernel(routes, own, recv, stream, first, second, gout, dgate, router, router_t, mixed, grad, gates):
    resid = stream[...].astype(F32) + (own[...] + recv[...])
    inverse = lax.rsqrt(jnp.mean(resid * resid, axis=-1, keepdims=True) + 1e-05)
    normed = (resid * inverse).astype(BF16)
    logits = dot_nn(normed, router[...])
    lane = lax.broadcasted_iota(jnp.int32, logits.shape, 1)
    is_first, is_second = lane == routes[:, 0:1], lane == routes[:, 1:2]
    chosen_first = jnp.sum(jnp.where(is_first, logits, 0.0), axis=-1, keepdims=True)
    chosen_second = jnp.sum(jnp.where(is_second, logits, 0.0), axis=-1, keepdims=True)
    gate_first = 1.0 / (1.0 + jnp.exp(chosen_second - chosen_first))
    gate_second = 1.0 - gate_first
    mixed[...] = (
        resid + gate_first * first[...].astype(F32) + gate_second * second[...].astype(F32)
    ).astype(BF16)
    d_first, d_second = dgate[:, 0:1], dgate[:, 1:2]
    common = gate_first * d_first + gate_second * d_second
    dlogit = jnp.where(is_first, gate_first * (d_first - common), 0.0)
    dlogit = dlogit + jnp.where(is_second, gate_second * (d_second - common), 0.0)
    high = dlogit.astype(BF16)
    rest = dlogit - high.astype(F32)
    middle = rest.astype(BF16)
    low = (rest - middle.astype(F32)).astype(BF16)
    weights = router_t[...]
    dnormed = dot_nn(high, weights) + (dot_nn(middle, weights) + dot_nn(low, weights))
    mean = jnp.mean(dnormed * resid, axis=-1, keepdims=True)
    grad[...] = (
        gout[...].astype(F32) + inverse * dnormed - resid * (inverse * inverse * inverse * mean)
    ).astype(BF16)
    gates[...] = jnp.where(lane == 0, gate_first, jnp.where(lane == 1, gate_second, 0.0))


def middle(routes, own, recv, stream, first, second, grad_out, dgate, router, router_t):
    rows, width = stream.shape
    size = 32 if rows % 32 == 0 else rows
    by_row = lambda n: pl.BlockSpec((size, n), lambda i: (i, 0))
    whole = lambda a: pl.BlockSpec(a.shape, lambda i: (0, 0))
    return pl.pallas_call(
        middle_kernel,
        grid=(rows // size,),
        in_specs=[by_row(2)] + [by_row(width)] * 6 + [by_row(128), whole(router), whole(router_t)],
        out_specs=[by_row(width), by_row(width), by_row(128)],
        out_shape=[jax.ShapeDtypeStruct((rows, width), BF16)] * 2 + [jax.ShapeDtypeStruct((rows, 128), F32)],
        compiler_params=params(),
        cost_estimate=cost(2 * rows * 128 * width * 4, 20 * rows * width),
        name="middle",
    )(routes, own, recv, stream, first, second, grad_out, dgate, router, router_t)


def spread_kernel(slots, gates, gout, here, there):
    room = here.shape[0]
    rows = gout.shape[0]
    place = lax.broadcasted_iota(jnp.int32, (room, rows), 0)
    grad = gout[...].astype(F32)
    near, far = 0.0, 0.0
    for i in range(2):
        part = (gates[:, i : i + 1] * grad).astype(BF16)
        near = near + dot_nn((slots[i : i + 1, :] == place).astype(BF16), part)
        far = far + dot_nn((slots[i : i + 1, :] == place + room).astype(BF16), part)
    here[...] = near.astype(BF16)
    there[...] = far.astype(BF16)


def spread(slots_t, gates, grad_out, room):
    rows, width = grad_out.shape
    size = width // CHUNKS
    by_column = lambda n: pl.BlockSpec((n, size), lambda i: (0, i))
    return pl.pallas_call(
        spread_kernel,
        grid=(CHUNKS,),
        in_specs=[
            pl.BlockSpec((2, rows), lambda i: (0, 0)),
            pl.BlockSpec((rows, 128), lambda i: (0, 0)),
            by_column(rows),
        ],
        out_specs=[by_column(room)] * 2,
        out_shape=[jax.ShapeDtypeStruct((room, width), BF16)] * 2,
        compiler_params=params(),
        cost_estimate=cost(8 * rows * room * width, 2 * rows * width + 4 * room * width),
        name="spread",
    )(slots_t, gates, grad_out)


def local(
    queries_in, rotated_keys, value_inputs, stream_in, w_out, w_router, routes, expert_out, grad_out
):
    place = lax.axis_index("ctx")
    core = lax.axis_index("exp")
    tok, heads_q, head_dim = queries_in.shape
    heads_kv = rotated_keys.shape[1]
    rows, width = stream_in.shape
    experts = w_router.shape[1]
    held, capacity = expert_out.shape[1], expert_out.shape[3]
    room = held * capacity
    scale = head_dim ** (-0.5)
    core_arg = core.astype(jnp.int32).reshape(1)
    place_arg = place.astype(jnp.int32).reshape(1)

    own_band = jnp.concatenate(
        [rotated_keys.reshape(tok, heads_kv * head_dim), value_inputs.reshape(tok, heads_kv * head_dim)], axis=1
    )
    queries = queries_in.reshape(tok, heads_q * head_dim)
    sent = lax.dynamic_index_in_dim(expert_out[0], 1 - core, 1, keepdims=False).reshape(room, width)
    kept = lax.dynamic_index_in_dim(expert_out[0], core, 1, keepdims=False).reshape(room, width)
    flat = routes.reshape(-1)
    number = jnp.arange(2 * rows, dtype=jnp.int32)
    earlier = (flat[None, :] == flat[:, None]) & (number[None, :] < number[:, None])
    rank = jnp.sum(earlier.astype(jnp.int32), axis=1)
    slots = (flat * capacity + rank - core * room) % (experts * capacity)
    slots = slots.reshape(rows, 2)
    made = {}

    def round_0(ready):
        made["arrived"] = swapped(sent, "exp")
        made["queries"] = queries
        return [made["arrived"], queries, own_band, slots]

    def round_1(ready):
        band = after([own_band], *ready)[0]
        bands = [band] + [passed_along(band, "ctx", step) for step in range(1, BAND_BLOCKS)]
        made["bands"] = bands[::-1]
        arrived = after([made["arrived"]], *ready)[0]
        made["picked"] = pick(slots, kept, arrived, grad_out)
        return [*made["bands"], made["picked"][2]]

    def attend(which):
        def task(ready):
            bands = after(made["bands"], *ready)
            made[which] = attention(queries, bands, place_arg, which, heads_q, heads_kv, head_dim, scale)
            return [made[which][0]]

        return task

    tasks = [round_0, round_1, attend(0), lambda ready: (), attend(1)]
    if heads_kv != 2:
        tasks[4] = lambda ready: [attend(i)(ready) for i in range(1, heads_kv)]
    arrays, table, plan = gathered(w_out, tasks)
    first, second, dgate = made["picked"]
    attn, probs = zip(*[made[i] for i in range(heads_kv)])
    bands = made["bands"]

    own, other = project(attn, arrays, table, plan, core_arg, heads_q, head_dim, width, rows)
    router = jnp.pad(w_router, ((0, 0), (0, 128 - experts)))
    mixed, grad_input, gates = middle(
        routes, own, swapped(other, "exp"), stream_in, first, second, grad_out, dgate, router, router.T
    )
    grad_other = swapped(grad_input, "exp")
    here, there = spread(slots.T, gates, grad_out, room)
    back = swapped(there, "exp").reshape(held, 1, capacity, width)
    here = here.reshape(held, 1, capacity, width)
    grad_expert = jnp.where(
        core == 0, jnp.concatenate([here, back], axis=1), jnp.concatenate([back, here], axis=1)
    )[None]

    dattn = dattention(grad_input, grad_other, arrays, table, plan, core_arg, heads_q, head_dim, width)
    grads, totals = [], []
    for i in range(heads_kv):
        grad = attention_grad(queries, dattn, attn[i], probs[i], bands, i, heads_q, heads_kv, head_dim, scale)
        passed = [passed_along(grad[BAND_BLOCKS - step], "ctx", -step) for step in range(1, BAND_BLOCKS)]
        grads.append(grad)
        totals.append(passed)
    grad_q = jnp.concatenate([g[0] for g in grads], axis=1).reshape(tok, heads_q, head_dim)
    totals, grad_q, grad_expert = lax.optimization_barrier((totals, grad_q, grad_expert))
    sums = []
    for grad, passed in zip(grads, totals):
        total = grad[BAND_BLOCKS]
        for part in passed:
            total = total + part.astype(F32)
        sums.append(total.astype(BF16))
    grad_k = jnp.stack([t[:, :head_dim] for t in sums], axis=1)
    grad_v = jnp.stack([t[:, head_dim:] for t in sums], axis=1)
    return (mixed, grad_input, grad_expert, grad_q, grad_k, grad_v)


def solution(mesh):
    in_specs = (
        P(("groups", "ctx"), "exp", None),
        P(("groups", "ctx"), "exp", None),
        P(("groups", "ctx"), "exp", None),
        P(("groups", "ctx", "exp"), None),
        P("exp", "ctx", None),
        P(),
        P(("groups", "ctx", "exp"), None),
        P(("groups", "ctx"), "exp", None, None, None),
        P(("groups", "ctx", "exp"), None),
    )
    out_specs = (
        P(("groups", "ctx", "exp"), None),
        P(("groups", "ctx", "exp"), None),
        P(("groups", "ctx"), "exp", None, None, None),
        P(("groups", "ctx"), "exp", None),
        P(("groups", "ctx"), "exp", None),
        P(("groups", "ctx"), "exp", None),
    )
    return jax.shard_map(local, mesh=mesh, in_specs=in_specs, out_specs=out_specs, check_vma=False)
```

```python
import functools

import jax
import jax.numpy as jnp
from jax import lax
from jax.experimental import pallas as pl
from jax.experimental.pallas import tpu as pltpu
from jax.sharding import PartitionSpec as P

BAND_BLOCKS = 4
F32 = jnp.float32
BF16 = jnp.bfloat16
VMEM_LIMIT = 56 * 1024 * 1024


def params(limit=VMEM_LIMIT):
    return pltpu.CompilerParams(vmem_limit_bytes=limit)


def cost(flops, nbytes, exps=0):
    return pl.CostEstimate(flops=flops, bytes_accessed=nbytes, transcendentals=exps)


def dot_nn(a, b):
    return lax.dot_general(a, b, (((1,), (0,)), ((), ())), preferred_element_type=F32)


def dot_nt(a, b):
    return lax.dot_general(a, b, (((1,), (1,)), ((), ())), preferred_element_type=F32)


def dot_tn(a, b):
    return lax.dot_general(a, b, (((0,), (0,)), ((), ())), preferred_element_type=F32)


def passed_along(value, axis, steps):
    count = lax.axis_size(axis)
    initial, last = (max(0, -steps), min(count, count - steps))
    return lax.ppermute(value, axis, [(source, source + steps) for source in range(initial, last)])


def swapped(value, axis):
    return lax.ppermute(value, axis, [(0, 1), (1, 0)])


def after(values, *others):
    return lax.optimization_barrier((tuple(values), others))[0]


def gathered(w_out, first_task, second_task, last_task):
    heads, depth, _ = w_out.shape
    count = lax.axis_size("ctx")
    place = lax.axis_index("ctx")
    if count != 8 or lax.axis_size("groups") != 2 or heads % 2:
        full = lax.all_gather(w_out, "ctx", axis=1, tiled=True)
        for task in (first_task, second_task, last_task):
            task()
        return [full], jnp.zeros((1,), jnp.int32), [(0, heads, 0, 0)]
    side = lax.axis_index("groups")
    half = heads // 2
    ring = lambda value: lax.ppermute(value, "ctx", [(c, (c + 2) % count) for c in range(count)])
    pair = lambda value: lax.ppermute(value, "ctx", [(c, c ^ 1) for c in range(count)])
    cross = lambda value: swapped(value, "groups")
    mine = lax.dynamic_slice_in_dim(w_out, side * half, half, 0)

    z1, y0 = ring(mine), pair(mine)
    (z1,) = after([z1], *first_task())
    z2, y1, x1 = ring(z1), pair(z1), cross(z1)
    z2, y0 = after([z2, y0], *second_task())
    z3, y2, x2 = ring(z2), pair(z2), cross(y0)
    z3, x1 = after([z3, x1], y1)
    z4, y3, x3 = ring(x1), pair(z3), cross(z3)
    y2, z4 = after([y2, z4], x2, y2)
    x4 = cross(y2)
    y3, last = after([y3, x1], x3, z4)
    y4, x5 = pair(last), cross(y3)
    last_task(z4, x3)

    table = [0, side * half, (1 - side) * half]
    table += [depth * ((place - 2 * k) % count) for k in range(4)]
    table += [depth * (((place - 2 * k) % count) ^ 1) for k in range(4)]
    arrays = [w_out, z1, z2, z3, y0, y1, y2, y3, x1, z4, x3, x2, y4, x4, x5]
    plan = [(0, heads, 0, 3)]
    plan += [(1 + k, half, 1, 4 + k) for k in range(7)]
    plan += [(8 + k, half, 2, 4 + k) for k in range(7)]
    return arrays, jnp.stack([jnp.asarray(t, jnp.int32) for t in table]), plan


def piece_copies(plan, table, pieces, buf, sem, chunk, chunk_size):
    copies = []
    columns = pl.ds(pl.multiple_of(chunk * chunk_size, chunk_size), chunk_size)
    depth_of = [p.shape[1] for p in pieces]
    for number, (array, size, head, row) in enumerate(plan):
        rows = pl.ds(pl.multiple_of(table[row], depth_of[array]), depth_of[array])
        copies.append(
            pltpu.make_async_copy(
                pieces[array].at[:, :, columns],
                buf.at[pl.ds(table[head], size), rows, columns],
                sem.at[number, chunk],
            )
        )
    return copies


CHUNKS = 3


def wait_chunk(plan, table, pieces, buf, sem, width):
    step = pl.program_id(0)
    size = width // CHUNKS

    @pl.when(step == 0)
    def _():
        for chunk in range(CHUNKS):
            for copy in piece_copies(plan, table, pieces, buf, sem, chunk, size):
                copy.start()

    for copy in piece_copies(plan, table, pieces, buf, sem, step, size):
        copy.wait()
    return pl.ds(pl.multiple_of(step * size, size), size)


def project_kernel(plan, count, parts, table, core, *refs):
    attn = jnp.concatenate([r[...] for r in refs[:parts]], axis=1)
    refs = refs[parts:]
    pieces, (own, other, buf, sem) = refs[:count], refs[count:]
    heads, head_dim, width = buf.shape
    columns = wait_chunk(plan, table, pieces, buf, sem, width)
    weights = buf[:, :, columns].reshape(heads * head_dim, width // CHUNKS)
    result = dot_nn(attn, weights)
    rows = own.shape[0]

    @pl.when(core[0] == 0)
    def _():
        own[...] = result[:rows]
        other[...] = result[rows:]

    @pl.when(core[0] != 0)
    def _():
        own[...] = result[rows:]
        other[...] = result[:rows]


def project(attn, arrays, table, plan, core, heads, head_dim, width, rows):
    tok = attn[0].shape[0]
    size = width // CHUNKS
    return pl.pallas_call(
        functools.partial(project_kernel, plan, len(arrays), len(attn)),
        grid_spec=pltpu.PrefetchScalarGridSpec(
            num_scalar_prefetch=2,
            grid=(CHUNKS,),
            in_specs=[pl.BlockSpec(a.shape, lambda i, *_: (0, 0)) for a in attn]
            + [pl.BlockSpec(memory_space=pl.ANY)] * len(arrays),
            out_specs=[pl.BlockSpec((rows, size), lambda i, *_: (0, i))] * 2,
            scratch_shapes=[
                pltpu.VMEM((heads, head_dim, width), BF16),
                pltpu.SemaphoreType.DMA((len(plan), CHUNKS)),
            ],
        ),
        out_shape=[jax.ShapeDtypeStruct((rows, width), F32)] * 2,
        compiler_params=params(),
        cost_estimate=cost(2 * tok * heads * head_dim * width, 2 * heads * head_dim * width),
        name="project",
    )(table, core, *attn, *arrays)


def dattn_kernel(plan, count, table, core, own, recv, *refs):
    pieces, (out, grad, acc, buf, sem) = refs[:count], refs[count:]
    heads, head_dim, width = buf.shape
    rows = own.shape[0]
    step = pl.program_id(0)

    @pl.when(core[0] == 0)
    def _():
        grad[:rows] = own[...]
        grad[rows:] = recv[...]

    @pl.when(core[0] != 0)
    def _():
        grad[rows:] = own[...]
        grad[:rows] = recv[...]

    columns = wait_chunk(plan, table, pieces, buf, sem, width)
    weights = buf[:, :, columns].reshape(heads * head_dim, width // CHUNKS)
    part = dot_nt(grad[...], weights)

    @pl.when(step == 0)
    def _():
        acc[...] = part

    @pl.when(step > 0)
    def _():
        acc[...] += part

    @pl.when(step == CHUNKS - 1)
    def _():
        out[...] = acc[...].astype(BF16)


def dattention(own, recv, arrays, table, plan, core, heads, head_dim, width):
    rows = own.shape[0]
    size = width // CHUNKS
    return pl.pallas_call(
        functools.partial(dattn_kernel, plan, len(arrays)),
        grid_spec=pltpu.PrefetchScalarGridSpec(
            num_scalar_prefetch=2,
            grid=(CHUNKS,),
            in_specs=[pl.BlockSpec((rows, size), lambda i, *_: (0, i))] * 2
            + [pl.BlockSpec(memory_space=pl.ANY)] * len(arrays),
            out_specs=pl.BlockSpec((2 * rows, heads * head_dim), lambda i, *_: (0, 0)),
            scratch_shapes=[
                pltpu.VMEM((2 * rows, size), BF16),
                pltpu.VMEM((2 * rows, heads * head_dim), F32),
                pltpu.VMEM((heads, head_dim, width), BF16),
                pltpu.SemaphoreType.DMA((len(plan), CHUNKS)),
            ],
        ),
        out_shape=jax.ShapeDtypeStruct((2 * rows, heads * head_dim), BF16),
        compiler_params=params(),
        cost_estimate=cost(4 * rows * heads * head_dim * width, 2 * heads * head_dim * width),
        name="dattention",
    )(table, core, own, recv, *arrays)


def band_of(refs):
    return jnp.concatenate([r[...] for r in refs], axis=0)


def attention_kernel(scale, place, q, *refs):
    keys, values, (attn, probs) = refs[:BAND_BLOCKS], refs[BAND_BLOCKS : 2 * BAND_BLOCKS], refs[-2:]
    tok = q.shape[0]
    scores = dot_nt(q[...], band_of(keys)) * scale
    shape = scores.shape
    row = lax.broadcasted_iota(jnp.int32, shape, 0)
    column = lax.broadcasted_iota(jnp.int32, shape, 1)
    offset = column - (BAND_BLOCKS - 1) * tok
    admitted = (offset <= row) & (offset + place[0] * tok >= 0)
    scores = jnp.where(admitted, scores, -1e30)
    top = jnp.max(scores, axis=-1, keepdims=True)
    grown = jnp.exp(scores - top)
    weight = (grown * (1.0 / jnp.sum(grown, axis=-1, keepdims=True))).astype(BF16)
    probs[0] = weight
    attn[...] = dot_nn(weight, band_of(values)).astype(BF16)


def attention(queries, bands, place, heads, heads_kv, head_dim, scale):
    tok = queries.shape[1]
    group = heads // heads_kv
    keys = pl.BlockSpec((tok, head_dim), lambda h, *_: (0, h // group))
    values = pl.BlockSpec((tok, head_dim), lambda h, *_: (0, heads_kv + h // group))
    span = BAND_BLOCKS * tok
    return pl.pallas_call(
        functools.partial(attention_kernel, scale),
        grid_spec=pltpu.PrefetchScalarGridSpec(
            num_scalar_prefetch=1,
            grid=(heads,),
            in_specs=[pl.BlockSpec((None, tok, head_dim), lambda h, *_: (h, 0, 0))]
            + [keys] * BAND_BLOCKS
            + [values] * BAND_BLOCKS,
            out_specs=[
                pl.BlockSpec((tok, head_dim), lambda h, *_: (0, h)),
                pl.BlockSpec((1, tok, span), lambda h, *_: (h, 0, 0)),
            ],
        ),
        out_shape=[
            jax.ShapeDtypeStruct((tok, heads * head_dim), BF16),
            jax.ShapeDtypeStruct((heads, tok, span), BF16),
        ],
        compiler_params=params(),
        cost_estimate=cost(4 * tok * span * heads * head_dim, 2 * heads * tok * span, heads * tok * span),
        name="attention",
    )(place, queries, *bands, *bands)


def attention_grad_kernel(scale, group, given, q, dout, attn, probs, *refs):
    refs = refs[:2 * BAND_BLOCKS] + refs[2 * BAND_BLOCKS + given :]
    keys, values = refs[:BAND_BLOCKS], refs[BAND_BLOCKS : 2 * BAND_BLOCKS]
    dq, outs, (dk, dv) = refs[2 * BAND_BLOCKS], refs[2 * BAND_BLOCKS + 1 : -2], refs[-2:]
    tok, head_dim = q.shape
    head = pl.program_id(0)
    grad = dout[...]
    weight = probs[0]
    delta = jnp.sum(grad.astype(F32) * attn[...].astype(F32), axis=-1, keepdims=True)
    dprob = dot_nt(grad, band_of(values))
    dscore = (weight.astype(F32) * (dprob - delta)).astype(BF16)
    dq[...] = (dot_nn(dscore, band_of(keys)) * scale).astype(BF16)
    dkey = dot_tn(dscore, q[...])
    dvalue = dot_tn(weight, grad)

    @pl.when(head == 0)
    def _():
        dk[...] = dkey
        dv[...] = dvalue

    @pl.when(head > 0)
    def _():
        dk[...] += dkey
        dv[...] += dvalue

    @pl.when(head == group - 1)
    def _():
        for block, out in enumerate(outs):
            rows = pl.ds(block * tok, tok)
            out[:, :head_dim] = (dk[rows, :] * scale).astype(out.dtype)
            out[:, head_dim:] = dv[rows, :].astype(out.dtype)


def attention_grad(queries, dout, attn, probs, bands, which, grad_q, heads_kv, scale):
    heads, tok, head_dim = queries.shape
    group = heads // heads_kv
    keys = pl.BlockSpec((tok, head_dim), lambda h: (0, which))
    values = pl.BlockSpec((tok, head_dim), lambda h: (0, heads_kv + which))
    by_head = pl.BlockSpec((None, tok, head_dim), lambda h: (which * group + h, 0, 0))
    of_all = pl.BlockSpec((tok, head_dim), lambda h: (0, which * group + h))
    span = BAND_BLOCKS * tok
    whole = pl.BlockSpec((tok, 2 * head_dim), lambda h: (0, 0))
    given = [] if grad_q is None else [grad_q]
    return pl.pallas_call(
        functools.partial(attention_grad_kernel, scale, group, len(given)),
        grid=(group,),
        in_specs=[by_head, of_all, of_all]
        + [pl.BlockSpec((1, tok, span), lambda h: (which * group + h, 0, 0))]
        + [keys] * BAND_BLOCKS
        + [values] * BAND_BLOCKS
        + [pl.BlockSpec(memory_space=pl.ANY)] * len(given),
        out_specs=[by_head] + [whole] * BAND_BLOCKS,
        out_shape=[jax.ShapeDtypeStruct((heads, tok, head_dim), BF16)]
        + [jax.ShapeDtypeStruct((tok, 2 * head_dim), BF16)] * (BAND_BLOCKS - 1)
        + [jax.ShapeDtypeStruct((tok, 2 * head_dim), F32)],
        scratch_shapes=[pltpu.VMEM((span, head_dim), F32)] * 2,
        input_output_aliases={4 + 2 * BAND_BLOCKS: 0} if given else {},
        compiler_params=params(),
        cost_estimate=cost(tok, tok),
        name="attention_grad",
    )(queries, dout, attn, probs, *bands, *bands, *given)


def pick_kernel(slots, here, there, gout, first, second, dgate):
    step = pl.program_id(0)
    rows, width = gout.shape
    room = here.shape[0]
    column = lax.broadcasted_iota(jnp.int32, (rows, room), 1)
    grad = gout[...].astype(F32)
    sums = []
    for i, out in enumerate((first, second)):
        near = (slots[:, i : i + 1] == column).astype(BF16)
        far = (slots[:, i : i + 1] == column + room).astype(BF16)
        row = dot_nn(near, here[...]) + dot_nn(far, there[...])
        out[...] = row.astype(BF16)
        sums.append(jnp.sum(grad * row, axis=-1, keepdims=True))
    lane = lax.broadcasted_iota(jnp.int32, dgate.shape, 1)
    total = jnp.where(lane == 0, sums[0], jnp.where(lane == 1, sums[1], 0.0))

    @pl.when(step == 0)
    def _():
        dgate[...] = total

    @pl.when(step > 0)
    def _():
        dgate[...] += total


def pick(slots, here, there, grad_out):
    rows, width = grad_out.shape
    room = here.shape[0]
    size = width // CHUNKS
    by_column = lambda n: pl.BlockSpec((n, size), lambda i: (0, i))
    return pl.pallas_call(
        pick_kernel,
        grid=(CHUNKS,),
        in_specs=[pl.BlockSpec((rows, 2), lambda i: (0, 0)), by_column(room), by_column(room), by_column(rows)],
        out_specs=[by_column(rows), by_column(rows), pl.BlockSpec((rows, 128), lambda i: (0, 0))],
        out_shape=[jax.ShapeDtypeStruct((rows, width), BF16)] * 2 + [jax.ShapeDtypeStruct((rows, 128), F32)],
        compiler_params=params(),
        cost_estimate=cost(8 * rows * room * width, 8 * rows * width + 4 * room * width),
        name="pick",
    )(slots, here, there, grad_out)


def middle_kernel(routes, own, recv, stream, first, second, gout, dgate, router, router_t, mixed, grad, gates):
    resid = stream[...].astype(F32) + (own[...] + recv[...])
    inverse = lax.rsqrt(jnp.mean(resid * resid, axis=-1, keepdims=True) + 1e-05)
    normed = (resid * inverse).astype(BF16)
    logits = dot_nn(normed, router[...])
    lane = lax.broadcasted_iota(jnp.int32, logits.shape, 1)
    is_first, is_second = lane == routes[:, 0:1], lane == routes[:, 1:2]
    chosen_first = jnp.sum(jnp.where(is_first, logits, 0.0), axis=-1, keepdims=True)
    chosen_second = jnp.sum(jnp.where(is_second, logits, 0.0), axis=-1, keepdims=True)
    gate_first = 1.0 / (1.0 + jnp.exp(chosen_second - chosen_first))
    gate_second = 1.0 - gate_first
    mixed[...] = (
        resid + gate_first * first[...].astype(F32) + gate_second * second[...].astype(F32)
    ).astype(BF16)
    d_first, d_second = dgate[:, 0:1], dgate[:, 1:2]
    common = gate_first * d_first + gate_second * d_second
    dlogit = jnp.where(is_first, gate_first * (d_first - common), 0.0)
    dlogit = dlogit + jnp.where(is_second, gate_second * (d_second - common), 0.0)
    high = dlogit.astype(BF16)
    rest = dlogit - high.astype(F32)
    middle = rest.astype(BF16)
    low = (rest - middle.astype(F32)).astype(BF16)
    weights = router_t[...]
    dnormed = dot_nn(high, weights) + (dot_nn(middle, weights) + dot_nn(low, weights))
    mean = jnp.mean(dnormed * resid, axis=-1, keepdims=True)
    grad[...] = (
        gout[...].astype(F32) + inverse * dnormed - resid * (inverse * inverse * inverse * mean)
    ).astype(BF16)
    gates[...] = jnp.where(lane == 0, gate_first, jnp.where(lane == 1, gate_second, 0.0))


def middle(routes, own, recv, stream, first, second, grad_out, dgate, router, router_t):
    rows, width = stream.shape
    size = 32 if rows % 32 == 0 else rows
    by_row = lambda n: pl.BlockSpec((size, n), lambda i: (i, 0))
    whole = lambda a: pl.BlockSpec(a.shape, lambda i: (0, 0))
    return pl.pallas_call(
        middle_kernel,
        grid=(rows // size,),
        in_specs=[by_row(2)] + [by_row(width)] * 6 + [by_row(128), whole(router), whole(router_t)],
        out_specs=[by_row(width), by_row(width), by_row(128)],
        out_shape=[jax.ShapeDtypeStruct((rows, width), BF16)] * 2 + [jax.ShapeDtypeStruct((rows, 128), F32)],
        compiler_params=params(),
        cost_estimate=cost(2 * rows * 128 * width * 4, 20 * rows * width),
        name="middle",
    )(routes, own, recv, stream, first, second, grad_out, dgate, router, router_t)


def spread_kernel(slots, gates, gout, here, there):
    room = here.shape[0]
    rows = gout.shape[0]
    place = lax.broadcasted_iota(jnp.int32, (room, rows), 0)
    grad = gout[...].astype(F32)
    near, far = 0.0, 0.0
    for i in range(2):
        part = (gates[:, i : i + 1] * grad).astype(BF16)
        near = near + dot_nn((slots[i : i + 1, :] == place).astype(BF16), part)
        far = far + dot_nn((slots[i : i + 1, :] == place + room).astype(BF16), part)
    here[...] = near.astype(BF16)
    there[...] = far.astype(BF16)


def spread(slots_t, gates, grad_out, room):
    rows, width = grad_out.shape
    size = width // CHUNKS
    by_column = lambda n: pl.BlockSpec((n, size), lambda i: (0, i))
    return pl.pallas_call(
        spread_kernel,
        grid=(CHUNKS,),
        in_specs=[
            pl.BlockSpec((2, rows), lambda i: (0, 0)),
            pl.BlockSpec((rows, 128), lambda i: (0, 0)),
            by_column(rows),
        ],
        out_specs=[by_column(room)] * 2,
        out_shape=[jax.ShapeDtypeStruct((room, width), BF16)] * 2,
        compiler_params=params(),
        cost_estimate=cost(8 * rows * room * width, 2 * rows * width + 4 * room * width),
        name="spread",
    )(slots_t, gates, grad_out)


def local(
    queries_in, rotated_keys, value_inputs, stream_in, w_out, w_router, routes, expert_out, grad_out
):
    place = lax.axis_index("ctx")
    core = lax.axis_index("exp")
    tok, heads_q, head_dim = queries_in.shape
    heads_kv = rotated_keys.shape[1]
    rows, width = stream_in.shape
    experts = w_router.shape[1]
    held, capacity = expert_out.shape[1], expert_out.shape[3]
    room = held * capacity
    scale = head_dim ** (-0.5)
    core_arg = core.astype(jnp.int32).reshape(1)
    place_arg = place.astype(jnp.int32).reshape(1)

    own_band = jnp.concatenate(
        [rotated_keys.reshape(tok, heads_kv * head_dim), value_inputs.reshape(tok, heads_kv * head_dim)], axis=1
    )
    queries = jnp.transpose(queries_in, (1, 0, 2))
    sent = lax.dynamic_index_in_dim(expert_out[0], 1 - core, 1, keepdims=False).reshape(room, width)
    kept = lax.dynamic_index_in_dim(expert_out[0], core, 1, keepdims=False).reshape(room, width)
    flat = routes.reshape(-1)
    number = jnp.arange(2 * rows, dtype=jnp.int32)
    earlier = (flat[None, :] == flat[:, None]) & (number[None, :] < number[:, None])
    rank = jnp.sum(earlier.astype(jnp.int32), axis=1)
    slots = (flat * capacity + rank - core * room) % (experts * capacity)
    slots = slots.reshape(rows, 2)
    router = jnp.pad(w_router, ((0, 0), (0, 128 - experts)))
    router_t = jnp.pad(w_router.T, ((0, 128 - experts), (0, 0)))
    made = {}

    def exchange_rows():
        made["arrived"] = swapped(sent, "exp")
        return [made["arrived"], slots, own_band, router, router_t]

    def pick_rows():
        made["picked"] = pick(slots, kept, made["arrived"], grad_out)
        return [made["picked"][2]]

    def attend(*ready):
        band = after([own_band], *ready)[0]
        bands = [band] + [passed_along(band, "ctx", step) for step in range(1, BAND_BLOCKS)]
        made["bands"] = bands[::-1]
        made["attention"] = attention(
            queries, made["bands"], place_arg, heads_q, heads_kv, head_dim, scale
        )

    arrays, table, plan = gathered(w_out, exchange_rows, pick_rows, attend)
    first, second, dgate = made["picked"]
    attn, probs = made["attention"]
    bands = made["bands"]

    own, other = project([attn], arrays, table, plan, core_arg, heads_q, head_dim, width, rows)
    mixed, grad_input, gates = middle(
        routes, own, swapped(other, "exp"), stream_in, first, second, grad_out, dgate, router, router_t
    )
    grad_other = swapped(grad_input, "exp")
    here, there = spread(slots.T, gates, grad_out, room)
    dattn = dattention(grad_input, grad_other, arrays, table, plan, core_arg, heads_q, head_dim, width)
    there = after([there], dattn)[0]
    back = swapped(there, "exp").reshape(held, 1, capacity, width)
    here = here.reshape(held, 1, capacity, width)
    grad_expert = jnp.where(
        core == 0, jnp.concatenate([here, back], axis=1), jnp.concatenate([back, here], axis=1)
    )[None]
    grads, totals, grad_q = [], [], None
    for i in range(heads_kv):
        grad = attention_grad(queries, dattn, attn, probs, bands, i, grad_q, heads_kv, scale)
        totals.append([passed_along(grad[BAND_BLOCKS - step], "ctx", -step) for step in range(1, BAND_BLOCKS)])
        grads.append(grad)
        grad_q = grad[0]
    grad_q = jnp.transpose(grad_q, (1, 0, 2))
    totals, grad_q, grad_expert = lax.optimization_barrier((totals, grad_q, grad_expert))
    sums = []
    for grad, passed in zip(grads, totals):
        total = grad[BAND_BLOCKS]
        for part in passed:
            total = total + part.astype(F32)
        sums.append(total.astype(BF16))
    grad_k = jnp.stack([t[:, :head_dim] for t in sums], axis=1)
    grad_v = jnp.stack([t[:, head_dim:] for t in sums], axis=1)
    return (mixed, grad_input, grad_expert, grad_q, grad_k, grad_v)


def solution(mesh):
    in_specs = (
        P(("groups", "ctx"), "exp", None),
        P(("groups", "ctx"), "exp", None),
        P(("groups", "ctx"), "exp", None),
        P(("groups", "ctx", "exp"), None),
        P("exp", "ctx", None),
        P(),
        P(("groups", "ctx", "exp"), None),
        P(("groups", "ctx"), "exp", None, None, None),
        P(("groups", "ctx", "exp"), None),
    )
    out_specs = (
        P(("groups", "ctx", "exp"), None),
        P(("groups", "ctx", "exp"), None),
        P(("groups", "ctx"), "exp", None, None, None),
        P(("groups", "ctx"), "exp", None),
        P(("groups", "ctx"), "exp", None),
        P(("groups", "ctx"), "exp", None),
    )
    return jax.shard_map(local, mesh=mesh, in_specs=in_specs, out_specs=out_specs, check_vma=False)
```

```python
import functools

import jax
import jax.numpy as jnp
from jax import lax
from jax.experimental import pallas as pl
from jax.experimental.pallas import tpu as pltpu
from jax.sharding import PartitionSpec as P

BAND_BLOCKS = 4
F32 = jnp.float32
BF16 = jnp.bfloat16
VMEM_LIMIT = 56 * 1024 * 1024


def params(limit=VMEM_LIMIT):
    return pltpu.CompilerParams(vmem_limit_bytes=limit)


def cost(flops, nbytes, exps=0):
    return pl.CostEstimate(flops=flops, bytes_accessed=nbytes, transcendentals=exps)


def dot_nn(a, b):
    return lax.dot_general(a, b, (((1,), (0,)), ((), ())), preferred_element_type=F32)


def dot_nt(a, b):
    return lax.dot_general(a, b, (((1,), (1,)), ((), ())), preferred_element_type=F32)


def dot_tn(a, b):
    return lax.dot_general(a, b, (((0,), (0,)), ((), ())), preferred_element_type=F32)


def passed_along(value, axis, steps):
    count = lax.axis_size(axis)
    initial, last = (max(0, -steps), min(count, count - steps))
    return lax.ppermute(value, axis, [(source, source + steps) for source in range(initial, last)])


def swapped(value, axis):
    return lax.ppermute(value, axis, [(0, 1), (1, 0)])


def after(values, *others):
    return lax.optimization_barrier((tuple(values), others))[0]


def gathered(w_out, *tasks):
    heads, depth, _ = w_out.shape
    count = lax.axis_size("ctx")
    place = lax.axis_index("ctx")
    if count != 8 or lax.axis_size("groups") != 2 or heads % 2:
        full = lax.all_gather(w_out, "ctx", axis=1, tiled=True)
        for task in tasks:
            task()
        return [full], jnp.zeros((1,), jnp.int32), [(0, heads, 0, 0)]
    side = lax.axis_index("groups")
    half = heads // 2
    ring = lambda value: lax.ppermute(value, "ctx", [(c, (c + 2) % count) for c in range(count)])
    pair = lambda value: lax.ppermute(value, "ctx", [(c, c ^ 1) for c in range(count)])
    cross = lambda value: swapped(value, "groups")
    mine = lax.dynamic_slice_in_dim(w_out, side * half, half, 0)

    z1, y0 = ring(mine), pair(mine)
    (z1,) = after([z1], *tasks[0]())
    z2, y1, x1 = ring(z1), pair(z1), cross(z1)
    z2, y0 = after([z2, y0], *tasks[1](z1))
    z3, y2, x2 = ring(z2), pair(z2), cross(y0)
    z3, x1 = after([z3, x1], y1, *tasks[2](z2))
    z4, y3, x3 = ring(x1), pair(z3), cross(z3)
    y2, z4 = after([y2, z4], x2, y2)
    x4 = cross(y2)
    y3, last = after([y3, x1], x3, z4)
    y4, x5 = pair(last), cross(y3)
    tasks[3](z4, x3)

    table = [0, side * half, (1 - side) * half]
    table += [depth * ((place - 2 * k) % count) for k in range(4)]
    table += [depth * (((place - 2 * k) % count) ^ 1) for k in range(4)]
    arrays = [w_out, z1, z2, z3, y0, y1, y2, y3, x1, z4, x3, x2, y4, x4, x5]
    plan = [(0, heads, 0, 3)]
    plan += [(1 + k, half, 1, 4 + k) for k in range(7)]
    plan += [(8 + k, half, 2, 4 + k) for k in range(7)]
    return arrays, jnp.stack([jnp.asarray(t, jnp.int32) for t in table]), plan


def piece_copies(plan, table, pieces, buf, sem, chunk, chunk_size):
    copies = []
    columns = pl.ds(pl.multiple_of(chunk * chunk_size, chunk_size), chunk_size)
    depth_of = [p.shape[1] for p in pieces]
    for number, (array, size, head, row) in enumerate(plan):
        rows = pl.ds(pl.multiple_of(table[row], depth_of[array]), depth_of[array])
        copies.append(
            pltpu.make_async_copy(
                pieces[array].at[:, :, columns],
                buf.at[pl.ds(table[head], size), rows, columns],
                sem.at[number, chunk],
            )
        )
    return copies


CHUNKS = 3


def wait_chunk(plan, table, pieces, buf, sem, width):
    step = pl.program_id(0)
    size = width // CHUNKS

    @pl.when(step == 0)
    def _():
        for chunk in range(CHUNKS):
            for copy in piece_copies(plan, table, pieces, buf, sem, chunk, size):
                copy.start()

    for copy in piece_copies(plan, table, pieces, buf, sem, step, size):
        copy.wait()
    return pl.ds(pl.multiple_of(step * size, size), size)


def project_kernel(plan, count, parts, table, core, *refs):
    attn = jnp.concatenate([r[...] for r in refs[:parts]], axis=1)
    refs = refs[parts:]
    pieces, (own, other, buf, sem) = refs[:count], refs[count:]
    heads, head_dim, width = buf.shape
    columns = wait_chunk(plan, table, pieces, buf, sem, width)
    weights = buf[:, :, columns].reshape(heads * head_dim, width // CHUNKS)
    result = dot_nn(attn, weights)
    rows = own.shape[0]

    @pl.when(core[0] == 0)
    def _():
        own[...] = result[:rows]
        other[...] = result[rows:]

    @pl.when(core[0] != 0)
    def _():
        own[...] = result[rows:]
        other[...] = result[:rows]


def project(attn, arrays, table, plan, core, heads, head_dim, width, rows):
    tok = attn[0].shape[0]
    size = width // CHUNKS
    return pl.pallas_call(
        functools.partial(project_kernel, plan, len(arrays), len(attn)),
        grid_spec=pltpu.PrefetchScalarGridSpec(
            num_scalar_prefetch=2,
            grid=(CHUNKS,),
            in_specs=[pl.BlockSpec(a.shape, lambda i, *_: (0, 0)) for a in attn]
            + [pl.BlockSpec(memory_space=pl.ANY)] * len(arrays),
            out_specs=[pl.BlockSpec((rows, size), lambda i, *_: (0, i))] * 2,
            scratch_shapes=[
                pltpu.VMEM((heads, head_dim, width), BF16),
                pltpu.SemaphoreType.DMA((len(plan), CHUNKS)),
            ],
        ),
        out_shape=[jax.ShapeDtypeStruct((rows, width), F32)] * 2,
        compiler_params=params(),
        cost_estimate=cost(2 * tok * heads * head_dim * width, 2 * heads * head_dim * width),
        name="project",
    )(table, core, *attn, *arrays)


def dattn_kernel(plan, count, table, core, own, recv, *refs):
    pieces, (out, grad, acc, buf, sem) = refs[:count], refs[count:]
    heads, head_dim, width = buf.shape
    rows = own.shape[0]
    step = pl.program_id(0)

    @pl.when(core[0] == 0)
    def _():
        grad[:rows] = own[...]
        grad[rows:] = recv[...]

    @pl.when(core[0] != 0)
    def _():
        grad[rows:] = own[...]
        grad[:rows] = recv[...]

    columns = wait_chunk(plan, table, pieces, buf, sem, width)
    weights = buf[:, :, columns].reshape(heads * head_dim, width // CHUNKS)
    part = dot_nt(grad[...], weights)

    @pl.when(step == 0)
    def _():
        acc[...] = part

    @pl.when(step > 0)
    def _():
        acc[...] += part

    @pl.when(step == CHUNKS - 1)
    def _():
        out[...] = acc[...].astype(BF16)


def dattention(own, recv, arrays, table, plan, core, heads, head_dim, width):
    rows = own.shape[0]
    size = width // CHUNKS
    return pl.pallas_call(
        functools.partial(dattn_kernel, plan, len(arrays)),
        grid_spec=pltpu.PrefetchScalarGridSpec(
            num_scalar_prefetch=2,
            grid=(CHUNKS,),
            in_specs=[pl.BlockSpec((rows, size), lambda i, *_: (0, i))] * 2
            + [pl.BlockSpec(memory_space=pl.ANY)] * len(arrays),
            out_specs=pl.BlockSpec((2 * rows, heads * head_dim), lambda i, *_: (0, 0)),
            scratch_shapes=[
                pltpu.VMEM((2 * rows, size), BF16),
                pltpu.VMEM((2 * rows, heads * head_dim), F32),
                pltpu.VMEM((heads, head_dim, width), BF16),
                pltpu.SemaphoreType.DMA((len(plan), CHUNKS)),
            ],
        ),
        out_shape=jax.ShapeDtypeStruct((2 * rows, heads * head_dim), BF16),
        compiler_params=params(),
        cost_estimate=cost(4 * rows * heads * head_dim * width, 2 * heads * head_dim * width),
        name="dattention",
    )(table, core, own, recv, *arrays)


def band_of(refs):
    return jnp.concatenate([r[...] for r in refs], axis=0)


HEADS_FORWARD = 6
HEADS_BACKWARD = 6


def heads_a_step(most, group):
    return max(n for n in range(1, most + 1) if group % n == 0)


def stacked(ref, count):
    size = ref.shape[1] // count
    return jnp.concatenate([ref[:, i * size : (i + 1) * size] for i in range(count)], axis=0)


def attention_kernel(scale, place, q, *refs):
    keys, values, (attn, probs) = refs[:BAND_BLOCKS], refs[BAND_BLOCKS : 2 * BAND_BLOCKS], refs[-2:]
    count, tok, head_dim = q.shape
    scores = dot_nt(q[...].reshape(count * tok, head_dim), band_of(keys)) * scale
    scores = scores.reshape(count, tok, BAND_BLOCKS * tok)
    row = lax.broadcasted_iota(jnp.int32, scores.shape, 1)
    column = lax.broadcasted_iota(jnp.int32, scores.shape, 2)
    offset = column - (BAND_BLOCKS - 1) * tok
    admitted = (offset <= row) & (offset + place[0] * tok >= 0)
    scores = jnp.where(admitted, scores, -1e30)
    top = jnp.max(scores, axis=-1, keepdims=True)
    grown = jnp.exp(scores - top)
    weight = (grown * (1.0 / jnp.sum(grown, axis=-1, keepdims=True))).astype(BF16)
    probs[...] = weight
    result = dot_nn(weight.reshape(count * tok, BAND_BLOCKS * tok), band_of(values)).astype(BF16)
    for i in range(count):
        attn[:, i * head_dim : (i + 1) * head_dim] = result[i * tok : (i + 1) * tok]


def attention(queries, bands, place, heads, heads_kv, head_dim, scale):
    tok = queries.shape[1]
    group = heads // heads_kv
    count = heads_a_step(HEADS_FORWARD, group)
    keys = pl.BlockSpec((tok, head_dim), lambda h, *_: (0, h * count // group))
    values = pl.BlockSpec((tok, head_dim), lambda h, *_: (0, heads_kv + h * count // group))
    span = BAND_BLOCKS * tok
    return pl.pallas_call(
        functools.partial(attention_kernel, scale),
        grid_spec=pltpu.PrefetchScalarGridSpec(
            num_scalar_prefetch=1,
            grid=(heads // count,),
            in_specs=[pl.BlockSpec((count, tok, head_dim), lambda h, *_: (h, 0, 0))]
            + [keys] * BAND_BLOCKS
            + [values] * BAND_BLOCKS,
            out_specs=[
                pl.BlockSpec((tok, count * head_dim), lambda h, *_: (0, h)),
                pl.BlockSpec((count, tok, span), lambda h, *_: (h, 0, 0)),
            ],
        ),
        out_shape=[
            jax.ShapeDtypeStruct((tok, heads * head_dim), BF16),
            jax.ShapeDtypeStruct((heads, tok, span), BF16),
        ],
        compiler_params=params(),
        cost_estimate=cost(4 * tok * span * heads * head_dim, 2 * heads * tok * span, heads * tok * span),
        name="attention",
    )(place, queries, *bands, *bands)


def attention_grad_kernel(scale, steps, last, q, dout, attn, probs, *refs):
    refs = list(refs)
    keys, values = refs[:BAND_BLOCKS], refs[BAND_BLOCKS : 2 * BAND_BLOCKS]
    refs = refs[2 * BAND_BLOCKS :]
    if last:
        (_, core, here, back), refs, sem = refs[:4], refs[4:-1], refs[-1]
        joined = refs.pop(1 + BAND_BLOCKS)
        copies = [
            pltpu.make_async_copy(here, joined.at[0, :, core[0]], sem.at[0]),
            pltpu.make_async_copy(back, joined.at[0, :, 1 - core[0]], sem.at[1]),
        ]

        @pl.when(pl.program_id(0) == 0)
        def _():
            for copy in copies:
                copy.start()

    dq, outs, (dk, dv) = refs[0], refs[1:-2], refs[-2:]
    count, tok, head_dim = q.shape
    step = pl.program_id(0)
    grad = stacked(dout, count)
    weight = probs[...].reshape(count * tok, BAND_BLOCKS * tok)
    delta = jnp.sum(grad.astype(F32) * stacked(attn, count).astype(F32), axis=-1, keepdims=True)
    dprob = dot_nt(grad, band_of(values))
    dscore = (weight.astype(F32) * (dprob - delta)).astype(BF16)
    dq[...] = (dot_nn(dscore, band_of(keys)) * scale).astype(BF16).reshape(count, tok, head_dim)
    dkey = dot_tn(dscore, q[...].reshape(count * tok, head_dim))
    dvalue = dot_tn(weight, grad)

    @pl.when(step == 0)
    def _():
        dk[...] = dkey
        dv[...] = dvalue

    @pl.when(step > 0)
    def _():
        dk[...] += dkey
        dv[...] += dvalue

    @pl.when(step == steps - 1)
    def _():
        for block, out in enumerate(outs):
            rows = pl.ds(block * tok, tok)
            out[:, :head_dim] = (dk[rows, :] * scale).astype(out.dtype)
            out[:, head_dim:] = dv[rows, :].astype(out.dtype)
        if last:
            for copy in copies:
                copy.wait()


def attention_grad(queries, dout, attn, probs, bands, which, given, heads_kv, scale):
    heads, tok, head_dim = queries.shape
    group = heads // heads_kv
    count = heads_a_step(HEADS_BACKWARD, group)
    steps = group // count
    keys = pl.BlockSpec((tok, head_dim), lambda h: (0, which))
    values = pl.BlockSpec((tok, head_dim), lambda h: (0, heads_kv + which))
    by_head = pl.BlockSpec((count, tok, head_dim), lambda h: (which * steps + h, 0, 0))
    of_all = pl.BlockSpec((tok, count * head_dim), lambda h: (0, which * steps + h))
    span = BAND_BLOCKS * tok
    whole = pl.BlockSpec((tok, 2 * head_dim), lambda h: (0, 0))
    anywhere = pl.BlockSpec(memory_space=pl.ANY)
    last = bool(given)
    joined = []
    if last:
        held, capacity, width = given[2].shape
        joined = [jax.ShapeDtypeStruct((1, held, 2, capacity, width), BF16)]
    return pl.pallas_call(
        functools.partial(attention_grad_kernel, scale, steps, last),
        grid=(steps,),
        in_specs=[by_head, of_all, of_all]
        + [pl.BlockSpec((count, tok, span), lambda h: (which * steps + h, 0, 0))]
        + [keys] * BAND_BLOCKS
        + [values] * BAND_BLOCKS
        + ([anywhere, pl.BlockSpec(memory_space=pltpu.SMEM), anywhere, anywhere] if last else []),
        out_specs=[by_head] + [whole] * BAND_BLOCKS + [anywhere] * len(joined),
        out_shape=[jax.ShapeDtypeStruct((heads, tok, head_dim), BF16)]
        + [jax.ShapeDtypeStruct((tok, 2 * head_dim), BF16)] * (BAND_BLOCKS - 1)
        + [jax.ShapeDtypeStruct((tok, 2 * head_dim), F32)]
        + joined,
        scratch_shapes=[pltpu.VMEM((span, head_dim), F32)] * 2 + [pltpu.SemaphoreType.DMA((2,))] * len(joined),
        input_output_aliases={4 + 2 * BAND_BLOCKS: 0} if last else {},
        compiler_params=params(),
        cost_estimate=cost(tok, tok),
        name="attention_grad",
    )(queries, dout, attn, probs, *bands, *bands, *given)


def pick_kernel(slots, here, there, gout, first, second, dgate):
    step = pl.program_id(0)
    rows, width = gout.shape
    room = here.shape[0]
    column = lax.broadcasted_iota(jnp.int32, (rows, room), 1)
    grad = gout[...].astype(F32)
    sums = []
    for i, out in enumerate((first, second)):
        near = (slots[:, i : i + 1] == column).astype(BF16)
        far = (slots[:, i : i + 1] == column + room).astype(BF16)
        row = dot_nn(near, here[...]) + dot_nn(far, there[...])
        out[...] = row.astype(BF16)
        sums.append(jnp.sum(grad * row, axis=-1, keepdims=True))
    lane = lax.broadcasted_iota(jnp.int32, dgate.shape, 1)
    total = jnp.where(lane == 0, sums[0], jnp.where(lane == 1, sums[1], 0.0))

    @pl.when(step == 0)
    def _():
        dgate[...] = total

    @pl.when(step > 0)
    def _():
        dgate[...] += total


def pick(slots, here, there, grad_out):
    rows, width = grad_out.shape
    room = here.shape[0]
    size = width // CHUNKS
    by_column = lambda n: pl.BlockSpec((n, size), lambda i: (0, i))
    return pl.pallas_call(
        pick_kernel,
        grid=(CHUNKS,),
        in_specs=[pl.BlockSpec((rows, 2), lambda i: (0, 0)), by_column(room), by_column(room), by_column(rows)],
        out_specs=[by_column(rows), by_column(rows), pl.BlockSpec((rows, 128), lambda i: (0, 0))],
        out_shape=[jax.ShapeDtypeStruct((rows, width), BF16)] * 2 + [jax.ShapeDtypeStruct((rows, 128), F32)],
        compiler_params=params(),
        cost_estimate=cost(8 * rows * room * width, 8 * rows * width + 4 * room * width),
        name="pick",
    )(slots, here, there, grad_out)


def middle_kernel(experts, routes, own, recv, stream, first, second, gout, dgate, router, router_t, mixed, grad, gates):
    resid = stream[...].astype(F32) + (own[...] + recv[...])
    inverse = lax.rsqrt(jnp.mean(resid * resid, axis=-1, keepdims=True) + 1e-05)
    normed = (resid * inverse).astype(BF16)
    logits = dot_nn(normed, router[...])
    lane = lax.broadcasted_iota(jnp.int32, logits.shape, 1)
    is_first, is_second = lane == routes[:, 0:1], lane == routes[:, 1:2]
    chosen_first = jnp.sum(jnp.where(is_first, logits, 0.0), axis=-1, keepdims=True)
    chosen_second = jnp.sum(jnp.where(is_second, logits, 0.0), axis=-1, keepdims=True)
    gate_first = 1.0 / (1.0 + jnp.exp(chosen_second - chosen_first))
    gate_second = 1.0 - gate_first
    mixed[...] = (
        resid + gate_first * first[...].astype(F32) + gate_second * second[...].astype(F32)
    ).astype(BF16)
    d_first, d_second = dgate[:, 0:1], dgate[:, 1:2]
    common = gate_first * d_first + gate_second * d_second
    expert = lane % experts
    dlogit = jnp.where(expert == routes[:, 0:1], gate_first * (d_first - common), 0.0)
    dlogit = dlogit + jnp.where(expert == routes[:, 1:2], gate_second * (d_second - common), 0.0)
    high = dlogit.astype(BF16)
    rest = dlogit - high.astype(F32)
    middle = rest.astype(BF16)
    low = (rest - middle.astype(F32)).astype(BF16)
    part = lane // experts
    parts = jnp.where(part == 0, high.astype(F32), jnp.where(part == 1, middle.astype(F32), low.astype(F32)))
    dnormed = dot_nn(parts.astype(BF16), router_t[...])
    mean = jnp.mean(dnormed * resid, axis=-1, keepdims=True)
    grad[...] = (
        gout[...].astype(F32) + inverse * dnormed - resid * (inverse * inverse * inverse * mean)
    ).astype(BF16)
    gates[...] = jnp.where(lane == 0, gate_first, jnp.where(lane == 1, gate_second, 0.0))


MIDDLE_ROWS = 64


def middle(routes, own, recv, stream, first, second, grad_out, dgate, router, router_t, experts):
    rows, width = stream.shape
    size = MIDDLE_ROWS if rows % MIDDLE_ROWS == 0 else rows
    by_row = lambda n: pl.BlockSpec((size, n), lambda i: (i, 0))
    whole = lambda a: pl.BlockSpec(a.shape, lambda i: (0, 0))
    return pl.pallas_call(
        functools.partial(middle_kernel, experts),
        grid=(rows // size,),
        in_specs=[by_row(2)] + [by_row(width)] * 6 + [by_row(128), whole(router), whole(router_t)],
        out_specs=[by_row(width), by_row(width), by_row(128)],
        out_shape=[jax.ShapeDtypeStruct((rows, width), BF16)] * 2 + [jax.ShapeDtypeStruct((rows, 128), F32)],
        compiler_params=params(),
        cost_estimate=cost(2 * rows * 128 * width * 4, 20 * rows * width),
        name="middle",
    )(routes, own, recv, stream, first, second, grad_out, dgate, router, router_t)


def spread_kernel(slots, gates, gout, here, there):
    room = here.shape[0]
    rows = gout.shape[0]
    place = lax.broadcasted_iota(jnp.int32, (room, rows), 0)
    grad = gout[...].astype(F32)
    near, far = 0.0, 0.0
    for i in range(2):
        part = (gates[:, i : i + 1] * grad).astype(BF16)
        near = near + dot_nn((slots[i : i + 1, :] == place).astype(BF16), part)
        far = far + dot_nn((slots[i : i + 1, :] == place + room).astype(BF16), part)
    here[...] = near.astype(BF16)
    there[...] = far.astype(BF16)


def spread(slots_t, gates, grad_out, room):
    rows, width = grad_out.shape
    size = width // CHUNKS
    by_column = lambda n: pl.BlockSpec((n, size), lambda i: (0, i))
    return pl.pallas_call(
        spread_kernel,
        grid=(CHUNKS,),
        in_specs=[
            pl.BlockSpec((2, rows), lambda i: (0, 0)),
            pl.BlockSpec((rows, 128), lambda i: (0, 0)),
            by_column(rows),
        ],
        out_specs=[by_column(room)] * 2,
        out_shape=[jax.ShapeDtypeStruct((room, width), BF16)] * 2,
        compiler_params=params(),
        cost_estimate=cost(8 * rows * room * width, 2 * rows * width + 4 * room * width),
        name="spread",
    )(slots_t, gates, grad_out)


def local(
    queries_in, rotated_keys, value_inputs, stream_in, w_out, w_router, routes, expert_out, grad_out
):
    place = lax.axis_index("ctx")
    core = lax.axis_index("exp")
    tok, heads_q, head_dim = queries_in.shape
    heads_kv = rotated_keys.shape[1]
    rows, width = stream_in.shape
    experts = w_router.shape[1]
    held, capacity = expert_out.shape[1], expert_out.shape[3]
    room = held * capacity
    scale = head_dim ** (-0.5)
    core_arg = core.astype(jnp.int32).reshape(1)
    place_arg = place.astype(jnp.int32).reshape(1)

    own_band = jnp.concatenate(
        [rotated_keys.reshape(tok, heads_kv * head_dim), value_inputs.reshape(tok, heads_kv * head_dim)], axis=1
    )
    queries = jnp.transpose(queries_in, (1, 0, 2))
    flat = routes.reshape(-1)
    number = jnp.arange(2 * rows, dtype=jnp.int32)
    earlier = (flat[None, :] == flat[:, None]) & (number[None, :] < number[:, None])
    rank = jnp.sum(earlier.astype(jnp.int32), axis=1)
    slots = (flat * capacity + rank - core * room) % (experts * capacity)
    slots = slots.reshape(rows, 2)
    router = jnp.pad(w_router, ((0, 0), (0, 128 - experts)))
    router_t = jnp.pad(jnp.concatenate([w_router.T] * 3, axis=0), ((0, 128 - 3 * experts), (0, 0)))
    made = {}

    def prepare(*ready):
        return [slots, own_band, router, router_t]

    def swap_rows(*ready):
        rows_out = after([expert_out[0]], *ready)[0]
        sent = lax.dynamic_index_in_dim(rows_out, 1 - core, 1, keepdims=False).reshape(room, width)
        kept = lax.dynamic_index_in_dim(rows_out, core, 1, keepdims=False).reshape(room, width)
        made["rows"] = kept, swapped(sent, "exp")
        return made["rows"]

    def pick_rows(*ready):
        kept, arrived = after(made["rows"], *ready)
        made["picked"] = pick(slots, kept, arrived, grad_out)
        return [made["picked"][2]]

    def attend(*ready):
        band = after([own_band], *ready)[0]
        bands = [band] + [passed_along(band, "ctx", step) for step in range(1, BAND_BLOCKS)]
        made["bands"] = bands[::-1]
        made["attention"] = attention(
            queries, made["bands"], place_arg, heads_q, heads_kv, head_dim, scale
        )

    arrays, table, plan = gathered(w_out, prepare, swap_rows, pick_rows, attend)
    first, second, dgate = made["picked"]
    attn, probs = made["attention"]
    bands = made["bands"]

    own, other = project([attn], arrays, table, plan, core_arg, heads_q, head_dim, width, rows)
    mixed, grad_input, gates = middle(
        routes, own, swapped(other, "exp"), stream_in, first, second, grad_out, dgate, router, router_t, experts
    )
    grad_other = swapped(grad_input, "exp")
    here, there = spread(slots.T, gates, grad_out, room)
    dattn = dattention(grad_input, grad_other, arrays, table, plan, core_arg, heads_q, head_dim, width)
    there = after([there], dattn)[0]
    back = swapped(there, "exp").reshape(held, capacity, width)
    here = here.reshape(held, capacity, width)
    grads, totals, given = [], [], ()
    for i in range(heads_kv):
        if i == heads_kv - 1:
            given = (grads[-1][0], core_arg, here, back)
        grad = attention_grad(queries, dattn, attn, probs, bands, i, given, heads_kv, scale)
        totals.append([passed_along(grad[BAND_BLOCKS - step], "ctx", -step) for step in range(1, BAND_BLOCKS)])
        grads.append(grad)
    grad_q = jnp.transpose(grads[-1][0], (1, 0, 2))
    grad_expert = grads[-1][1 + BAND_BLOCKS]
    totals = lax.optimization_barrier(totals)
    sums = []
    for grad, passed in zip(grads, totals):
        total = grad[BAND_BLOCKS]
        for part in passed:
            total = total + part.astype(F32)
        sums.append(total.astype(BF16))
    grad_k = jnp.stack([t[:, :head_dim] for t in sums], axis=1)
    grad_v = jnp.stack([t[:, head_dim:] for t in sums], axis=1)
    return (mixed, grad_input, grad_expert, grad_q, grad_k, grad_v)


def solution(mesh):
    in_specs = (
        P(("groups", "ctx"), "exp", None),
        P(("groups", "ctx"), "exp", None),
        P(("groups", "ctx"), "exp", None),
        P(("groups", "ctx", "exp"), None),
        P("exp", "ctx", None),
        P(),
        P(("groups", "ctx", "exp"), None),
        P(("groups", "ctx"), "exp", None, None, None),
        P(("groups", "ctx", "exp"), None),
    )
    out_specs = (
        P(("groups", "ctx", "exp"), None),
        P(("groups", "ctx", "exp"), None),
        P(("groups", "ctx"), "exp", None, None, None),
        P(("groups", "ctx"), "exp", None),
        P(("groups", "ctx"), "exp", None),
        P(("groups", "ctx"), "exp", None),
    )
    return jax.shard_map(local, mesh=mesh, in_specs=in_specs, out_specs=out_specs, check_vma=False)
```

```python
import functools

import jax
import jax.numpy as jnp
from jax import lax
from jax.experimental import pallas as pl
from jax.experimental.pallas import tpu as pltpu
from jax.sharding import PartitionSpec as P

BAND_BLOCKS = 4
F32 = jnp.float32
BF16 = jnp.bfloat16
VMEM_LIMIT = 56 * 1024 * 1024


def params(limit=VMEM_LIMIT):
    return pltpu.CompilerParams(vmem_limit_bytes=limit)


def cost(flops, nbytes, exps=0):
    return pl.CostEstimate(flops=flops, bytes_accessed=nbytes, transcendentals=exps)


def dot_nn(a, b):
    return lax.dot_general(a, b, (((1,), (0,)), ((), ())), preferred_element_type=F32)


def dot_nt(a, b):
    return lax.dot_general(a, b, (((1,), (1,)), ((), ())), preferred_element_type=F32)


def dot_tn(a, b):
    return lax.dot_general(a, b, (((0,), (0,)), ((), ())), preferred_element_type=F32)


def passed_along(value, axis, steps):
    count = lax.axis_size(axis)
    initial, last = (max(0, -steps), min(count, count - steps))
    return lax.ppermute(value, axis, [(source, source + steps) for source in range(initial, last)])


def swapped(value, axis):
    return lax.ppermute(value, axis, [(0, 1), (1, 0)])


def after(values, *others):
    return lax.optimization_barrier((tuple(values), others))[0]


def gathered(w_out, *tasks):
    heads, depth, _ = w_out.shape
    count = lax.axis_size("ctx")
    place = lax.axis_index("ctx")
    if count != 8 or lax.axis_size("groups") != 2 or heads % 2:
        full = lax.all_gather(w_out, "ctx", axis=1, tiled=True)
        for task in tasks:
            task()
        return [full], jnp.zeros((1,), jnp.int32), [(0, heads, 0, 0)]
    side = lax.axis_index("groups")
    half = heads // 2
    ring = lambda value: lax.ppermute(value, "ctx", [(c, (c + 2) % count) for c in range(count)])
    pair = lambda value: lax.ppermute(value, "ctx", [(c, c ^ 1) for c in range(count)])
    cross = lambda value: swapped(value, "groups")
    mine = lax.dynamic_slice_in_dim(w_out, side * half, half, 0)

    z1, y0 = ring(mine), pair(mine)
    (z1,) = after([z1], *tasks[0]())
    z2, y1, x1 = ring(z1), pair(z1), cross(z1)
    z2, y0 = after([z2, y0], *tasks[1](z1))
    z3, y2, x2 = ring(z2), pair(z2), cross(y0)
    z3, x1 = after([z3, x1], y1, *tasks[2](z2))
    z4, y3, x3 = ring(x1), pair(z3), cross(z3)
    y2, z4 = after([y2, z4], x2, y2)
    x4 = cross(y2)
    y3, last = after([y3, x1], x3, z4)
    y4, x5 = pair(last), cross(y3)
    tasks[3](z4, x3)

    table = [0, side * half, (1 - side) * half]
    table += [depth * ((place - 2 * k) % count) for k in range(4)]
    table += [depth * (((place - 2 * k) % count) ^ 1) for k in range(4)]
    arrays = [w_out, z1, z2, z3, y0, y1, y2, y3, x1, z4, x3, x2, y4, x4, x5]
    plan = [(0, heads, 0, 3)]
    plan += [(1 + k, half, 1, 4 + k) for k in range(7)]
    plan += [(8 + k, half, 2, 4 + k) for k in range(7)]
    return arrays, jnp.stack([jnp.asarray(t, jnp.int32) for t in table]), plan


def piece_copies(plan, table, pieces, buf, sem, chunk, chunk_size):
    copies = []
    columns = pl.ds(pl.multiple_of(chunk * chunk_size, chunk_size), chunk_size)
    depth_of = [p.shape[1] for p in pieces]
    for number, (array, size, head, row) in enumerate(plan):
        rows = pl.ds(pl.multiple_of(table[row], depth_of[array]), depth_of[array])
        copies.append(
            pltpu.make_async_copy(
                pieces[array].at[:, :, columns],
                buf.at[pl.ds(table[head], size), rows, columns],
                sem.at[number, chunk],
            )
        )
    return copies


CHUNKS = 3


def wait_chunk(plan, table, pieces, buf, sem, width):
    step = pl.program_id(0)
    size = width // CHUNKS

    @pl.when(step == 0)
    def _():
        for chunk in range(CHUNKS):
            for copy in piece_copies(plan, table, pieces, buf, sem, chunk, size):
                copy.start()

    for copy in piece_copies(plan, table, pieces, buf, sem, step, size):
        copy.wait()
    return pl.ds(pl.multiple_of(step * size, size), size)


def project_kernel(plan, count, parts, table, core, *refs):
    attn = jnp.concatenate([r[...] for r in refs[:parts]], axis=1)
    refs = refs[parts:]
    pieces, (own, other, buf, sem) = refs[:count], refs[count:]
    heads, head_dim, width = buf.shape
    columns = wait_chunk(plan, table, pieces, buf, sem, width)
    weights = buf[:, :, columns].reshape(heads * head_dim, width // CHUNKS)
    result = dot_nn(attn, weights)
    rows = own.shape[0]

    @pl.when(core[0] == 0)
    def _():
        own[...] = result[:rows]
        other[...] = result[rows:]

    @pl.when(core[0] != 0)
    def _():
        own[...] = result[rows:]
        other[...] = result[:rows]


def project(attn, arrays, table, plan, core, heads, head_dim, width, rows):
    tok = attn[0].shape[0]
    size = width // CHUNKS
    return pl.pallas_call(
        functools.partial(project_kernel, plan, len(arrays), len(attn)),
        grid_spec=pltpu.PrefetchScalarGridSpec(
            num_scalar_prefetch=2,
            grid=(CHUNKS,),
            in_specs=[pl.BlockSpec(a.shape, lambda i, *_: (0, 0)) for a in attn]
            + [pl.BlockSpec(memory_space=pl.ANY)] * len(arrays),
            out_specs=[pl.BlockSpec((rows, size), lambda i, *_: (0, i))] * 2,
            scratch_shapes=[
                pltpu.VMEM((heads, head_dim, width), BF16),
                pltpu.SemaphoreType.DMA((len(plan), CHUNKS)),
            ],
        ),
        out_shape=[jax.ShapeDtypeStruct((rows, width), F32)] * 2,
        compiler_params=params(),
        cost_estimate=cost(2 * tok * heads * head_dim * width, 2 * heads * head_dim * width),
        name="project",
    )(table, core, *attn, *arrays)


def dattn_kernel(plan, count, table, core, own, recv, *refs):
    pieces, (out, grad, acc, buf, sem) = refs[:count], refs[count:]
    heads, head_dim, width = buf.shape
    rows = own.shape[0]
    step = pl.program_id(0)

    @pl.when(core[0] == 0)
    def _():
        grad[:rows] = own[...]
        grad[rows:] = recv[...]

    @pl.when(core[0] != 0)
    def _():
        grad[rows:] = own[...]
        grad[:rows] = recv[...]

    columns = wait_chunk(plan, table, pieces, buf, sem, width)
    weights = buf[:, :, columns].reshape(heads * head_dim, width // CHUNKS)
    part = dot_nt(grad[...], weights)

    @pl.when(step == 0)
    def _():
        acc[...] = part

    @pl.when(step > 0)
    def _():
        acc[...] += part

    @pl.when(step == CHUNKS - 1)
    def _():
        out[...] = acc[...].astype(BF16)


def dattention(own, recv, arrays, table, plan, core, heads, head_dim, width):
    rows = own.shape[0]
    size = width // CHUNKS
    return pl.pallas_call(
        functools.partial(dattn_kernel, plan, len(arrays)),
        grid_spec=pltpu.PrefetchScalarGridSpec(
            num_scalar_prefetch=2,
            grid=(CHUNKS,),
            in_specs=[pl.BlockSpec((rows, size), lambda i, *_: (0, i))] * 2
            + [pl.BlockSpec(memory_space=pl.ANY)] * len(arrays),
            out_specs=pl.BlockSpec((2 * rows, heads * head_dim), lambda i, *_: (0, 0)),
            scratch_shapes=[
                pltpu.VMEM((2 * rows, size), BF16),
                pltpu.VMEM((2 * rows, heads * head_dim), F32),
                pltpu.VMEM((heads, head_dim, width), BF16),
                pltpu.SemaphoreType.DMA((len(plan), CHUNKS)),
            ],
        ),
        out_shape=jax.ShapeDtypeStruct((2 * rows, heads * head_dim), BF16),
        compiler_params=params(),
        cost_estimate=cost(4 * rows * heads * head_dim * width, 2 * heads * head_dim * width),
        name="dattention",
    )(table, core, own, recv, *arrays)


def band_of(refs):
    return jnp.concatenate([r[...] for r in refs], axis=0)


HEADS_FORWARD = 6
HEADS_BACKWARD = 6


def heads_a_step(most, group):
    return max(n for n in range(1, most + 1) if group % n == 0)


def stacked(ref, count):
    size = ref.shape[1] // count
    return jnp.concatenate([ref[:, i * size : (i + 1) * size] for i in range(count)], axis=0)


def attention_kernel(scale, place, q, *refs):
    keys, values, (attn, probs) = refs[:BAND_BLOCKS], refs[BAND_BLOCKS : 2 * BAND_BLOCKS], refs[-2:]
    count, tok, head_dim = q.shape
    scores = dot_nt(q[...].reshape(count * tok, head_dim), band_of(keys)) * scale
    scores = scores.reshape(count, tok, BAND_BLOCKS * tok)
    row = lax.broadcasted_iota(jnp.int32, scores.shape, 1)
    column = lax.broadcasted_iota(jnp.int32, scores.shape, 2)
    offset = column - (BAND_BLOCKS - 1) * tok
    admitted = (offset <= row) & (offset + place[0] * tok >= 0)
    scores = jnp.where(admitted, scores, -1e30)
    top = jnp.max(scores, axis=-1, keepdims=True)
    grown = jnp.exp(scores - top)
    weight = (grown * (1.0 / jnp.sum(grown, axis=-1, keepdims=True))).astype(BF16)
    probs[...] = weight
    result = dot_nn(weight.reshape(count * tok, BAND_BLOCKS * tok), band_of(values)).astype(BF16)
    for i in range(count):
        attn[:, i * head_dim : (i + 1) * head_dim] = result[i * tok : (i + 1) * tok]


def attention(queries, bands, place, heads, heads_kv, head_dim, scale):
    tok = queries.shape[1]
    group = heads // heads_kv
    count = heads_a_step(HEADS_FORWARD, group)
    keys = pl.BlockSpec((tok, head_dim), lambda h, *_: (0, h * count // group))
    values = pl.BlockSpec((tok, head_dim), lambda h, *_: (0, heads_kv + h * count // group))
    span = BAND_BLOCKS * tok
    return pl.pallas_call(
        functools.partial(attention_kernel, scale),
        grid_spec=pltpu.PrefetchScalarGridSpec(
            num_scalar_prefetch=1,
            grid=(heads // count,),
            in_specs=[pl.BlockSpec((count, tok, head_dim), lambda h, *_: (h, 0, 0))]
            + [keys] * BAND_BLOCKS
            + [values] * BAND_BLOCKS,
            out_specs=[
                pl.BlockSpec((tok, count * head_dim), lambda h, *_: (0, h)),
                pl.BlockSpec((count, tok, span), lambda h, *_: (h, 0, 0)),
            ],
        ),
        out_shape=[
            jax.ShapeDtypeStruct((tok, heads * head_dim), BF16),
            jax.ShapeDtypeStruct((heads, tok, span), BF16),
        ],
        compiler_params=params(),
        cost_estimate=cost(4 * tok * span * heads * head_dim, 2 * heads * tok * span, heads * tok * span),
        name="attention",
    )(place, queries, *bands, *bands)


def attention_grad_kernel(scale, steps, last, q, dout, attn, probs, *refs):
    refs = list(refs)
    keys, values = refs[:BAND_BLOCKS], refs[BAND_BLOCKS : 2 * BAND_BLOCKS]
    refs = refs[2 * BAND_BLOCKS :]
    if last:
        (_, core, here, back), refs, (held, sem) = refs[:4], refs[4:-2], refs[-2:]
        joined = refs.pop(1 + BAND_BLOCKS)
        places = core[0], 1 - core[0]
        inward = [pltpu.make_async_copy(r, held.at[i], sem.at[0, i]) for i, r in enumerate((here, back))]
        outward = [
            pltpu.make_async_copy(held.at[i], joined.at[0, :, at], sem.at[1, i]) for i, at in enumerate(places)
        ]

        @pl.when(pl.program_id(0) == 0)
        def _():
            for copy in inward:
                copy.start()

    dq, outs, (dk, dv) = refs[0], refs[1:-2], refs[-2:]
    count, tok, head_dim = q.shape
    step = pl.program_id(0)
    grad = stacked(dout, count)
    weight = probs[...].reshape(count * tok, BAND_BLOCKS * tok)
    delta = jnp.sum(grad.astype(F32) * stacked(attn, count).astype(F32), axis=-1, keepdims=True)
    dprob = dot_nt(grad, band_of(values))
    dscore = (weight.astype(F32) * (dprob - delta)).astype(BF16)
    dq[...] = (dot_nn(dscore, band_of(keys)) * scale).astype(BF16).reshape(count, tok, head_dim)
    if last:

        @pl.when(step == 0)
        def _():
            for copy in inward:
                copy.wait()
            for copy in outward:
                copy.start()

    dkey = dot_tn(dscore, q[...].reshape(count * tok, head_dim))
    dvalue = dot_tn(weight, grad)

    @pl.when(step == 0)
    def _():
        dk[...] = dkey
        dv[...] = dvalue

    @pl.when(step > 0)
    def _():
        dk[...] += dkey
        dv[...] += dvalue

    @pl.when(step == steps - 1)
    def _():
        for block, out in enumerate(outs):
            rows = pl.ds(block * tok, tok)
            out[:, :head_dim] = (dk[rows, :] * scale).astype(out.dtype)
            out[:, head_dim:] = dv[rows, :].astype(out.dtype)
        if last:
            for copy in outward:
                copy.wait()


def attention_grad(queries, dout, attn, probs, bands, which, given, heads_kv, scale):
    heads, tok, head_dim = queries.shape
    group = heads // heads_kv
    count = heads_a_step(HEADS_BACKWARD, group)
    steps = group // count
    keys = pl.BlockSpec((tok, head_dim), lambda h: (0, which))
    values = pl.BlockSpec((tok, head_dim), lambda h: (0, heads_kv + which))
    by_head = pl.BlockSpec((count, tok, head_dim), lambda h: (which * steps + h, 0, 0))
    of_all = pl.BlockSpec((tok, count * head_dim), lambda h: (0, which * steps + h))
    span = BAND_BLOCKS * tok
    whole = pl.BlockSpec((tok, 2 * head_dim), lambda h: (0, 0))
    anywhere = pl.BlockSpec(memory_space=pl.ANY)
    last = bool(given)
    joined, extra = [], []
    if last:
        held, capacity, width = given[2].shape
        joined = [jax.ShapeDtypeStruct((1, held, 2, capacity, width), BF16)]
        extra = [pltpu.VMEM((2, held, capacity, width), BF16), pltpu.SemaphoreType.DMA((2, 2))]
    return pl.pallas_call(
        functools.partial(attention_grad_kernel, scale, steps, last),
        grid=(steps,),
        in_specs=[by_head, of_all, of_all]
        + [pl.BlockSpec((count, tok, span), lambda h: (which * steps + h, 0, 0))]
        + [keys] * BAND_BLOCKS
        + [values] * BAND_BLOCKS
        + ([anywhere, pl.BlockSpec(memory_space=pltpu.SMEM), anywhere, anywhere] if last else []),
        out_specs=[by_head] + [whole] * BAND_BLOCKS + [anywhere] * len(joined),
        out_shape=[jax.ShapeDtypeStruct((heads, tok, head_dim), BF16)]
        + [jax.ShapeDtypeStruct((tok, 2 * head_dim), BF16)] * (BAND_BLOCKS - 1)
        + [jax.ShapeDtypeStruct((tok, 2 * head_dim), F32)]
        + joined,
        scratch_shapes=[pltpu.VMEM((span, head_dim), F32)] * 2 + extra,
        input_output_aliases={4 + 2 * BAND_BLOCKS: 0} if last else {},
        compiler_params=params(),
        cost_estimate=cost(tok, tok),
        name="attention_grad",
    )(queries, dout, attn, probs, *bands, *bands, *given)


def pick_kernel(slots, here, there, gout, first, second, dgate):
    step = pl.program_id(0)
    rows, width = gout.shape
    room = here.shape[0]
    column = lax.broadcasted_iota(jnp.int32, (rows, room), 1)
    grad = gout[...].astype(F32)
    sums = []
    for i, out in enumerate((first, second)):
        near = (slots[:, i : i + 1] == column).astype(BF16)
        far = (slots[:, i : i + 1] == column + room).astype(BF16)
        row = dot_nn(near, here[...]) + dot_nn(far, there[...])
        out[...] = row.astype(BF16)
        sums.append(jnp.sum(grad * row, axis=-1, keepdims=True))
    lane = lax.broadcasted_iota(jnp.int32, dgate.shape, 1)
    total = jnp.where(lane == 0, sums[0], jnp.where(lane == 1, sums[1], 0.0))

    @pl.when(step == 0)
    def _():
        dgate[...] = total

    @pl.when(step > 0)
    def _():
        dgate[...] += total


def pick(slots, here, there, grad_out):
    rows, width = grad_out.shape
    room = here.shape[0]
    size = width // CHUNKS
    by_column = lambda n: pl.BlockSpec((n, size), lambda i: (0, i))
    return pl.pallas_call(
        pick_kernel,
        grid=(CHUNKS,),
        in_specs=[pl.BlockSpec((rows, 2), lambda i: (0, 0)), by_column(room), by_column(room), by_column(rows)],
        out_specs=[by_column(rows), by_column(rows), pl.BlockSpec((rows, 128), lambda i: (0, 0))],
        out_shape=[jax.ShapeDtypeStruct((rows, width), BF16)] * 2 + [jax.ShapeDtypeStruct((rows, 128), F32)],
        compiler_params=params(),
        cost_estimate=cost(8 * rows * room * width, 8 * rows * width + 4 * room * width),
        name="pick",
    )(slots, here, there, grad_out)


def middle_kernel(experts, routes, own, recv, stream, first, second, gout, dgate, router, router_t, mixed, grad, gates):
    resid = stream[...].astype(F32) + (own[...] + recv[...])
    inverse = lax.rsqrt(jnp.mean(resid * resid, axis=-1, keepdims=True) + 1e-05)
    normed = (resid * inverse).astype(BF16)
    logits = dot_nn(normed, router[...])
    lane = lax.broadcasted_iota(jnp.int32, logits.shape, 1)
    is_first, is_second = lane == routes[:, 0:1], lane == routes[:, 1:2]
    chosen_first = jnp.sum(jnp.where(is_first, logits, 0.0), axis=-1, keepdims=True)
    chosen_second = jnp.sum(jnp.where(is_second, logits, 0.0), axis=-1, keepdims=True)
    gate_first = 1.0 / (1.0 + jnp.exp(chosen_second - chosen_first))
    gate_second = 1.0 - gate_first
    mixed[...] = (
        resid + gate_first * first[...].astype(F32) + gate_second * second[...].astype(F32)
    ).astype(BF16)
    d_first, d_second = dgate[:, 0:1], dgate[:, 1:2]
    common = gate_first * d_first + gate_second * d_second
    expert = lane % experts
    dlogit = jnp.where(expert == routes[:, 0:1], gate_first * (d_first - common), 0.0)
    dlogit = dlogit + jnp.where(expert == routes[:, 1:2], gate_second * (d_second - common), 0.0)
    high = dlogit.astype(BF16)
    rest = dlogit - high.astype(F32)
    middle = rest.astype(BF16)
    low = (rest - middle.astype(F32)).astype(BF16)
    part = lane // experts
    parts = jnp.where(part == 0, high.astype(F32), jnp.where(part == 1, middle.astype(F32), low.astype(F32)))
    dnormed = dot_nn(parts.astype(BF16), router_t[...])
    mean = jnp.mean(dnormed * resid, axis=-1, keepdims=True)
    grad[...] = (
        gout[...].astype(F32) + inverse * dnormed - resid * (inverse * inverse * inverse * mean)
    ).astype(BF16)
    gates[...] = jnp.where(lane == 0, gate_first, jnp.where(lane == 1, gate_second, 0.0))


MIDDLE_ROWS = 64


def middle(routes, own, recv, stream, first, second, grad_out, dgate, router, router_t, experts):
    rows, width = stream.shape
    size = MIDDLE_ROWS if rows % MIDDLE_ROWS == 0 else rows
    by_row = lambda n: pl.BlockSpec((size, n), lambda i: (i, 0))
    whole = lambda a: pl.BlockSpec(a.shape, lambda i: (0, 0))
    return pl.pallas_call(
        functools.partial(middle_kernel, experts),
        grid=(rows // size,),
        in_specs=[by_row(2)] + [by_row(width)] * 6 + [by_row(128), whole(router), whole(router_t)],
        out_specs=[by_row(width), by_row(width), by_row(128)],
        out_shape=[jax.ShapeDtypeStruct((rows, width), BF16)] * 2 + [jax.ShapeDtypeStruct((rows, 128), F32)],
        compiler_params=params(),
        cost_estimate=cost(2 * rows * 128 * width * 4, 20 * rows * width),
        name="middle",
    )(routes, own, recv, stream, first, second, grad_out, dgate, router, router_t)


def spread_kernel(slots, gates, gout, here, there):
    room = here.shape[0]
    rows = gout.shape[0]
    place = lax.broadcasted_iota(jnp.int32, (room, rows), 0)
    grad = gout[...].astype(F32)
    near, far = 0.0, 0.0
    for i in range(2):
        part = (gates[:, i : i + 1] * grad).astype(BF16)
        near = near + dot_nn((slots[i : i + 1, :] == place).astype(BF16), part)
        far = far + dot_nn((slots[i : i + 1, :] == place + room).astype(BF16), part)
    here[...] = near.astype(BF16)
    there[...] = far.astype(BF16)


def spread(slots_t, gates, grad_out, room):
    rows, width = grad_out.shape
    size = width // CHUNKS
    by_column = lambda n: pl.BlockSpec((n, size), lambda i: (0, i))
    return pl.pallas_call(
        spread_kernel,
        grid=(CHUNKS,),
        in_specs=[
            pl.BlockSpec((2, rows), lambda i: (0, 0)),
            pl.BlockSpec((rows, 128), lambda i: (0, 0)),
            by_column(rows),
        ],
        out_specs=[by_column(room)] * 2,
        out_shape=[jax.ShapeDtypeStruct((room, width), BF16)] * 2,
        compiler_params=params(),
        cost_estimate=cost(8 * rows * room * width, 2 * rows * width + 4 * room * width),
        name="spread",
    )(slots_t, gates, grad_out)


def local(
    queries_in, rotated_keys, value_inputs, stream_in, w_out, w_router, routes, expert_out, grad_out
):
    place = lax.axis_index("ctx")
    core = lax.axis_index("exp")
    tok, heads_q, head_dim = queries_in.shape
    heads_kv = rotated_keys.shape[1]
    rows, width = stream_in.shape
    experts = w_router.shape[1]
    held, capacity = expert_out.shape[1], expert_out.shape[3]
    room = held * capacity
    scale = head_dim ** (-0.5)
    core_arg = core.astype(jnp.int32).reshape(1)
    place_arg = place.astype(jnp.int32).reshape(1)

    own_band = jnp.concatenate(
        [rotated_keys.reshape(tok, heads_kv * head_dim), value_inputs.reshape(tok, heads_kv * head_dim)], axis=1
    )
    queries = jnp.transpose(queries_in, (1, 0, 2))
    flat = routes.reshape(-1)
    number = jnp.arange(2 * rows, dtype=jnp.int32)
    earlier = (flat[None, :] == flat[:, None]) & (number[None, :] < number[:, None])
    rank = jnp.sum(earlier.astype(jnp.int32), axis=1)
    slots = (flat * capacity + rank - core * room) % (experts * capacity)
    slots = slots.reshape(rows, 2)
    router = jnp.pad(w_router, ((0, 0), (0, 128 - experts)))
    router_t = jnp.pad(jnp.concatenate([w_router.T] * 3, axis=0), ((0, 128 - 3 * experts), (0, 0)))
    made = {}

    def prepare(*ready):
        return [slots, own_band, router, router_t]

    def swap_rows(*ready):
        rows_out = after([expert_out[0]], *ready)[0]
        sent = lax.dynamic_index_in_dim(rows_out, 1 - core, 1, keepdims=False).reshape(room, width)
        kept = lax.dynamic_index_in_dim(rows_out, core, 1, keepdims=False).reshape(room, width)
        made["rows"] = kept, swapped(sent, "exp")
        return made["rows"]

    def pick_rows(*ready):
        kept, arrived = after(made["rows"], *ready)
        made["picked"] = pick(slots, kept, arrived, grad_out)
        return [made["picked"][2]]

    def attend(*ready):
        band = after([own_band], *ready)[0]
        bands = [band] + [passed_along(band, "ctx", step) for step in range(1, BAND_BLOCKS)]
        made["bands"] = bands[::-1]
        made["attention"] = attention(
            queries, made["bands"], place_arg, heads_q, heads_kv, head_dim, scale
        )

    arrays, table, plan = gathered(w_out, prepare, swap_rows, pick_rows, attend)
    first, second, dgate = made["picked"]
    attn, probs = made["attention"]
    bands = made["bands"]

    own, other = project([attn], arrays, table, plan, core_arg, heads_q, head_dim, width, rows)
    mixed, grad_input, gates = middle(
        routes, own, swapped(other, "exp"), stream_in, first, second, grad_out, dgate, router, router_t, experts
    )
    grad_other = swapped(grad_input, "exp")
    here, there = spread(slots.T, gates, grad_out, room)
    dattn = dattention(grad_input, grad_other, arrays, table, plan, core_arg, heads_q, head_dim, width)
    there = after([there], dattn)[0]
    back = swapped(there, "exp").reshape(held, capacity, width)
    here = here.reshape(held, capacity, width)
    grads, totals, given = [], [], ()
    for i in range(heads_kv):
        if i == heads_kv - 1:
            given = (grads[-1][0], core_arg, here, back)
        grad = attention_grad(queries, dattn, attn, probs, bands, i, given, heads_kv, scale)
        totals.append([passed_along(grad[BAND_BLOCKS - step], "ctx", -step) for step in range(1, BAND_BLOCKS)])
        grads.append(grad)
    grad_q = jnp.transpose(grads[-1][0], (1, 0, 2))
    grad_expert = grads[-1][1 + BAND_BLOCKS]
    totals = lax.optimization_barrier(totals)
    sums = []
    for grad, passed in zip(grads, totals):
        total = grad[BAND_BLOCKS]
        for part in passed:
            total = total + part.astype(F32)
        sums.append(total.astype(BF16))
    grad_k = jnp.stack([t[:, :head_dim] for t in sums], axis=1)
    grad_v = jnp.stack([t[:, head_dim:] for t in sums], axis=1)
    return (mixed, grad_input, grad_expert, grad_q, grad_k, grad_v)


def solution(mesh):
    in_specs = (
        P(("groups", "ctx"), "exp", None),
        P(("groups", "ctx"), "exp", None),
        P(("groups", "ctx"), "exp", None),
        P(("groups", "ctx", "exp"), None),
        P("exp", "ctx", None),
        P(),
        P(("groups", "ctx", "exp"), None),
        P(("groups", "ctx"), "exp", None, None, None),
        P(("groups", "ctx", "exp"), None),
    )
    out_specs = (
        P(("groups", "ctx", "exp"), None),
        P(("groups", "ctx", "exp"), None),
        P(("groups", "ctx"), "exp", None, None, None),
        P(("groups", "ctx"), "exp", None),
        P(("groups", "ctx"), "exp", None),
        P(("groups", "ctx"), "exp", None),
    )
    return jax.shard_map(local, mesh=mesh, in_specs=in_specs, out_specs=out_specs, check_vma=False)
```

```python
import functools

import jax
import jax.numpy as jnp
from jax import lax
from jax.experimental import pallas as pl
from jax.experimental.pallas import tpu as pltpu
from jax.sharding import PartitionSpec as P

BAND_BLOCKS = 4
F32 = jnp.float32
BF16 = jnp.bfloat16
VMEM_LIMIT = 56 * 1024 * 1024


def params(limit=VMEM_LIMIT):
    return pltpu.CompilerParams(vmem_limit_bytes=limit)


def cost(flops, nbytes, exps=0):
    return pl.CostEstimate(flops=flops, bytes_accessed=nbytes, transcendentals=exps)


def dot_nn(a, b):
    return lax.dot_general(a, b, (((1,), (0,)), ((), ())), preferred_element_type=F32)


def dot_nt(a, b):
    return lax.dot_general(a, b, (((1,), (1,)), ((), ())), preferred_element_type=F32)


def dot_tn(a, b):
    return lax.dot_general(a, b, (((0,), (0,)), ((), ())), preferred_element_type=F32)


def passed_along(value, axis, steps):
    count = lax.axis_size(axis)
    initial, last = (max(0, -steps), min(count, count - steps))
    return lax.ppermute(value, axis, [(source, source + steps) for source in range(initial, last)])


def swapped(value, axis):
    return lax.ppermute(value, axis, [(0, 1), (1, 0)])


def exchanged(one, three):
    count = lax.axis_size("ctx")
    pairs = [(c, c ^ 1) for c in range(count)]
    others = [(c, c - 1 if c % 2 else c - 3) for c in range(count) if c % 2 or c >= 4]
    return lax.ppermute(one, "ctx", pairs), lax.ppermute(three, "ctx", others)


def combined(two, by_one, by_three):
    even = lax.axis_index("ctx") % 2 == 0
    onward = (two.astype(F32) + jnp.where(even, by_three, by_one).astype(F32)).astype(BF16)
    return passed_along(onward, "ctx", -2), jnp.where(even, by_one, by_three)


def after(values, *others):
    return lax.optimization_barrier((tuple(values), others))[0]


def gathered(w_out, *tasks):
    heads, depth, _ = w_out.shape
    count = lax.axis_size("ctx")
    place = lax.axis_index("ctx")
    if count != 8 or lax.axis_size("groups") != 2 or heads % 2:
        full = lax.all_gather(w_out, "ctx", axis=1, tiled=True)
        for task in tasks:
            task()
        return [full], jnp.zeros((1,), jnp.int32), [(0, heads, 0, 0)]
    side = lax.axis_index("groups")
    half = heads // 2
    ring = lambda value: lax.ppermute(value, "ctx", [(c, (c + 2) % count) for c in range(count)])
    pair = lambda value: lax.ppermute(value, "ctx", [(c, c ^ 1) for c in range(count)])
    cross = lambda value: swapped(value, "groups")
    mine = lax.dynamic_slice_in_dim(w_out, side * half, half, 0)

    z1, y0 = ring(mine), pair(mine)
    z1, y0 = after([z1, y0], *tasks[0]())
    z2, y1, x1 = ring(z1), pair(z1), cross(z1)
    z2, y0 = after([z2, y0], *tasks[1](z1))
    z3, y2, x2 = ring(z2), pair(z2), cross(y0)
    z3, x1 = after([z3, x1], y1, *tasks[2](z2))
    z4, y3, x3 = ring(x1), pair(z3), cross(z3)
    y2, z4 = after([y2, z4], x2, y2)
    x4 = cross(y2)
    y3, last = after([y3, x1], x3, z4)
    y4, x5 = pair(last), cross(y3)
    tasks[3](z4, x3)

    table = [0, side * half, (1 - side) * half]
    table += [depth * ((place - 2 * k) % count) for k in range(4)]
    table += [depth * (((place - 2 * k) % count) ^ 1) for k in range(4)]
    arrays = [w_out, z1, z2, z3, y0, y1, y2, y3, x1, z4, x3, x2, y4, x4, x5]
    plan = [(0, heads, 0, 3)]
    plan += [(1 + k, half, 1, 4 + k) for k in range(7)]
    plan += [(8 + k, half, 2, 4 + k) for k in range(7)]
    return arrays, jnp.stack([jnp.asarray(t, jnp.int32) for t in table]), plan


def piece_copies(plan, table, pieces, buf, sem, chunk, chunk_size):
    copies = []
    columns = pl.ds(pl.multiple_of(chunk * chunk_size, chunk_size), chunk_size)
    depth_of = [p.shape[1] for p in pieces]
    for number, (array, size, head, row) in enumerate(plan):
        rows = pl.ds(pl.multiple_of(table[row], depth_of[array]), depth_of[array])
        copies.append(
            pltpu.make_async_copy(
                pieces[array].at[:, :, columns],
                buf.at[pl.ds(table[head], size), rows, columns],
                sem.at[number, chunk],
            )
        )
    return copies


CHUNKS = 3


def wait_chunk(plan, table, pieces, buf, sem, width):
    step = pl.program_id(0)
    size = width // CHUNKS

    @pl.when(step == 0)
    def _():
        for chunk in range(CHUNKS):
            for copy in piece_copies(plan, table, pieces, buf, sem, chunk, size):
                copy.start()

    for copy in piece_copies(plan, table, pieces, buf, sem, step, size):
        copy.wait()
    return pl.ds(pl.multiple_of(step * size, size), size)


def project_kernel(plan, count, parts, table, core, *refs):
    attn = jnp.concatenate([r[...] for r in refs[:parts]], axis=1)
    refs = refs[parts:]
    pieces, (own, other, buf, sem) = refs[:count], refs[count:]
    heads, head_dim, width = buf.shape
    columns = wait_chunk(plan, table, pieces, buf, sem, width)
    weights = buf[:, :, columns].reshape(heads * head_dim, width // CHUNKS)
    result = dot_nn(attn, weights)
    rows = own.shape[0]

    @pl.when(core[0] == 0)
    def _():
        own[...] = result[:rows]
        other[...] = result[rows:].astype(BF16)

    @pl.when(core[0] != 0)
    def _():
        own[...] = result[rows:]
        other[...] = result[:rows].astype(BF16)


def project(attn, arrays, table, plan, core, heads, head_dim, width, rows):
    tok = attn[0].shape[0]
    size = width // CHUNKS
    return pl.pallas_call(
        functools.partial(project_kernel, plan, len(arrays), len(attn)),
        grid_spec=pltpu.PrefetchScalarGridSpec(
            num_scalar_prefetch=2,
            grid=(CHUNKS,),
            in_specs=[pl.BlockSpec(a.shape, lambda i, *_: (0, 0)) for a in attn]
            + [pl.BlockSpec(memory_space=pl.ANY)] * len(arrays),
            out_specs=[pl.BlockSpec((rows, size), lambda i, *_: (0, i))] * 2,
            scratch_shapes=[
                pltpu.VMEM((heads, head_dim, width), BF16),
                pltpu.SemaphoreType.DMA((len(plan), CHUNKS)),
            ],
        ),
        out_shape=[jax.ShapeDtypeStruct((rows, width), F32), jax.ShapeDtypeStruct((rows, width), BF16)],
        compiler_params=params(),
        cost_estimate=cost(2 * tok * heads * head_dim * width, 2 * heads * head_dim * width),
        name="project",
    )(table, core, *attn, *arrays)


def dattn_kernel(plan, count, table, core, own, recv, *refs):
    pieces, (out, grad, acc, buf, sem) = refs[:count], refs[count:]
    heads, head_dim, width = buf.shape
    rows = own.shape[0]
    step = pl.program_id(0)

    @pl.when(core[0] == 0)
    def _():
        grad[:rows] = own[...]
        grad[rows:] = recv[...]

    @pl.when(core[0] != 0)
    def _():
        grad[rows:] = own[...]
        grad[:rows] = recv[...]

    columns = wait_chunk(plan, table, pieces, buf, sem, width)
    weights = buf[:, :, columns].reshape(heads * head_dim, width // CHUNKS)
    part = dot_nt(grad[...], weights)

    @pl.when(step == 0)
    def _():
        acc[...] = part

    @pl.when(step > 0)
    def _():
        acc[...] += part

    @pl.when(step == CHUNKS - 1)
    def _():
        out[...] = acc[...].astype(BF16)


def dattention(own, recv, arrays, table, plan, core, heads, head_dim, width):
    rows = own.shape[0]
    size = width // CHUNKS
    return pl.pallas_call(
        functools.partial(dattn_kernel, plan, len(arrays)),
        grid_spec=pltpu.PrefetchScalarGridSpec(
            num_scalar_prefetch=2,
            grid=(CHUNKS,),
            in_specs=[pl.BlockSpec((rows, size), lambda i, *_: (0, i))] * 2
            + [pl.BlockSpec(memory_space=pl.ANY)] * len(arrays),
            out_specs=pl.BlockSpec((2 * rows, heads * head_dim), lambda i, *_: (0, 0)),
            scratch_shapes=[
                pltpu.VMEM((2 * rows, size), BF16),
                pltpu.VMEM((2 * rows, heads * head_dim), F32),
                pltpu.VMEM((heads, head_dim, width), BF16),
                pltpu.SemaphoreType.DMA((len(plan), CHUNKS)),
            ],
        ),
        out_shape=jax.ShapeDtypeStruct((2 * rows, heads * head_dim), BF16),
        compiler_params=params(),
        cost_estimate=cost(4 * rows * heads * head_dim * width, 2 * heads * head_dim * width),
        name="dattention",
    )(table, core, own, recv, *arrays)


def band_of(refs):
    return jnp.concatenate([r[...] for r in refs], axis=0)


HEADS_FORWARD = 6
HEADS_BACKWARD = 6


def heads_a_step(most, group):
    return max(n for n in range(1, most + 1) if group % n == 0)


def stacked(ref, count):
    size = ref.shape[1] // count
    return jnp.concatenate([ref[:, i * size : (i + 1) * size] for i in range(count)], axis=0)


def attention_kernel(scale, place, q, *refs):
    keys, values, (attn, probs) = refs[:BAND_BLOCKS], refs[BAND_BLOCKS : 2 * BAND_BLOCKS], refs[-2:]
    count, tok, head_dim = q.shape
    scores = dot_nt(q[...].reshape(count * tok, head_dim), band_of(keys)) * scale
    scores = scores.reshape(count, tok, BAND_BLOCKS * tok)
    row = lax.broadcasted_iota(jnp.int32, scores.shape, 1)
    column = lax.broadcasted_iota(jnp.int32, scores.shape, 2)
    offset = column - (BAND_BLOCKS - 1) * tok
    admitted = (offset <= row) & (offset + place[0] * tok >= 0)
    scores = jnp.where(admitted, scores, -1e30)
    top = jnp.max(scores, axis=-1, keepdims=True)
    grown = jnp.exp(scores - top)
    weight = (grown * (1.0 / jnp.sum(grown, axis=-1, keepdims=True))).astype(BF16)
    probs[...] = weight
    result = dot_nn(weight.reshape(count * tok, BAND_BLOCKS * tok), band_of(values)).astype(BF16)
    for i in range(count):
        attn[:, i * head_dim : (i + 1) * head_dim] = result[i * tok : (i + 1) * tok]


def attention(queries, bands, place, heads, heads_kv, head_dim, scale):
    tok = queries.shape[1]
    group = heads // heads_kv
    count = heads_a_step(HEADS_FORWARD, group)
    keys = pl.BlockSpec((tok, head_dim), lambda h, *_: (0, h * count // group))
    values = pl.BlockSpec((tok, head_dim), lambda h, *_: (0, heads_kv + h * count // group))
    span = BAND_BLOCKS * tok
    return pl.pallas_call(
        functools.partial(attention_kernel, scale),
        grid_spec=pltpu.PrefetchScalarGridSpec(
            num_scalar_prefetch=1,
            grid=(heads // count,),
            in_specs=[pl.BlockSpec((count, tok, head_dim), lambda h, *_: (h, 0, 0))]
            + [keys] * BAND_BLOCKS
            + [values] * BAND_BLOCKS,
            out_specs=[
                pl.BlockSpec((tok, count * head_dim), lambda h, *_: (0, h)),
                pl.BlockSpec((count, tok, span), lambda h, *_: (h, 0, 0)),
            ],
        ),
        out_shape=[
            jax.ShapeDtypeStruct((tok, heads * head_dim), BF16),
            jax.ShapeDtypeStruct((heads, tok, span), BF16),
        ],
        compiler_params=params(),
        cost_estimate=cost(4 * tok * span * heads * head_dim, 2 * heads * tok * span, heads * tok * span),
        name="attention",
    )(place, queries, *bands, *bands)


def attention_grad_kernel(scale, steps, last, q, dout, attn, probs, *refs):
    refs = list(refs)
    keys, values = refs[:BAND_BLOCKS], refs[BAND_BLOCKS : 2 * BAND_BLOCKS]
    refs = refs[2 * BAND_BLOCKS :]
    if last:
        (_, core, here, back), refs, (held, sem) = refs[:4], refs[4:-2], refs[-2:]
        joined = refs.pop(1 + BAND_BLOCKS)
        places = core[0], 1 - core[0]
        inward = [pltpu.make_async_copy(r, held.at[i], sem.at[0, i]) for i, r in enumerate((here, back))]
        outward = [
            pltpu.make_async_copy(held.at[i], joined.at[0, :, at], sem.at[1, i]) for i, at in enumerate(places)
        ]

        @pl.when(pl.program_id(0) == 0)
        def _():
            for copy in inward:
                copy.start()

    dq, outs, (dk, dv) = refs[0], refs[1:-2], refs[-2:]
    count, tok, head_dim = q.shape
    step = pl.program_id(0)
    grad = stacked(dout, count)
    weight = probs[...].reshape(count * tok, BAND_BLOCKS * tok)
    delta = jnp.sum(grad.astype(F32) * stacked(attn, count).astype(F32), axis=-1, keepdims=True)
    dprob = dot_nt(grad, band_of(values))
    dscore = (weight.astype(F32) * (dprob - delta)).astype(BF16)
    dq[...] = (dot_nn(dscore, band_of(keys)) * scale).astype(BF16).reshape(count, tok, head_dim)
    if last:

        @pl.when(step == 0)
        def _():
            for copy in inward:
                copy.wait()
            for copy in outward:
                copy.start()

    dkey = dot_tn(dscore, q[...].reshape(count * tok, head_dim))
    dvalue = dot_tn(weight, grad)

    @pl.when(step == 0)
    def _():
        dk[...] = dkey
        dv[...] = dvalue

    @pl.when(step > 0)
    def _():
        dk[...] += dkey
        dv[...] += dvalue

    @pl.when(step == steps - 1)
    def _():
        for block, out in enumerate(outs):
            rows = pl.ds(block * tok, tok)
            out[:, :head_dim] = (dk[rows, :] * scale).astype(out.dtype)
            out[:, head_dim:] = dv[rows, :].astype(out.dtype)
        if last:
            for copy in outward:
                copy.wait()


def attention_grad(queries, dout, attn, probs, bands, which, given, heads_kv, scale):
    heads, tok, head_dim = queries.shape
    group = heads // heads_kv
    count = heads_a_step(HEADS_BACKWARD, group)
    steps = group // count
    keys = pl.BlockSpec((tok, head_dim), lambda h: (0, which))
    values = pl.BlockSpec((tok, head_dim), lambda h: (0, heads_kv + which))
    by_head = pl.BlockSpec((count, tok, head_dim), lambda h: (which * steps + h, 0, 0))
    of_all = pl.BlockSpec((tok, count * head_dim), lambda h: (0, which * steps + h))
    span = BAND_BLOCKS * tok
    whole = pl.BlockSpec((tok, 2 * head_dim), lambda h: (0, 0))
    anywhere = pl.BlockSpec(memory_space=pl.ANY)
    last = bool(given)
    joined, extra = [], []
    if last:
        held, capacity, width = given[2].shape
        joined = [jax.ShapeDtypeStruct((1, held, 2, capacity, width), BF16)]
        extra = [pltpu.VMEM((2, held, capacity, width), BF16), pltpu.SemaphoreType.DMA((2, 2))]
    return pl.pallas_call(
        functools.partial(attention_grad_kernel, scale, steps, last),
        grid=(steps,),
        in_specs=[by_head, of_all, of_all]
        + [pl.BlockSpec((count, tok, span), lambda h: (which * steps + h, 0, 0))]
        + [keys] * BAND_BLOCKS
        + [values] * BAND_BLOCKS
        + ([anywhere, pl.BlockSpec(memory_space=pltpu.SMEM), anywhere, anywhere] if last else []),
        out_specs=[by_head] + [whole] * BAND_BLOCKS + [anywhere] * len(joined),
        out_shape=[jax.ShapeDtypeStruct((heads, tok, head_dim), BF16)]
        + [jax.ShapeDtypeStruct((tok, 2 * head_dim), BF16)] * (BAND_BLOCKS - 1)
        + [jax.ShapeDtypeStruct((tok, 2 * head_dim), F32)]
        + joined,
        scratch_shapes=[pltpu.VMEM((span, head_dim), F32)] * 2 + extra,
        input_output_aliases={4 + 2 * BAND_BLOCKS: 0} if last else {},
        compiler_params=params(),
        cost_estimate=cost(tok, tok),
        name="attention_grad",
    )(queries, dout, attn, probs, *bands, *bands, *given)


def pick_kernel(core, slots, here_ref, there_ref, gout, first, second, dgate):
    step = pl.program_id(0)
    rows, width = gout.shape
    held, capacity, size = here_ref.shape
    room = held * capacity
    here, there = (r[...].reshape(room, size) for r in (here_ref, there_ref))
    column = lax.broadcasted_iota(jnp.int32, (rows, room), 1)
    grad = gout[...].astype(F32)
    sums = []
    for i, out in enumerate((first, second)):
        near = (slots[:, i : i + 1] == column).astype(BF16)
        far = (slots[:, i : i + 1] == column + room).astype(BF16)
        row = dot_nn(near, here) + dot_nn(far, there)
        out[...] = row.astype(BF16)
        sums.append(jnp.sum(grad * row, axis=-1, keepdims=True))
    lane = lax.broadcasted_iota(jnp.int32, dgate.shape, 1)
    total = jnp.where(lane == 0, sums[0], jnp.where(lane == 1, sums[1], 0.0))

    @pl.when(step == 0)
    def _():
        dgate[...] = total

    @pl.when(step > 0)
    def _():
        dgate[...] += total


def pick(core, slots, here, there, grad_out):
    rows, width = grad_out.shape
    held, capacity = here.shape[1], here.shape[3]
    room = held * capacity
    size = width // CHUNKS
    by_column = lambda n: pl.BlockSpec((n, size), lambda i, core: (0, i))
    table = pl.BlockSpec((None, held, None, capacity, size), lambda i, core: (0, 0, core[0], 0, i))
    whole = lambda n: pl.BlockSpec((rows, n), lambda i, core: (0, 0))
    return pl.pallas_call(
        pick_kernel,
        grid_spec=pltpu.PrefetchScalarGridSpec(
            num_scalar_prefetch=1,
            grid=(CHUNKS,),
            in_specs=[whole(2), table, table, by_column(rows)],
            out_specs=[by_column(rows), by_column(rows), whole(128)],
        ),
        out_shape=[jax.ShapeDtypeStruct((rows, width), BF16)] * 2 + [jax.ShapeDtypeStruct((rows, 128), F32)],
        compiler_params=params(),
        cost_estimate=cost(8 * rows * room * width, 8 * rows * width + 4 * room * width),
        name="pick",
    )(core, slots, here, there, grad_out)


def middle_kernel(experts, routes, own, recv, stream, first, second, gout, dgate, router, router_t, mixed, grad, gates):
    resid = stream[...].astype(F32) + (own[...] + recv[...].astype(F32))
    inverse = lax.rsqrt(jnp.mean(resid * resid, axis=-1, keepdims=True) + 1e-05)
    normed = (resid * inverse).astype(BF16)
    logits = dot_nn(normed, router[...])
    lane = lax.broadcasted_iota(jnp.int32, logits.shape, 1)
    is_first, is_second = lane == routes[:, 0:1], lane == routes[:, 1:2]
    chosen_first = jnp.sum(jnp.where(is_first, logits, 0.0), axis=-1, keepdims=True)
    chosen_second = jnp.sum(jnp.where(is_second, logits, 0.0), axis=-1, keepdims=True)
    gate_first = 1.0 / (1.0 + jnp.exp(chosen_second - chosen_first))
    gate_second = 1.0 - gate_first
    mixed[...] = (
        resid + gate_first * first[...].astype(F32) + gate_second * second[...].astype(F32)
    ).astype(BF16)
    d_first, d_second = dgate[:, 0:1], dgate[:, 1:2]
    common = gate_first * d_first + gate_second * d_second
    expert = lane % experts
    dlogit = jnp.where(expert == routes[:, 0:1], gate_first * (d_first - common), 0.0)
    dlogit = dlogit + jnp.where(expert == routes[:, 1:2], gate_second * (d_second - common), 0.0)
    high = dlogit.astype(BF16)
    rest = dlogit - high.astype(F32)
    middle = rest.astype(BF16)
    low = (rest - middle.astype(F32)).astype(BF16)
    part = lane // experts
    parts = jnp.where(part == 0, high.astype(F32), jnp.where(part == 1, middle.astype(F32), low.astype(F32)))
    dnormed = dot_nn(parts.astype(BF16), router_t[...])
    mean = jnp.mean(dnormed * resid, axis=-1, keepdims=True)
    grad[...] = (
        gout[...].astype(F32) + inverse * dnormed - resid * (inverse * inverse * inverse * mean)
    ).astype(BF16)
    gates[...] = jnp.where(lane == 0, gate_first, jnp.where(lane == 1, gate_second, 0.0))


MIDDLE_ROWS = 64


def middle(routes, own, recv, stream, first, second, grad_out, dgate, router, router_t, experts):
    rows, width = stream.shape
    size = MIDDLE_ROWS if rows % MIDDLE_ROWS == 0 else rows
    by_row = lambda n: pl.BlockSpec((size, n), lambda i: (i, 0))
    whole = lambda a: pl.BlockSpec(a.shape, lambda i: (0, 0))
    return pl.pallas_call(
        functools.partial(middle_kernel, experts),
        grid=(rows // size,),
        in_specs=[by_row(2)] + [by_row(width)] * 6 + [by_row(128), whole(router), whole(router_t)],
        out_specs=[by_row(width), by_row(width), by_row(128)],
        out_shape=[jax.ShapeDtypeStruct((rows, width), BF16)] * 2 + [jax.ShapeDtypeStruct((rows, 128), F32)],
        compiler_params=params(),
        cost_estimate=cost(2 * rows * 128 * width * 4, 20 * rows * width),
        name="middle",
    )(routes, own, recv, stream, first, second, grad_out, dgate, router, router_t)


def spread_kernel(slots, gates, gout, here, there):
    room = here.shape[0]
    rows = gout.shape[0]
    place = lax.broadcasted_iota(jnp.int32, (room, rows), 0)
    grad = gout[...].astype(F32)
    near, far = 0.0, 0.0
    for i in range(2):
        part = (gates[:, i : i + 1] * grad).astype(BF16)
        near = near + dot_nn((slots[i : i + 1, :] == place).astype(BF16), part)
        far = far + dot_nn((slots[i : i + 1, :] == place + room).astype(BF16), part)
    here[...] = near.astype(BF16)
    there[...] = far.astype(BF16)


def spread(slots_t, gates, grad_out, room):
    rows, width = grad_out.shape
    size = width // CHUNKS
    by_column = lambda n: pl.BlockSpec((n, size), lambda i: (0, i))
    return pl.pallas_call(
        spread_kernel,
        grid=(CHUNKS,),
        in_specs=[
            pl.BlockSpec((2, rows), lambda i: (0, 0)),
            pl.BlockSpec((rows, 128), lambda i: (0, 0)),
            by_column(rows),
        ],
        out_specs=[by_column(room)] * 2,
        out_shape=[jax.ShapeDtypeStruct((room, width), BF16)] * 2,
        compiler_params=params(),
        cost_estimate=cost(8 * rows * room * width, 2 * rows * width + 4 * room * width),
        name="spread",
    )(slots_t, gates, grad_out)


def local(
    queries_in, rotated_keys, value_inputs, stream_in, w_out, w_router, routes, expert_out, grad_out
):
    place = lax.axis_index("ctx")
    core = lax.axis_index("exp")
    tok, heads_q, head_dim = queries_in.shape
    heads_kv = rotated_keys.shape[1]
    rows, width = stream_in.shape
    experts = w_router.shape[1]
    held, capacity = expert_out.shape[1], expert_out.shape[3]
    room = held * capacity
    scale = head_dim ** (-0.5)
    core_arg = core.astype(jnp.int32).reshape(1)
    place_arg = place.astype(jnp.int32).reshape(1)

    own_band = jnp.concatenate(
        [rotated_keys.reshape(tok, heads_kv * head_dim), value_inputs.reshape(tok, heads_kv * head_dim)], axis=1
    )
    queries = jnp.transpose(queries_in, (1, 0, 2))
    flat = routes.reshape(-1)
    number = jnp.arange(2 * rows, dtype=jnp.int32)
    earlier = (flat[None, :] == flat[:, None]) & (number[None, :] < number[:, None])
    rank = jnp.sum(earlier.astype(jnp.int32), axis=1)
    slots = (flat * capacity + rank - core * room) % (experts * capacity)
    slots = slots.reshape(rows, 2)
    router = jnp.pad(w_router, ((0, 0), (0, 128 - experts)))
    router_t = jnp.pad(jnp.concatenate([w_router.T] * 3, axis=0), ((0, 128 - 3 * experts), (0, 0)))
    made = {}

    def prepare(*ready):
        return [slots, own_band, router, router_t]

    def swap_rows(*ready):
        rows_out = after([expert_out], *ready)[0]
        made["rows"] = swapped(rows_out, "exp")
        return [made["rows"]]

    def pick_rows(*ready):
        arrived = after([made["rows"]], *ready)[0]
        made["picked"] = pick(core_arg, slots, expert_out, arrived, grad_out)
        return [made["picked"][2]]

    def attend(*ready):
        band = after([own_band], *ready)[0]
        bands = [band] + [passed_along(band, "ctx", step) for step in range(1, BAND_BLOCKS)]
        made["bands"] = bands[::-1]
        made["attention"] = attention(
            queries, made["bands"], place_arg, heads_q, heads_kv, head_dim, scale
        )

    arrays, table, plan = gathered(w_out, prepare, swap_rows, pick_rows, attend)
    first, second, dgate = made["picked"]
    attn, probs = made["attention"]
    bands = made["bands"]

    own, other = project([attn], arrays, table, plan, core_arg, heads_q, head_dim, width, rows)
    mixed, grad_input, gates = middle(
        routes, own, swapped(other, "exp"), stream_in, first, second, grad_out, dgate, router, router_t, experts
    )
    grad_other = swapped(grad_input, "exp")
    here, there = spread(slots.T, gates, grad_out, room)
    dattn = dattention(grad_input, grad_other, arrays, table, plan, core_arg, heads_q, head_dim, width)
    there = after([there], dattn)[0]
    back = swapped(there, "exp").reshape(held, capacity, width)
    here = here.reshape(held, capacity, width)
    grads, totals, given = [], [], ()
    for i in range(heads_kv):
        if i == heads_kv - 1:
            given = (grads[-1][0], core_arg, here, back)
        grad = attention_grad(queries, dattn, attn, probs, bands, i, given, heads_kv, scale)
        if i > 0:
            totals[-1] = after(totals[-1], grad[0])
        totals.append(exchanged(grad[BAND_BLOCKS - 1], grad[BAND_BLOCKS - 3]))
        grads.append(grad)
    grad_q = jnp.transpose(grads[-1][0], (1, 0, 2))
    grad_expert = grads[-1][1 + BAND_BLOCKS]
    totals = [combined(grad[BAND_BLOCKS - 2], *pair) for grad, pair in zip(grads, totals)]
    sums = [
        (grad[BAND_BLOCKS] + (near.astype(F32) + far.astype(F32))).astype(BF16)
        for grad, (near, far) in zip(grads, totals)
    ]
    grad_k = jnp.stack([t[:, :head_dim] for t in sums], axis=1)
    grad_v = jnp.stack([t[:, head_dim:] for t in sums], axis=1)
    return (mixed, grad_input, grad_expert, grad_q, grad_k, grad_v)


def solution(mesh):
    in_specs = (
        P(("groups", "ctx"), "exp", None),
        P(("groups", "ctx"), "exp", None),
        P(("groups", "ctx"), "exp", None),
        P(("groups", "ctx", "exp"), None),
        P("exp", "ctx", None),
        P(),
        P(("groups", "ctx", "exp"), None),
        P(("groups", "ctx"), "exp", None, None, None),
        P(("groups", "ctx", "exp"), None),
    )
    out_specs = (
        P(("groups", "ctx", "exp"), None),
        P(("groups", "ctx", "exp"), None),
        P(("groups", "ctx"), "exp", None, None, None),
        P(("groups", "ctx"), "exp", None),
        P(("groups", "ctx"), "exp", None),
        P(("groups", "ctx"), "exp", None),
    )
    return jax.shard_map(local, mesh=mesh, in_specs=in_specs, out_specs=out_specs, check_vma=False)
```

```python
import functools

import jax
import jax.numpy as jnp
from jax import lax
from jax.experimental import pallas as pl
from jax.experimental.pallas import tpu as pltpu
from jax.sharding import PartitionSpec as P

BAND_BLOCKS = 4
F32 = jnp.float32
BF16 = jnp.bfloat16
VMEM_LIMIT = 56 * 1024 * 1024


def params(limit=VMEM_LIMIT):
    return pltpu.CompilerParams(vmem_limit_bytes=limit)


def cost(flops, nbytes, exps=0):
    return pl.CostEstimate(flops=flops, bytes_accessed=nbytes, transcendentals=exps)


def dot_nn(a, b):
    return lax.dot_general(a, b, (((1,), (0,)), ((), ())), preferred_element_type=F32)


def dot_nt(a, b):
    return lax.dot_general(a, b, (((1,), (1,)), ((), ())), preferred_element_type=F32)


def dot_tn(a, b):
    return lax.dot_general(a, b, (((0,), (0,)), ((), ())), preferred_element_type=F32)


def passed_along(value, axis, steps):
    count = lax.axis_size(axis)
    initial, last = (max(0, -steps), min(count, count - steps))
    return lax.ppermute(value, axis, [(source, source + steps) for source in range(initial, last)])


def swapped(value, axis):
    return lax.ppermute(value, axis, [(0, 1), (1, 0)])


def exchanged(one, three):
    count = lax.axis_size("ctx")
    pairs = [(c, c ^ 1) for c in range(count)]
    others = [(c, c - 1 if c % 2 else c - 3) for c in range(count) if c % 2 or c >= 4]
    return lax.ppermute(one, "ctx", pairs), lax.ppermute(three, "ctx", others)


def combined(two, by_one, by_three):
    even = lax.axis_index("ctx") % 2 == 0
    onward = (two.astype(F32) + jnp.where(even, by_three, by_one).astype(F32)).astype(BF16)
    return onward, jnp.where(even, by_one, by_three)


def after(values, *others):
    return lax.optimization_barrier((tuple(values), others))[0]


def gathered(w_out, *tasks):
    heads, depth, _ = w_out.shape
    count = lax.axis_size("ctx")
    place = lax.axis_index("ctx")
    if count != 8 or lax.axis_size("groups") != 2 or heads % 2:
        full = lax.all_gather(w_out, "ctx", axis=1, tiled=True)
        for task in tasks:
            task()
        return [full], jnp.zeros((1,), jnp.int32), [(0, heads, 0, 0)]
    side = lax.axis_index("groups")
    half = heads // 2
    ring = lambda value: lax.ppermute(value, "ctx", [(c, (c + 2) % count) for c in range(count)])
    pair = lambda value: lax.ppermute(value, "ctx", [(c, c ^ 1) for c in range(count)])
    cross = lambda value: swapped(value, "groups")
    mine = lax.dynamic_slice_in_dim(w_out, side * half, half, 0)

    z1, y0 = ring(mine), pair(mine)
    z1, y0 = after([z1, y0], *tasks[0]())
    z2, y1, x1 = ring(z1), pair(z1), cross(z1)
    z2, y0 = after([z2, y0], *tasks[1](z1))
    z3, y2, x2 = ring(z2), pair(z2), cross(y0)
    z3, x1 = after([z3, x1], y1, *tasks[2](z2))
    z4, y3, x3 = ring(x1), pair(z3), cross(z3)
    y2, z4 = after([y2, z4], x2, y2)
    x4 = cross(y2)
    y3, last = after([y3, x1], x3, z4)
    y4, x5 = pair(last), cross(y3)
    tasks[3](z4, x3)

    table = [0, side * half, (1 - side) * half]
    table += [depth * ((place - 2 * k) % count) for k in range(4)]
    table += [depth * (((place - 2 * k) % count) ^ 1) for k in range(4)]
    arrays = [w_out, z1, z2, z3, y0, y1, y2, y3, x1, z4, x3, x2, y4, x4, x5]
    plan = [(0, heads, 0, 3)]
    plan += [(1 + k, half, 1, 4 + k) for k in range(7)]
    plan += [(8 + k, half, 2, 4 + k) for k in range(7)]
    return arrays, jnp.stack([jnp.asarray(t, jnp.int32) for t in table]), plan


def piece_copies(plan, table, pieces, buf, sem, chunk, chunk_size):
    copies = []
    columns = pl.ds(pl.multiple_of(chunk * chunk_size, chunk_size), chunk_size)
    depth_of = [p.shape[1] for p in pieces]
    for number, (array, size, head, row) in enumerate(plan):
        rows = pl.ds(pl.multiple_of(table[row], depth_of[array]), depth_of[array])
        copies.append(
            pltpu.make_async_copy(
                pieces[array].at[:, :, columns],
                buf.at[pl.ds(table[head], size), rows, columns],
                sem.at[number, chunk],
            )
        )
    return copies


CHUNKS = 3


def wait_chunk(plan, table, pieces, buf, sem, width):
    step = pl.program_id(0)
    size = width // CHUNKS

    @pl.when(step == 0)
    def _():
        for chunk in range(CHUNKS):
            for copy in piece_copies(plan, table, pieces, buf, sem, chunk, size):
                copy.start()

    for copy in piece_copies(plan, table, pieces, buf, sem, step, size):
        copy.wait()
    return pl.ds(pl.multiple_of(step * size, size), size)


def project_kernel(plan, count, parts, table, core, *refs):
    attn = jnp.concatenate([r[...] for r in refs[:parts]], axis=1)
    refs = refs[parts:]
    pieces, (own, other, buf, sem) = refs[:count], refs[count:]
    heads, head_dim, width = buf.shape
    columns = wait_chunk(plan, table, pieces, buf, sem, width)
    weights = buf[:, :, columns].reshape(heads * head_dim, width // CHUNKS)
    result = dot_nn(attn, weights)
    rows = own.shape[0]

    @pl.when(core[0] == 0)
    def _():
        own[...] = result[:rows]
        other[...] = result[rows:].astype(BF16)

    @pl.when(core[0] != 0)
    def _():
        own[...] = result[rows:]
        other[...] = result[:rows].astype(BF16)


def project(attn, arrays, table, plan, core, heads, head_dim, width, rows):
    tok = attn[0].shape[0]
    size = width // CHUNKS
    return pl.pallas_call(
        functools.partial(project_kernel, plan, len(arrays), len(attn)),
        grid_spec=pltpu.PrefetchScalarGridSpec(
            num_scalar_prefetch=2,
            grid=(CHUNKS,),
            in_specs=[pl.BlockSpec(a.shape, lambda i, *_: (0, 0)) for a in attn]
            + [pl.BlockSpec(memory_space=pl.ANY)] * len(arrays),
            out_specs=[pl.BlockSpec((rows, size), lambda i, *_: (0, i))] * 2,
            scratch_shapes=[
                pltpu.VMEM((heads, head_dim, width), BF16),
                pltpu.SemaphoreType.DMA((len(plan), CHUNKS)),
            ],
        ),
        out_shape=[jax.ShapeDtypeStruct((rows, width), F32), jax.ShapeDtypeStruct((rows, width), BF16)],
        compiler_params=params(),
        cost_estimate=cost(2 * tok * heads * head_dim * width, 2 * heads * head_dim * width),
        name="project",
    )(table, core, *attn, *arrays)


def dattn_kernel(plan, count, table, core, own, recv, *refs):
    pieces, (out, grad, acc, buf, sem) = refs[:count], refs[count:]
    heads, head_dim, width = buf.shape
    rows = own.shape[0]
    step = pl.program_id(0)

    @pl.when(core[0] == 0)
    def _():
        grad[:rows] = own[...]
        grad[rows:] = recv[...]

    @pl.when(core[0] != 0)
    def _():
        grad[rows:] = own[...]
        grad[:rows] = recv[...]

    columns = wait_chunk(plan, table, pieces, buf, sem, width)
    weights = buf[:, :, columns].reshape(heads * head_dim, width // CHUNKS)
    part = dot_nt(grad[...], weights)

    @pl.when(step == 0)
    def _():
        acc[...] = part

    @pl.when(step > 0)
    def _():
        acc[...] += part

    @pl.when(step == CHUNKS - 1)
    def _():
        out[...] = acc[...].astype(BF16)


def dattention(own, recv, arrays, table, plan, core, heads, head_dim, width):
    rows = own.shape[0]
    size = width // CHUNKS
    return pl.pallas_call(
        functools.partial(dattn_kernel, plan, len(arrays)),
        grid_spec=pltpu.PrefetchScalarGridSpec(
            num_scalar_prefetch=2,
            grid=(CHUNKS,),
            in_specs=[pl.BlockSpec((rows, size), lambda i, *_: (0, i))] * 2
            + [pl.BlockSpec(memory_space=pl.ANY)] * len(arrays),
            out_specs=pl.BlockSpec((2 * rows, heads * head_dim), lambda i, *_: (0, 0)),
            scratch_shapes=[
                pltpu.VMEM((2 * rows, size), BF16),
                pltpu.VMEM((2 * rows, heads * head_dim), F32),
                pltpu.VMEM((heads, head_dim, width), BF16),
                pltpu.SemaphoreType.DMA((len(plan), CHUNKS)),
            ],
        ),
        out_shape=jax.ShapeDtypeStruct((2 * rows, heads * head_dim), BF16),
        compiler_params=params(),
        cost_estimate=cost(4 * rows * heads * head_dim * width, 2 * heads * head_dim * width),
        name="dattention",
    )(table, core, own, recv, *arrays)


def band_of(refs):
    return jnp.concatenate([r[...] for r in refs], axis=0)


HEADS_FORWARD = 6


def heads_a_step(most, group):
    return max(n for n in range(1, most + 1) if group % n == 0)


def stacked(ref, count):
    size = ref.shape[1] // count
    return jnp.concatenate([ref[:, i * size : (i + 1) * size] for i in range(count)], axis=0)


def attention_kernel(scale, place, q, *refs):
    keys, values, (attn, probs) = refs[:BAND_BLOCKS], refs[BAND_BLOCKS : 2 * BAND_BLOCKS], refs[-2:]
    count, tok, head_dim = q.shape
    scores = dot_nt(q[...].reshape(count * tok, head_dim), band_of(keys)) * scale
    scores = scores.reshape(count, tok, BAND_BLOCKS * tok)
    row = lax.broadcasted_iota(jnp.int32, scores.shape, 1)
    column = lax.broadcasted_iota(jnp.int32, scores.shape, 2)
    offset = column - (BAND_BLOCKS - 1) * tok
    admitted = (offset <= row) & (offset + place[0] * tok >= 0)
    scores = jnp.where(admitted, scores, -1e30)
    top = jnp.max(scores, axis=-1, keepdims=True)
    grown = jnp.exp(scores - top)
    weight = (grown * (1.0 / jnp.sum(grown, axis=-1, keepdims=True))).astype(BF16)
    probs[...] = weight
    result = dot_nn(weight.reshape(count * tok, BAND_BLOCKS * tok), band_of(values)).astype(BF16)
    for i in range(count):
        attn[:, i * head_dim : (i + 1) * head_dim] = result[i * tok : (i + 1) * tok]


def attention(queries, bands, place, heads, heads_kv, head_dim, scale):
    tok = queries.shape[1]
    group = heads // heads_kv
    count = heads_a_step(HEADS_FORWARD, group)
    keys = pl.BlockSpec((tok, head_dim), lambda h, *_: (0, h * count // group))
    values = pl.BlockSpec((tok, head_dim), lambda h, *_: (0, heads_kv + h * count // group))
    span = BAND_BLOCKS * tok
    return pl.pallas_call(
        functools.partial(attention_kernel, scale),
        grid_spec=pltpu.PrefetchScalarGridSpec(
            num_scalar_prefetch=1,
            grid=(heads // count,),
            in_specs=[pl.BlockSpec((count, tok, head_dim), lambda h, *_: (h, 0, 0))]
            + [keys] * BAND_BLOCKS
            + [values] * BAND_BLOCKS,
            out_specs=[
                pl.BlockSpec((tok, count * head_dim), lambda h, *_: (0, h)),
                pl.BlockSpec((count, tok, span), lambda h, *_: (h, 0, 0)),
            ],
        ),
        out_shape=[
            jax.ShapeDtypeStruct((tok, heads * head_dim), BF16),
            jax.ShapeDtypeStruct((heads, tok, span), BF16),
        ],
        compiler_params=params(),
        cost_estimate=cost(4 * tok * span * heads * head_dim, 2 * heads * tok * span, heads * tok * span),
        name="attention",
    )(place, queries, *bands, *bands)


def score_grads(scale, q, dout, attn, probs, keys, values):
    count, tok, head_dim = q.shape
    grad = stacked(dout, count)
    delta = jnp.sum(grad.astype(F32) * stacked(attn, count).astype(F32), axis=-1, keepdims=True)
    dprob = dot_nt(grad, band_of(values))
    weight = probs[...].reshape(dprob.shape)
    dscore = (weight.astype(F32) * (dprob - delta)).astype(BF16)
    dquery = (dot_nn(dscore, band_of(keys)) * scale).astype(BF16).reshape(count, tok, head_dim)
    return dquery, dot_tn(dscore, q[...].reshape(count * tok, head_dim)) * scale


def value_grads(dout, probs):
    count, tok, span = probs.shape
    return dot_tn(probs[...].reshape(count * tok, span), stacked(dout, count))


def put(outs, part, value):
    tok, head_dim = outs[0].shape[0], value.shape[1]
    for block, out in enumerate(outs):
        rows = value[block * tok : (block + 1) * tok]
        out[:, part * head_dim : (part + 1) * head_dim] = rows.astype(out.dtype)


def first_grad_kernel(scale, heads_kv, q, dout, attn, probs, *refs):
    keys, values = refs[:BAND_BLOCKS], refs[BAND_BLOCKS : 2 * BAND_BLOCKS]
    dq, outs = refs[2 * BAND_BLOCKS], refs[2 * BAND_BLOCKS + 1 :]
    for head in range(heads_kv):

        @pl.when(pl.program_id(0) == head)
        def _():
            if head < heads_kv - 1:
                dq[...], dkey = score_grads(scale, q, dout, attn, probs, keys, values)
                put(outs, heads_kv + head, dkey)
            put(outs, head, value_grads(dout, probs))


def last_grad_kernel(scale, core, q, dout, attn, probs, *refs):
    keys, values = refs[:BAND_BLOCKS], refs[BAND_BLOCKS : 2 * BAND_BLOCKS]
    _, here, back, dq = refs[2 * BAND_BLOCKS : 2 * BAND_BLOCKS + 4]
    outs, (joined, held, sem) = refs[2 * BAND_BLOCKS + 4 : -3], refs[-3:]
    inward = [pltpu.make_async_copy(r, held.at[i], sem.at[0, i]) for i, r in enumerate((here, back))]
    outward = [
        pltpu.make_async_copy(held.at[i], joined.at[0, :, at], sem.at[1, i])
        for i, at in enumerate((core[0], 1 - core[0]))
    ]
    for copy in inward:
        copy.start()
    dquery, dkey = score_grads(scale, q, dout, attn, probs, keys, values)
    for copy in inward:
        copy.wait()
    for copy in outward:
        copy.start()
    dq[...] = dquery
    put(outs, 0, dkey)
    for copy in outward:
        copy.wait()


def grad_specs(tok, head_dim, group, heads_kv, which):
    span = BAND_BLOCKS * tok
    flat = pl.BlockSpec((tok, group * head_dim), lambda h, *_: (0, which(h)))
    keys = pl.BlockSpec((tok, head_dim), lambda h, *_: (0, which(h)))
    values = pl.BlockSpec((tok, head_dim), lambda h, *_: (0, heads_kv + which(h)))
    return (
        [pl.BlockSpec((group, tok, head_dim), lambda h, *_: (which(h), 0, 0)), flat, flat]
        + [pl.BlockSpec((group, tok, span), lambda h, *_: (which(h), 0, 0))]
        + [keys] * BAND_BLOCKS
        + [values] * BAND_BLOCKS
    )


def sums_shapes(tok, lanes):
    return [jax.ShapeDtypeStruct((tok, lanes), BF16)] * (BAND_BLOCKS - 1) + [
        jax.ShapeDtypeStruct((tok, lanes), F32)
    ]


def first_grads(queries, dout, attn, probs, bands, heads_kv, scale):
    heads, tok, head_dim = queries.shape
    group = heads // heads_kv
    lanes = (2 * heads_kv - 1) * head_dim
    whole = pl.BlockSpec((tok, lanes), lambda h: (0, 0))
    return pl.pallas_call(
        functools.partial(first_grad_kernel, scale, heads_kv),
        grid=(heads_kv,),
        in_specs=grad_specs(tok, head_dim, group, heads_kv, lambda h: h),
        out_specs=[pl.BlockSpec((group, tok, head_dim), lambda h: (jnp.minimum(h, heads_kv - 2), 0, 0))]
        + [whole] * BAND_BLOCKS,
        out_shape=[jax.ShapeDtypeStruct((heads, tok, head_dim), BF16)] + sums_shapes(tok, lanes),
        compiler_params=params(),
        cost_estimate=cost(tok, tok),
        name="first_grads",
    )(queries, dout, attn, probs, *bands, *bands)


def last_grads(core, queries, dout, attn, probs, bands, grad_q, here, back, heads_kv, scale):
    heads, tok, head_dim = queries.shape
    group = heads // heads_kv
    held, capacity, width = here.shape
    anywhere = pl.BlockSpec(memory_space=pl.ANY)
    whole = pl.BlockSpec((tok, head_dim), lambda h, *_: (0, 0))
    return pl.pallas_call(
        functools.partial(last_grad_kernel, scale),
        grid_spec=pltpu.PrefetchScalarGridSpec(
            num_scalar_prefetch=1,
            grid=(1,),
            in_specs=grad_specs(tok, head_dim, group, heads_kv, lambda h: heads_kv - 1) + [anywhere] * 3,
            out_specs=[pl.BlockSpec((group, tok, head_dim), lambda h, *_: (heads_kv - 1, 0, 0))]
            + [whole] * BAND_BLOCKS
            + [anywhere],
            scratch_shapes=[pltpu.VMEM((2, held, capacity, width), BF16), pltpu.SemaphoreType.DMA((2, 2))],
        ),
        out_shape=[jax.ShapeDtypeStruct((heads, tok, head_dim), BF16)]
        + sums_shapes(tok, head_dim)
        + [jax.ShapeDtypeStruct((1, held, 2, capacity, width), BF16)],
        input_output_aliases={5 + 2 * BAND_BLOCKS: 0},
        compiler_params=params(),
        cost_estimate=cost(tok, tok),
        name="last_grads",
    )(core, queries, dout, attn, probs, *bands, *bands, grad_q, here, back)


def pick_kernel(core, slots, here_ref, there_ref, gout, first, second, dgate):
    step = pl.program_id(0)
    rows, width = gout.shape
    held, capacity, size = here_ref.shape
    room = held * capacity
    here, there = (r[...].reshape(room, size) for r in (here_ref, there_ref))
    column = lax.broadcasted_iota(jnp.int32, (rows, room), 1)
    grad = gout[...].astype(F32)
    sums = []
    for i, out in enumerate((first, second)):
        near = (slots[:, i : i + 1] == column).astype(BF16)
        far = (slots[:, i : i + 1] == column + room).astype(BF16)
        row = dot_nn(near, here) + dot_nn(far, there)
        out[...] = row.astype(BF16)
        sums.append(jnp.sum(grad * row, axis=-1, keepdims=True))
    lane = lax.broadcasted_iota(jnp.int32, dgate.shape, 1)
    total = jnp.where(lane == 0, sums[0], jnp.where(lane == 1, sums[1], 0.0))

    @pl.when(step == 0)
    def _():
        dgate[...] = total

    @pl.when(step > 0)
    def _():
        dgate[...] += total


def pick(core, slots, here, there, grad_out):
    rows, width = grad_out.shape
    held, capacity = here.shape[1], here.shape[3]
    room = held * capacity
    size = width // CHUNKS
    by_column = lambda n: pl.BlockSpec((n, size), lambda i, core: (0, i))
    table = pl.BlockSpec((None, held, None, capacity, size), lambda i, core: (0, 0, core[0], 0, i))
    whole = lambda n: pl.BlockSpec((rows, n), lambda i, core: (0, 0))
    return pl.pallas_call(
        pick_kernel,
        grid_spec=pltpu.PrefetchScalarGridSpec(
            num_scalar_prefetch=1,
            grid=(CHUNKS,),
            in_specs=[whole(2), table, table, by_column(rows)],
            out_specs=[by_column(rows), by_column(rows), whole(128)],
        ),
        out_shape=[jax.ShapeDtypeStruct((rows, width), BF16)] * 2 + [jax.ShapeDtypeStruct((rows, 128), F32)],
        compiler_params=params(),
        cost_estimate=cost(8 * rows * room * width, 8 * rows * width + 4 * room * width),
        name="pick",
    )(core, slots, here, there, grad_out)


def middle_kernel(experts, routes, own, recv, stream, first, second, gout, dgate, router, router_t, mixed, grad, gates):
    resid = stream[...].astype(F32) + (own[...] + recv[...].astype(F32))
    inverse = lax.rsqrt(jnp.mean(resid * resid, axis=-1, keepdims=True) + 1e-05)
    normed = (resid * inverse).astype(BF16)
    logits = dot_nn(normed, router[...])
    lane = lax.broadcasted_iota(jnp.int32, logits.shape, 1)
    is_first, is_second = lane == routes[:, 0:1], lane == routes[:, 1:2]
    chosen_first = jnp.sum(jnp.where(is_first, logits, 0.0), axis=-1, keepdims=True)
    chosen_second = jnp.sum(jnp.where(is_second, logits, 0.0), axis=-1, keepdims=True)
    gate_first = 1.0 / (1.0 + jnp.exp(chosen_second - chosen_first))
    gate_second = 1.0 - gate_first
    mixed[...] = (
        resid + gate_first * first[...].astype(F32) + gate_second * second[...].astype(F32)
    ).astype(BF16)
    d_first, d_second = dgate[:, 0:1], dgate[:, 1:2]
    common = gate_first * d_first + gate_second * d_second
    expert = lane % experts
    dlogit = jnp.where(expert == routes[:, 0:1], gate_first * (d_first - common), 0.0)
    dlogit = dlogit + jnp.where(expert == routes[:, 1:2], gate_second * (d_second - common), 0.0)
    high = dlogit.astype(BF16)
    rest = dlogit - high.astype(F32)
    middle = rest.astype(BF16)
    low = (rest - middle.astype(F32)).astype(BF16)
    part = lane // experts
    parts = jnp.where(part == 0, high.astype(F32), jnp.where(part == 1, middle.astype(F32), low.astype(F32)))
    dnormed = dot_nn(parts.astype(BF16), router_t[...])
    mean = jnp.mean(dnormed * resid, axis=-1, keepdims=True)
    grad[...] = (
        gout[...].astype(F32) + inverse * dnormed - resid * (inverse * inverse * inverse * mean)
    ).astype(BF16)
    gates[...] = jnp.where(lane == 0, gate_first, jnp.where(lane == 1, gate_second, 0.0))


MIDDLE_ROWS = 64


def middle(routes, own, recv, stream, first, second, grad_out, dgate, router, router_t, experts):
    rows, width = stream.shape
    size = MIDDLE_ROWS if rows % MIDDLE_ROWS == 0 else rows
    by_row = lambda n: pl.BlockSpec((size, n), lambda i: (i, 0))
    whole = lambda a: pl.BlockSpec(a.shape, lambda i: (0, 0))
    return pl.pallas_call(
        functools.partial(middle_kernel, experts),
        grid=(rows // size,),
        in_specs=[by_row(2)] + [by_row(width)] * 6 + [by_row(128), whole(router), whole(router_t)],
        out_specs=[by_row(width), by_row(width), by_row(128)],
        out_shape=[jax.ShapeDtypeStruct((rows, width), BF16)] * 2 + [jax.ShapeDtypeStruct((rows, 128), F32)],
        compiler_params=params(),
        cost_estimate=cost(2 * rows * 128 * width * 4, 20 * rows * width),
        name="middle",
    )(routes, own, recv, stream, first, second, grad_out, dgate, router, router_t)


def spread_kernel(slots, gates, gout, here, there):
    room = here.shape[0]
    rows = gout.shape[0]
    place = lax.broadcasted_iota(jnp.int32, (room, rows), 0)
    grad = gout[...].astype(F32)
    near, far = 0.0, 0.0
    for i in range(2):
        part = (gates[:, i : i + 1] * grad).astype(BF16)
        near = near + dot_nn((slots[i : i + 1, :] == place).astype(BF16), part)
        far = far + dot_nn((slots[i : i + 1, :] == place + room).astype(BF16), part)
    here[...] = near.astype(BF16)
    there[...] = far.astype(BF16)


def spread(slots_t, gates, grad_out, room):
    rows, width = grad_out.shape
    size = width // CHUNKS
    by_column = lambda n: pl.BlockSpec((n, size), lambda i: (0, i))
    return pl.pallas_call(
        spread_kernel,
        grid=(CHUNKS,),
        in_specs=[
            pl.BlockSpec((2, rows), lambda i: (0, 0)),
            pl.BlockSpec((rows, 128), lambda i: (0, 0)),
            by_column(rows),
        ],
        out_specs=[by_column(room)] * 2,
        out_shape=[jax.ShapeDtypeStruct((room, width), BF16)] * 2,
        compiler_params=params(),
        cost_estimate=cost(8 * rows * room * width, 2 * rows * width + 4 * room * width),
        name="spread",
    )(slots_t, gates, grad_out)


def local(
    queries_in, rotated_keys, value_inputs, stream_in, w_out, w_router, routes, expert_out, grad_out
):
    place = lax.axis_index("ctx")
    core = lax.axis_index("exp")
    tok, heads_q, head_dim = queries_in.shape
    heads_kv = rotated_keys.shape[1]
    rows, width = stream_in.shape
    experts = w_router.shape[1]
    held, capacity = expert_out.shape[1], expert_out.shape[3]
    room = held * capacity
    scale = head_dim ** (-0.5)
    core_arg = core.astype(jnp.int32).reshape(1)
    place_arg = place.astype(jnp.int32).reshape(1)

    own_band = jnp.concatenate(
        [rotated_keys.reshape(tok, heads_kv * head_dim), value_inputs.reshape(tok, heads_kv * head_dim)], axis=1
    )
    queries = jnp.transpose(queries_in, (1, 0, 2))
    flat = routes.reshape(-1)
    number = jnp.arange(2 * rows, dtype=jnp.int32)
    earlier = (flat[None, :] == flat[:, None]) & (number[None, :] < number[:, None])
    rank = jnp.sum(earlier.astype(jnp.int32), axis=1)
    slots = (flat * capacity + rank - core * room) % (experts * capacity)
    slots = slots.reshape(rows, 2)
    router = jnp.pad(w_router, ((0, 0), (0, 128 - experts)))
    router_t = jnp.pad(jnp.concatenate([w_router.T] * 3, axis=0), ((0, 128 - 3 * experts), (0, 0)))
    made = {}

    def prepare(*ready):
        return [slots, own_band, router, router_t]

    def swap_rows(*ready):
        rows_out = after([expert_out], *ready)[0]
        made["rows"] = swapped(rows_out, "exp")
        return [made["rows"]]

    def pick_rows(*ready):
        arrived = after([made["rows"]], *ready)[0]
        made["picked"] = pick(core_arg, slots, expert_out, arrived, grad_out)
        return [made["picked"][2]]

    def attend(*ready):
        band = after([own_band], *ready)[0]
        bands = [band] + [passed_along(band, "ctx", step) for step in range(1, BAND_BLOCKS)]
        made["bands"] = bands[::-1]
        made["attention"] = attention(
            queries, made["bands"], place_arg, heads_q, heads_kv, head_dim, scale
        )

    arrays, table, plan = gathered(w_out, prepare, swap_rows, pick_rows, attend)
    first, second, dgate = made["picked"]
    attn, probs = made["attention"]
    bands = made["bands"]

    own, other = project([attn], arrays, table, plan, core_arg, heads_q, head_dim, width, rows)
    mixed, grad_input, gates = middle(
        routes, own, swapped(other, "exp"), stream_in, first, second, grad_out, dgate, router, router_t, experts
    )
    grad_other = swapped(grad_input, "exp")
    here, there = spread(slots.T, gates, grad_out, room)
    dattn = dattention(grad_input, grad_other, arrays, table, plan, core_arg, heads_q, head_dim, width)
    there = after([there], dattn)[0]
    back = swapped(there, "exp").reshape(held, capacity, width)
    here = here.reshape(held, capacity, width)
    early = first_grads(queries, dattn, attn, probs, bands, heads_kv, scale)
    early_by = exchanged(early[BAND_BLOCKS - 1], early[BAND_BLOCKS - 3])
    late = last_grads(core_arg, queries, dattn, attn, probs, bands, early[0], here, back, heads_kv, scale)
    early_by = after(early_by, late[0])
    late_by = exchanged(late[BAND_BLOCKS - 1], late[BAND_BLOCKS - 3])
    early_sum, early_part = combined(early[BAND_BLOCKS - 2], *early_by)
    late_by = after(late_by, early_sum)
    late_sum, late_part = combined(late[BAND_BLOCKS - 2], *late_by)
    sums = []
    for grad, onward, part in ((early, early_sum, early_part), (late, late_sum, late_part)):
        moved = passed_along(onward, "ctx", -2)
        sums.append((grad[BAND_BLOCKS] + (moved.astype(F32) + part.astype(F32))).astype(BF16))
    sums = jnp.concatenate(sums, axis=1).reshape(tok, 2, heads_kv, head_dim)
    grad_v, grad_k = sums[:, 0], sums[:, 1]
    grad_q = jnp.transpose(late[0], (1, 0, 2))
    grad_expert = late[1 + BAND_BLOCKS]
    return (mixed, grad_input, grad_expert, grad_q, grad_k, grad_v)


def solution(mesh):
    in_specs = (
        P(("groups", "ctx"), "exp", None),
        P(("groups", "ctx"), "exp", None),
        P(("groups", "ctx"), "exp", None),
        P(("groups", "ctx", "exp"), None),
        P("exp", "ctx", None),
        P(),
        P(("groups", "ctx", "exp"), None),
        P(("groups", "ctx"), "exp", None, None, None),
        P(("groups", "ctx", "exp"), None),
    )
    out_specs = (
        P(("groups", "ctx", "exp"), None),
        P(("groups", "ctx", "exp"), None),
        P(("groups", "ctx"), "exp", None, None, None),
        P(("groups", "ctx"), "exp", None),
        P(("groups", "ctx"), "exp", None),
        P(("groups", "ctx"), "exp", None),
    )
    return jax.shard_map(local, mesh=mesh, in_specs=in_specs, out_specs=out_specs, check_vma=False)
```

```python
import functools

import jax
import jax.numpy as jnp
from jax import lax
from jax.experimental import pallas as pl
from jax.experimental.pallas import tpu as pltpu
from jax.sharding import PartitionSpec as P

BAND_BLOCKS = 4
F32 = jnp.float32
BF16 = jnp.bfloat16
VMEM_LIMIT = 56 * 1024 * 1024


def params(limit=VMEM_LIMIT):
    return pltpu.CompilerParams(vmem_limit_bytes=limit)


def cost(flops, nbytes, exps=0):
    return pl.CostEstimate(flops=flops, bytes_accessed=nbytes, transcendentals=exps)


def dot_nn(a, b):
    return lax.dot_general(a, b, (((1,), (0,)), ((), ())), preferred_element_type=F32)


def dot_nt(a, b):
    return lax.dot_general(a, b, (((1,), (1,)), ((), ())), preferred_element_type=F32)


def dot_tn(a, b):
    return lax.dot_general(a, b, (((0,), (0,)), ((), ())), preferred_element_type=F32)


def passed_along(value, axis, steps):
    count = lax.axis_size(axis)
    initial, last = (max(0, -steps), min(count, count - steps))
    return lax.ppermute(value, axis, [(source, source + steps) for source in range(initial, last)])


def swapped(value, axis):
    return lax.ppermute(value, axis, [(0, 1), (1, 0)])


def exchanged(one, three):
    count = lax.axis_size("ctx")
    pairs = [(c, c ^ 1) for c in range(count)]
    others = [(c, c - 1 if c % 2 else c - 3) for c in range(count) if c % 2 or c >= 4]
    return lax.ppermute(one, "ctx", pairs), lax.ppermute(three, "ctx", others)


def combined(two, by_one, by_three):
    even = lax.axis_index("ctx") % 2 == 0
    onward = (two.astype(F32) + jnp.where(even, by_three, by_one).astype(F32)).astype(BF16)
    return passed_along(onward, "ctx", -2), jnp.where(even, by_one, by_three)


def after(values, *others):
    return lax.optimization_barrier((tuple(values), others))[0]


def gathered(w_out, *tasks):
    heads, depth, _ = w_out.shape
    count = lax.axis_size("ctx")
    place = lax.axis_index("ctx")
    if count != 8 or lax.axis_size("groups") != 2 or heads % 2:
        full = lax.all_gather(w_out, "ctx", axis=1, tiled=True)
        for task in tasks:
            task()
        return [full], jnp.zeros((1,), jnp.int32), [(0, heads, 0, 0)]
    side = lax.axis_index("groups")
    half = heads // 2
    ring = lambda value: lax.ppermute(value, "ctx", [(c, (c + 2) % count) for c in range(count)])
    pair = lambda value: lax.ppermute(value, "ctx", [(c, c ^ 1) for c in range(count)])
    cross = lambda value: swapped(value, "groups")
    mine = lax.dynamic_slice_in_dim(w_out, side * half, half, 0)

    z1, y0 = ring(mine), pair(mine)
    z1, y0 = after([z1, y0], *tasks[0]())
    z2, y1, x1 = ring(z1), pair(z1), cross(z1)
    z2, y0 = after([z2, y0], *tasks[1](z1))
    z3, y2, x2 = ring(z2), pair(z2), cross(y0)
    z3, x1 = after([z3, x1], y1, *tasks[2](z2))
    z4, y3, x3 = ring(x1), pair(z3), cross(z3)
    y2, z4 = after([y2, z4], x2, y2)
    x4 = cross(y2)
    y3, last = after([y3, x1], x3, z4)
    y4, x5 = pair(last), cross(y3)
    tasks[3](z4, x3)

    table = [0, side * half, (1 - side) * half]
    table += [depth * ((place - 2 * k) % count) for k in range(4)]
    table += [depth * (((place - 2 * k) % count) ^ 1) for k in range(4)]
    arrays = [w_out, z1, z2, z3, y0, y1, y2, y3, x1, z4, x3, x2, y4, x4, x5]
    plan = [(0, heads, 0, 3)]
    plan += [(1 + k, half, 1, 4 + k) for k in range(7)]
    plan += [(8 + k, half, 2, 4 + k) for k in range(7)]
    return arrays, jnp.stack([jnp.asarray(t, jnp.int32) for t in table]), plan


def piece_copies(plan, table, pieces, buf, sem, chunk, chunk_size):
    copies = []
    columns = pl.ds(pl.multiple_of(chunk * chunk_size, chunk_size), chunk_size)
    depth_of = [p.shape[1] for p in pieces]
    for number, (array, size, head, row) in enumerate(plan):
        rows = pl.ds(pl.multiple_of(table[row], depth_of[array]), depth_of[array])
        copies.append(
            pltpu.make_async_copy(
                pieces[array].at[:, :, columns],
                buf.at[pl.ds(table[head], size), rows, columns],
                sem.at[number, chunk],
            )
        )
    return copies


CHUNKS = 3


def wait_chunk(plan, table, pieces, buf, sem, width):
    step = pl.program_id(0)
    size = width // CHUNKS

    @pl.when(step == 0)
    def _():
        for chunk in range(CHUNKS):
            for copy in piece_copies(plan, table, pieces, buf, sem, chunk, size):
                copy.start()

    for copy in piece_copies(plan, table, pieces, buf, sem, step, size):
        copy.wait()
    return pl.ds(pl.multiple_of(step * size, size), size)


def project_kernel(plan, count, parts, table, core, *refs):
    attn = jnp.concatenate([r[...] for r in refs[:parts]], axis=1)
    refs = refs[parts:]
    pieces, (own, other, buf, sem) = refs[:count], refs[count:]
    heads, head_dim, width = buf.shape
    columns = wait_chunk(plan, table, pieces, buf, sem, width)
    weights = buf[:, :, columns].reshape(heads * head_dim, width // CHUNKS)
    result = dot_nn(attn, weights)
    rows = own.shape[0]

    @pl.when(core[0] == 0)
    def _():
        own[...] = result[:rows]
        other[...] = result[rows:].astype(BF16)

    @pl.when(core[0] != 0)
    def _():
        own[...] = result[rows:]
        other[...] = result[:rows].astype(BF16)


def project(attn, arrays, table, plan, core, heads, head_dim, width, rows):
    tok = attn[0].shape[0]
    size = width // CHUNKS
    return pl.pallas_call(
        functools.partial(project_kernel, plan, len(arrays), len(attn)),
        grid_spec=pltpu.PrefetchScalarGridSpec(
            num_scalar_prefetch=2,
            grid=(CHUNKS,),
            in_specs=[pl.BlockSpec(a.shape, lambda i, *_: (0, 0)) for a in attn]
            + [pl.BlockSpec(memory_space=pl.ANY)] * len(arrays),
            out_specs=[pl.BlockSpec((rows, size), lambda i, *_: (0, i))] * 2,
            scratch_shapes=[
                pltpu.VMEM((heads, head_dim, width), BF16),
                pltpu.SemaphoreType.DMA((len(plan), CHUNKS)),
            ],
        ),
        out_shape=[jax.ShapeDtypeStruct((rows, width), F32), jax.ShapeDtypeStruct((rows, width), BF16)],
        compiler_params=params(20 << 20),
        cost_estimate=cost(2 * tok * heads * head_dim * width, 2 * heads * head_dim * width),
        name="project",
    )(table, core, *attn, *arrays)


def dattn_kernel(plan, count, table, core, own, recv, *refs):
    pieces, (out, grad, acc, buf, sem) = refs[:count], refs[count:]
    heads, head_dim, width = buf.shape
    rows = own.shape[0]
    step = pl.program_id(0)

    @pl.when(core[0] == 0)
    def _():
        grad[:rows] = own[...]
        grad[rows:] = recv[...]

    @pl.when(core[0] != 0)
    def _():
        grad[rows:] = own[...]
        grad[:rows] = recv[...]

    columns = wait_chunk(plan, table, pieces, buf, sem, width)
    weights = buf[:, :, columns].reshape(heads * head_dim, width // CHUNKS)
    part = dot_nt(grad[...], weights)

    @pl.when(step == 0)
    def _():
        acc[...] = part

    @pl.when(step > 0)
    def _():
        acc[...] += part

    @pl.when(step == CHUNKS - 1)
    def _():
        out[...] = acc[...].astype(BF16)


def dattention(own, recv, arrays, table, plan, core, heads, head_dim, width):
    rows = own.shape[0]
    size = width // CHUNKS
    return pl.pallas_call(
        functools.partial(dattn_kernel, plan, len(arrays)),
        grid_spec=pltpu.PrefetchScalarGridSpec(
            num_scalar_prefetch=2,
            grid=(CHUNKS,),
            in_specs=[pl.BlockSpec((rows, size), lambda i, *_: (0, i))] * 2
            + [pl.BlockSpec(memory_space=pl.ANY)] * len(arrays),
            out_specs=pl.BlockSpec((2 * rows, heads * head_dim), lambda i, *_: (0, 0)),
            scratch_shapes=[
                pltpu.VMEM((2 * rows, size), BF16),
                pltpu.VMEM((2 * rows, heads * head_dim), F32),
                pltpu.VMEM((heads, head_dim, width), BF16),
                pltpu.SemaphoreType.DMA((len(plan), CHUNKS)),
            ],
        ),
        out_shape=jax.ShapeDtypeStruct((2 * rows, heads * head_dim), BF16),
        compiler_params=params(20 << 20),
        cost_estimate=cost(4 * rows * heads * head_dim * width, 2 * heads * head_dim * width),
        name="dattention",
    )(table, core, own, recv, *arrays)


def band_of(refs):
    return jnp.concatenate([r[...] for r in refs], axis=0)


HEADS_FORWARD = 6
HEADS_BACKWARD = 6


def heads_a_step(most, group):
    return max(n for n in range(1, most + 1) if group % n == 0)


def stacked(ref, count):
    size = ref.shape[1] // count
    return jnp.concatenate([ref[:, i * size : (i + 1) * size] for i in range(count)], axis=0)


def attention_kernel(scale, place, q, *refs):
    keys, values, (attn, probs) = refs[:BAND_BLOCKS], refs[BAND_BLOCKS : 2 * BAND_BLOCKS], refs[-2:]
    count, tok, head_dim = q.shape
    scores = dot_nt(q[...].reshape(count * tok, head_dim), band_of(keys)) * scale
    scores = scores.reshape(count, tok, BAND_BLOCKS * tok)
    row = lax.broadcasted_iota(jnp.int32, scores.shape, 1)
    column = lax.broadcasted_iota(jnp.int32, scores.shape, 2)
    offset = column - (BAND_BLOCKS - 1) * tok
    admitted = (offset <= row) & (offset + place[0] * tok >= 0)
    scores = jnp.where(admitted, scores, -1e30)
    top = jnp.max(scores, axis=-1, keepdims=True)
    grown = jnp.exp(scores - top)
    weight = (grown * (1.0 / jnp.sum(grown, axis=-1, keepdims=True))).astype(BF16)
    probs[...] = weight
    result = dot_nn(weight.reshape(count * tok, BAND_BLOCKS * tok), band_of(values)).astype(BF16)
    for i in range(count):
        attn[:, i * head_dim : (i + 1) * head_dim] = result[i * tok : (i + 1) * tok]


def attention(queries, bands, place, heads, heads_kv, head_dim, scale):
    tok = queries.shape[1]
    group = heads // heads_kv
    count = heads_a_step(HEADS_FORWARD, group)
    keys = pl.BlockSpec((tok, head_dim), lambda h, *_: (0, h * count // group))
    values = pl.BlockSpec((tok, head_dim), lambda h, *_: (0, heads_kv + h * count // group))
    span = BAND_BLOCKS * tok
    return pl.pallas_call(
        functools.partial(attention_kernel, scale),
        grid_spec=pltpu.PrefetchScalarGridSpec(
            num_scalar_prefetch=1,
            grid=(heads // count,),
            in_specs=[pl.BlockSpec((count, tok, head_dim), lambda h, *_: (h, 0, 0))]
            + [keys] * BAND_BLOCKS
            + [values] * BAND_BLOCKS,
            out_specs=[
                pl.BlockSpec((tok, count * head_dim), lambda h, *_: (0, h)),
                pl.BlockSpec((count, tok, span), lambda h, *_: (h, 0, 0)),
            ],
        ),
        out_shape=[
            jax.ShapeDtypeStruct((tok, heads * head_dim), BF16),
            jax.ShapeDtypeStruct((heads, tok, span), BF16),
        ],
        compiler_params=params(),
        cost_estimate=cost(4 * tok * span * heads * head_dim, 2 * heads * tok * span, heads * tok * span),
        name="attention",
    )(place, queries, *bands, *bands)


def attention_grad_kernel(scale, steps, last, q, dout, attn, probs, *refs):
    refs = list(refs)
    keys, values = refs[:BAND_BLOCKS], refs[BAND_BLOCKS : 2 * BAND_BLOCKS]
    refs = refs[2 * BAND_BLOCKS :]
    if last:
        (_, core, here, back), refs, (held, sem) = refs[:4], refs[4:-2], refs[-2:]
        joined = refs.pop(1 + BAND_BLOCKS)
        places = core[0], 1 - core[0]
        inward = [pltpu.make_async_copy(r, held.at[i], sem.at[0, i]) for i, r in enumerate((here, back))]
        outward = [
            pltpu.make_async_copy(held.at[i], joined.at[0, :, at], sem.at[1, i]) for i, at in enumerate(places)
        ]

        @pl.when(pl.program_id(0) == 0)
        def _():
            for copy in inward:
                copy.start()

    dq, outs, (dk, dv) = refs[0], refs[1:-2], refs[-2:]
    count, tok, head_dim = q.shape
    step = pl.program_id(0)
    grad = stacked(dout, count)
    weight = probs[...].reshape(count * tok, BAND_BLOCKS * tok)
    delta = jnp.sum(grad.astype(F32) * stacked(attn, count).astype(F32), axis=-1, keepdims=True)
    dprob = dot_nt(grad, band_of(values))
    dscore = (weight.astype(F32) * (dprob - delta)).astype(BF16)
    dq[...] = (dot_nn(dscore, band_of(keys)) * scale).astype(BF16).reshape(count, tok, head_dim)
    if last:

        @pl.when(step == 0)
        def _():
            for copy in inward:
                copy.wait()
            for copy in outward:
                copy.start()

    dkey = dot_tn(dscore, q[...].reshape(count * tok, head_dim))
    dvalue = dot_tn(weight, grad)

    @pl.when(step == 0)
    def _():
        dk[...] = dkey
        dv[...] = dvalue

    @pl.when(step > 0)
    def _():
        dk[...] += dkey
        dv[...] += dvalue

    @pl.when(step == steps - 1)
    def _():
        for block, out in enumerate(outs):
            rows = pl.ds(block * tok, tok)
            out[:, :head_dim] = (dk[rows, :] * scale).astype(out.dtype)
            out[:, head_dim:] = dv[rows, :].astype(out.dtype)
        if last:
            for copy in outward:
                copy.wait()


def attention_grad(queries, dout, attn, probs, bands, which, given, heads_kv, scale):
    heads, tok, head_dim = queries.shape
    group = heads // heads_kv
    count = heads_a_step(HEADS_BACKWARD, group)
    steps = group // count
    keys = pl.BlockSpec((tok, head_dim), lambda h: (0, which))
    values = pl.BlockSpec((tok, head_dim), lambda h: (0, heads_kv + which))
    by_head = pl.BlockSpec((count, tok, head_dim), lambda h: (which * steps + h, 0, 0))
    of_all = pl.BlockSpec((tok, count * head_dim), lambda h: (0, which * steps + h))
    span = BAND_BLOCKS * tok
    whole = pl.BlockSpec((tok, 2 * head_dim), lambda h: (0, 0))
    anywhere = pl.BlockSpec(memory_space=pl.ANY)
    last = bool(given)
    joined, extra = [], []
    if last:
        held, capacity, width = given[2].shape
        joined = [jax.ShapeDtypeStruct((1, held, 2, capacity, width), BF16)]
        extra = [pltpu.VMEM((2, held, capacity, width), BF16), pltpu.SemaphoreType.DMA((2, 2))]
    return pl.pallas_call(
        functools.partial(attention_grad_kernel, scale, steps, last),
        grid=(steps,),
        in_specs=[by_head, of_all, of_all]
        + [pl.BlockSpec((count, tok, span), lambda h: (which * steps + h, 0, 0))]
        + [keys] * BAND_BLOCKS
        + [values] * BAND_BLOCKS
        + ([anywhere, pl.BlockSpec(memory_space=pltpu.SMEM), anywhere, anywhere] if last else []),
        out_specs=[by_head] + [whole] * BAND_BLOCKS + [anywhere] * len(joined),
        out_shape=[jax.ShapeDtypeStruct((heads, tok, head_dim), BF16)]
        + [jax.ShapeDtypeStruct((tok, 2 * head_dim), BF16)] * (BAND_BLOCKS - 1)
        + [jax.ShapeDtypeStruct((tok, 2 * head_dim), F32)]
        + joined,
        scratch_shapes=[pltpu.VMEM((span, head_dim), F32)] * 2 + extra,
        input_output_aliases={4 + 2 * BAND_BLOCKS: 0} if last else {},
        compiler_params=params(),
        cost_estimate=cost(tok, tok),
        name="attention_grad",
    )(queries, dout, attn, probs, *bands, *bands, *given)


def pick_kernel(core, slots, here_ref, there_ref, gout, first, second, dgate):
    step = pl.program_id(0)
    rows, width = gout.shape
    held, capacity, size = here_ref.shape
    room = held * capacity
    here, there = (r[...].reshape(room, size) for r in (here_ref, there_ref))
    column = lax.broadcasted_iota(jnp.int32, (rows, room), 1)
    grad = gout[...].astype(F32)
    sums = []
    for i, out in enumerate((first, second)):
        near = (slots[:, i : i + 1] == column).astype(BF16)
        far = (slots[:, i : i + 1] == column + room).astype(BF16)
        row = dot_nn(near, here) + dot_nn(far, there)
        out[...] = row.astype(BF16)
        sums.append(jnp.sum(grad * row, axis=-1, keepdims=True))
    lane = lax.broadcasted_iota(jnp.int32, dgate.shape, 1)
    total = jnp.where(lane == 0, sums[0], jnp.where(lane == 1, sums[1], 0.0))

    @pl.when(step == 0)
    def _():
        dgate[...] = total

    @pl.when(step > 0)
    def _():
        dgate[...] += total


def pick(core, slots, here, there, grad_out):
    rows, width = grad_out.shape
    held, capacity = here.shape[1], here.shape[3]
    room = held * capacity
    size = width // CHUNKS
    by_column = lambda n: pl.BlockSpec((n, size), lambda i, core: (0, i))
    table = pl.BlockSpec((None, held, None, capacity, size), lambda i, core: (0, 0, core[0], 0, i))
    whole = lambda n: pl.BlockSpec((rows, n), lambda i, core: (0, 0))
    return pl.pallas_call(
        pick_kernel,
        grid_spec=pltpu.PrefetchScalarGridSpec(
            num_scalar_prefetch=1,
            grid=(CHUNKS,),
            in_specs=[whole(2), table, table, by_column(rows)],
            out_specs=[by_column(rows), by_column(rows), whole(128)],
        ),
        out_shape=[jax.ShapeDtypeStruct((rows, width), BF16)] * 2 + [jax.ShapeDtypeStruct((rows, 128), F32)],
        compiler_params=params(),
        cost_estimate=cost(8 * rows * room * width, 8 * rows * width + 4 * room * width),
        name="pick",
    )(core, slots, here, there, grad_out)


def middle_kernel(experts, routes, own, recv, stream, first, second, gout, dgate, router, router_t, mixed, grad, gates):
    resid = stream[...].astype(F32) + (own[...] + recv[...].astype(F32))
    inverse = lax.rsqrt(jnp.mean(resid * resid, axis=-1, keepdims=True) + 1e-05)
    normed = (resid * inverse).astype(BF16)
    logits = dot_nn(normed, router[...])
    lane = lax.broadcasted_iota(jnp.int32, logits.shape, 1)
    is_first, is_second = lane == routes[:, 0:1], lane == routes[:, 1:2]
    chosen_first = jnp.sum(jnp.where(is_first, logits, 0.0), axis=-1, keepdims=True)
    chosen_second = jnp.sum(jnp.where(is_second, logits, 0.0), axis=-1, keepdims=True)
    gate_first = 1.0 / (1.0 + jnp.exp(chosen_second - chosen_first))
    gate_second = 1.0 - gate_first
    mixed[...] = (
        resid + gate_first * first[...].astype(F32) + gate_second * second[...].astype(F32)
    ).astype(BF16)
    d_first, d_second = dgate[:, 0:1], dgate[:, 1:2]
    common = gate_first * d_first + gate_second * d_second
    expert = lane % experts
    dlogit = jnp.where(expert == routes[:, 0:1], gate_first * (d_first - common), 0.0)
    dlogit = dlogit + jnp.where(expert == routes[:, 1:2], gate_second * (d_second - common), 0.0)
    high = dlogit.astype(BF16)
    rest = dlogit - high.astype(F32)
    middle = rest.astype(BF16)
    low = (rest - middle.astype(F32)).astype(BF16)
    part = lane // experts
    parts = jnp.where(part == 0, high.astype(F32), jnp.where(part == 1, middle.astype(F32), low.astype(F32)))
    dnormed = dot_nn(parts.astype(BF16), router_t[...])
    mean = jnp.mean(dnormed * resid, axis=-1, keepdims=True)
    grad[...] = (
        gout[...].astype(F32) + inverse * dnormed - resid * (inverse * inverse * inverse * mean)
    ).astype(BF16)
    gates[...] = jnp.where(lane == 0, gate_first, jnp.where(lane == 1, gate_second, 0.0))


MIDDLE_ROWS = 64


def middle(routes, own, recv, stream, first, second, grad_out, dgate, router, router_t, experts):
    rows, width = stream.shape
    size = MIDDLE_ROWS if rows % MIDDLE_ROWS == 0 else rows
    by_row = lambda n: pl.BlockSpec((size, n), lambda i: (i, 0))
    whole = lambda a: pl.BlockSpec(a.shape, lambda i: (0, 0))
    return pl.pallas_call(
        functools.partial(middle_kernel, experts),
        grid=(rows // size,),
        in_specs=[by_row(2)] + [by_row(width)] * 6 + [by_row(128), whole(router), whole(router_t)],
        out_specs=[by_row(width), by_row(width), by_row(128)],
        out_shape=[jax.ShapeDtypeStruct((rows, width), BF16)] * 2 + [jax.ShapeDtypeStruct((rows, 128), F32)],
        compiler_params=params(20 << 20),
        cost_estimate=cost(2 * rows * 128 * width * 4, 20 * rows * width),
        name="middle",
    )(routes, own, recv, stream, first, second, grad_out, dgate, router, router_t)


def spread_kernel(slots, gates, gout, here, there):
    room = here.shape[0]
    rows = gout.shape[0]
    place = lax.broadcasted_iota(jnp.int32, (room, rows), 0)
    grad = gout[...].astype(F32)
    near, far = 0.0, 0.0
    for i in range(2):
        part = (gates[:, i : i + 1] * grad).astype(BF16)
        near = near + dot_nn((slots[i : i + 1, :] == place).astype(BF16), part)
        far = far + dot_nn((slots[i : i + 1, :] == place + room).astype(BF16), part)
    here[...] = near.astype(BF16)
    there[...] = far.astype(BF16)


def spread(slots_t, gates, grad_out, room):
    rows, width = grad_out.shape
    size = width // CHUNKS
    by_column = lambda n: pl.BlockSpec((n, size), lambda i: (0, i))
    return pl.pallas_call(
        spread_kernel,
        grid=(CHUNKS,),
        in_specs=[
            pl.BlockSpec((2, rows), lambda i: (0, 0)),
            pl.BlockSpec((rows, 128), lambda i: (0, 0)),
            by_column(rows),
        ],
        out_specs=[by_column(room)] * 2,
        out_shape=[jax.ShapeDtypeStruct((room, width), BF16)] * 2,
        compiler_params=params(20 << 20),
        cost_estimate=cost(8 * rows * room * width, 2 * rows * width + 4 * room * width),
        name="spread",
    )(slots_t, gates, grad_out)


def local(
    queries_in, rotated_keys, value_inputs, stream_in, w_out, w_router, routes, expert_out, grad_out
):
    place = lax.axis_index("ctx")
    core = lax.axis_index("exp")
    tok, heads_q, head_dim = queries_in.shape
    heads_kv = rotated_keys.shape[1]
    rows, width = stream_in.shape
    experts = w_router.shape[1]
    held, capacity = expert_out.shape[1], expert_out.shape[3]
    room = held * capacity
    scale = head_dim ** (-0.5)
    core_arg = core.astype(jnp.int32).reshape(1)
    place_arg = place.astype(jnp.int32).reshape(1)

    own_band = jnp.concatenate(
        [rotated_keys.reshape(tok, heads_kv * head_dim), value_inputs.reshape(tok, heads_kv * head_dim)], axis=1
    )
    queries = jnp.transpose(queries_in, (1, 0, 2))
    flat = routes.reshape(-1)
    number = jnp.arange(2 * rows, dtype=jnp.int32)
    earlier = (flat[None, :] == flat[:, None]) & (number[None, :] < number[:, None])
    rank = jnp.sum(earlier.astype(jnp.int32), axis=1)
    slots = (flat * capacity + rank - core * room) % (experts * capacity)
    slots = slots.reshape(rows, 2)
    router = jnp.pad(w_router, ((0, 0), (0, 128 - experts)))
    router_t = jnp.pad(jnp.concatenate([w_router.T] * 3, axis=0), ((0, 128 - 3 * experts), (0, 0)))
    made = {}

    def prepare(*ready):
        return [slots, own_band, router, router_t]

    def swap_rows(*ready):
        rows_out = after([expert_out], *ready)[0]
        made["rows"] = swapped(rows_out, "exp")
        return [made["rows"]]

    def pick_rows(*ready):
        arrived = after([made["rows"]], *ready)[0]
        made["picked"] = pick(core_arg, slots, expert_out, arrived, grad_out)
        return [made["picked"][2]]

    def attend(*ready):
        band = after([own_band], *ready)[0]
        bands = [band] + [passed_along(band, "ctx", step) for step in range(1, BAND_BLOCKS)]
        made["bands"] = bands[::-1]
        made["attention"] = attention(
            queries, made["bands"], place_arg, heads_q, heads_kv, head_dim, scale
        )

    arrays, table, plan = gathered(w_out, prepare, swap_rows, pick_rows, attend)
    first, second, dgate = made["picked"]
    attn, probs = made["attention"]
    bands = made["bands"]

    own, other = project([attn], arrays, table, plan, core_arg, heads_q, head_dim, width, rows)
    mixed, grad_input, gates = middle(
        routes, own, swapped(other, "exp"), stream_in, first, second, grad_out, dgate, router, router_t, experts
    )
    grad_other = swapped(grad_input, "exp")
    here, there = spread(slots.T, gates, grad_out, room)
    dattn = dattention(grad_input, grad_other, arrays, table, plan, core_arg, heads_q, head_dim, width)
    there = after([there], dattn)[0]
    back = swapped(there, "exp").reshape(held, capacity, width)
    here = here.reshape(held, capacity, width)
    grads, totals, given = [], [], ()
    for i in range(heads_kv):
        if i == heads_kv - 1:
            given = (grads[-1][0], core_arg, here, back)
        grad = attention_grad(queries, dattn, attn, probs, bands, i, given, heads_kv, scale)
        if i > 0:
            totals[-1] = after(totals[-1], grad[0])
        totals.append(exchanged(grad[BAND_BLOCKS - 1], grad[BAND_BLOCKS - 3]))
        grads.append(grad)
    grad_q = jnp.transpose(grads[-1][0], (1, 0, 2))
    grad_expert = grads[-1][1 + BAND_BLOCKS]
    totals = [combined(grad[BAND_BLOCKS - 2], *pair) for grad, pair in zip(grads, totals)]
    sums = [
        (grad[BAND_BLOCKS] + (near.astype(F32) + far.astype(F32))).astype(BF16)
        for grad, (near, far) in zip(grads, totals)
    ]
    join = lambda lanes: jnp.concatenate([t[:, lanes] for t in sums], axis=1).reshape(tok, heads_kv, head_dim)
    grad_k, grad_v = join(slice(0, head_dim)), join(slice(head_dim, None))
    return (mixed, grad_input, grad_expert, grad_q, grad_k, grad_v)


def solution(mesh):
    in_specs = (
        P(("groups", "ctx"), "exp", None),
        P(("groups", "ctx"), "exp", None),
        P(("groups", "ctx"), "exp", None),
        P(("groups", "ctx", "exp"), None),
        P("exp", "ctx", None),
        P(),
        P(("groups", "ctx", "exp"), None),
        P(("groups", "ctx"), "exp", None, None, None),
        P(("groups", "ctx", "exp"), None),
    )
    out_specs = (
        P(("groups", "ctx", "exp"), None),
        P(("groups", "ctx", "exp"), None),
        P(("groups", "ctx"), "exp", None, None, None),
        P(("groups", "ctx"), "exp", None),
        P(("groups", "ctx"), "exp", None),
        P(("groups", "ctx"), "exp", None),
    )
    return jax.shard_map(local, mesh=mesh, in_specs=in_specs, out_specs=out_specs, check_vma=False)
```
